32 devices in a mesh: visit: 4 (over z), prow: 4 (over y, x), pcol: 2 (over core).
Axes of the slice: x: 2, y: 2, z: 4, core: 2. Of those that a mesh axis runs over, the one named last changes fastest.
Arguments:
- stamps: float32 [256, 36864], P(('visit', 'prow', 'pcol')), may hold values from -8 to 8
- variance: float32 [256, 128, 128], P(('visit', 'prow', 'pcol')), may hold values from 0.5 to 8
- coefficients: float32 [256, 9], P(('visit', 'prow', 'pcol')), may hold values from -2 to 2
- band_offsets: int32 [256, 2], P(('visit', 'prow', 'pcol')), may hold values from 2 to 31
- shifts: float32 [256, 2], P(('visit', 'prow', 'pcol')), may hold values from 0 to 1
- destination: int32 [256], P(('visit', 'prow', 'pcol')), may hold values from 0 to 7, as said below
- position: int32 [256], P(('visit', 'prow', 'pcol')), may hold values from 0 to 15
- psf_taps: float32 [17], replicated, may hold values from 0.1 to 1
Outputs:
- coadd: float32 [2048, 1024], P('prow', 'pcol')
- detection: float32 [2048, 1024], P('prow', 'pcol')
The draws below stay inside these ranges and needn't reach their ends.
Inputs may be any that keep to these rules, and one draw needn't show every extreme that they name: `destination`: each device's blocks name patches 0 .. 7; no device sends more than 2 of its blocks to one patch, and in every visit group one patch receives exactly 2 blocks from every device of that group.
All inputs are finite; a program needn't handle non-finite values.
Results may differ from the reference program's by a relative error of at most 0.0003.
Values sent between devices are 32-bit elements; how exact they have to be, the bound alone decides.
No kernel may reach another device: no remote copies, remote signals or barrier semaphores. Data moves between devices by JAX's collectives and lax.ppermute only.
A program may use at most 64 MiB of HBM per device.

```python
import math
import jax
import jax.numpy as jnp
from jax import lax

NB = 8
S = 192
B = 128
KR = 15
NBASIS = 9
PB = 4
RF = 8
MATCHED = 162
PCOLS = 2
PROWS = 4
OWNERS = 8
CAP = 2
GROUPS = 4
BLOCKS = 256
TROWS = 2048
TCOLS = 1024


def draw_destination(key, part):
    devices = BLOCKS // NB
    others = (OWNERS - 1) * CAP

    def one_device(device):
        group_index = device // OWNERS
        hot_owner = jax.random.randint(jax.random.fold_in(jax.random.fold_in(key, 101), group_index), (), 0, OWNERS)
        device_key = jax.random.fold_in(jax.random.fold_in(key, 202), device)
        ordering = jax.random.permutation(device_key, others)
        spread = ordering[:NB - CAP] // CAP
        spread = spread + (spread >= hot_owner).astype(jnp.int32)
        chosen = jnp.concatenate([jnp.full((CAP,), hot_owner, dtype=jnp.int32), spread.astype(jnp.int32)])
        shuffle = jax.random.permutation(jax.random.fold_in(device_key, 303), NB)
        return chosen[shuffle]
    return jax.vmap(one_device)(jnp.arange(devices, dtype=jnp.int32)).reshape(BLOCKS)


def plant(values, own_key, least, top_value):
    spot = [jax.random.randint(jax.random.fold_in(own_key, axis), (), 0, length) for axis, length in enumerate(values.shape)]
    main_axis = values.shape.index(max(values.shape))
    neighbour = spot[:main_axis] + [(spot[main_axis] + 1) % values.shape[main_axis]] + spot[main_axis + 1:]
    return values.at[tuple(spot)].set(least).at[tuple(neighbour)].set(top_value)


def block_scale(own_key, shape, cuts, smallest, top_value):
    def one(dim, blocks):
        draws = jax.random.uniform(jax.random.fold_in(jax.random.fold_in(own_key, 6), dim), (blocks,), jnp.float32, smallest / len(cuts), top_value / len(cuts))
        return jnp.repeat(jnp.exp(draws), shape[dim] // blocks).reshape((-1,) + (1,) * (len(shape) - dim - 1))

    loudness = one(*cuts[0])
    for cut in cuts[1:]:
        loudness = loudness * one(*cut)
    return loudness


def bell_draw(key, extent, deviation, most, cuts=(), kind=jnp.bfloat16):
    gain = block_scale(key, extent, cuts, -0.22, 0.18) if cuts else 1.0
    values = jax.random.normal(key, extent, jnp.float32) * deviation * gain
    return jnp.minimum(jnp.maximum(values, -most), most).astype(kind)


def setup_inputs(seed: int = 0) -> dict:
    keys = jax.random.split(jax.random.key(seed), 9)
    return {
        "stamps": bell_draw(keys[0], (BLOCKS, S * S), 1.0, 8.0, ((0, 32),), jnp.float32),
        "variance": jnp.clip(jnp.exp(math.log(8.0) - 2.7725887 * jax.random.uniform(keys[1], (BLOCKS, B, B), jnp.float32) ** block_scale(keys[1], (BLOCKS, B, B), ((0, 32),), -0.2, 0.2)), 0.5, 8.0),
        "coefficients": bell_draw(keys[2], (BLOCKS, NBASIS), 0.4, 2.0, ((0, 32),), jnp.float32),
        "band_offsets": plant(jax.random.randint(keys[3], (BLOCKS, 2), 2, MATCHED - B - 2), jax.random.fold_in(keys[3], 1), 2, (MATCHED - B - 2) - 1).astype(jnp.int32),
        "shifts": jnp.clip(1.0 * jax.random.uniform(keys[4], (BLOCKS, 2), jnp.float32) ** block_scale(keys[4], (BLOCKS, 2), ((0, 32),), -0.2, 0.2), 0.0, 1.0),
        "destination": draw_destination(jax.random.fold_in(keys[8], 71), 0),
        "position": plant(jax.random.randint(keys[6], (BLOCKS,), 0, PB * PB), jax.random.fold_in(keys[6], 1), 0, (PB * PB) - 1).astype(jnp.int32),
        "psf_taps": jnp.clip(jnp.exp(jax.random.uniform(keys[7], (2 * RF + 1,), jnp.float32, math.log(0.1), math.log(1.0))), 0.1, 1.0),
    }


basis_widths = (1.0, 2.0, 4.0)

def factor_tables(span, radius):
    matched_len = span - 2 * radius
    row_index = jnp.arange(matched_len, dtype=jnp.int32)[:, None]
    col_index = jnp.arange(span, dtype=jnp.int32)[None, :]
    lag_index = col_index - row_index - radius
    inside = (jnp.abs(lag_index) <= radius).astype(jnp.float32)
    lagged = lag_index.astype(jnp.float32)
    offsets = jnp.arange(-radius, radius + 1, dtype=jnp.int32).astype(jnp.float32)
    result = []
    for width in basis_widths:
        scaled = offsets / width
        gauss_norm = jnp.sqrt(jnp.sum(jnp.exp(-scaled * scaled)))
        quad_norm = jnp.sqrt(jnp.sum(scaled ** 4 * jnp.exp(-scaled * scaled)))
        ratio = lagged / width
        bell = jnp.exp(-0.5 * ratio * ratio) * inside
        result.append(jnp.stack([bell / gauss_norm, ratio * ratio * bell / quad_norm]))
    return jnp.stack(result)

def lanczos_bands(offsets, fractions, out_len, in_len):
    row_index = jnp.arange(out_len, dtype=jnp.int32)[None, :, None]
    col_index = jnp.arange(in_len, dtype=jnp.int32)[None, None, :]
    start = offsets.astype(jnp.int32)[:, None, None]
    distance = (col_index - row_index - start).astype(jnp.float32) - fractions[:, None, None]
    return jnp.where(jnp.abs(distance) < 3.0, jnp.sinc(distance) * jnp.sinc(distance / 3.0), 0.0)

def warp_blocks(stamps, coefficients, band_offsets, shifts, tables, side):
    highest = lax.Precision.HIGHEST
    count = stamps.shape[0]
    matched_len = tables.shape[2]
    matched = jnp.zeros((count, matched_len, matched_len), jnp.float32)
    for width_index in range(len(basis_widths)):
        bell = tables[width_index, 0]
        quad = tables[width_index, 1]
        rows_bell = jnp.einsum('ms,bst->bmt', bell, stamps, precision=highest, preferred_element_type=jnp.float32)
        rows_quad = jnp.einsum('ms,bst->bmt', quad, stamps, precision=highest, preferred_element_type=jnp.float32)
        first = coefficients[:, 3 * width_index][:, None, None]
        second = coefficients[:, 3 * width_index + 1][:, None, None]
        third = coefficients[:, 3 * width_index + 2][:, None, None]
        left = first * rows_bell + second * rows_quad
        matched = matched + jnp.einsum('bmt,nt->bmn', left, bell, precision=highest, preferred_element_type=jnp.float32)
        matched = matched + third * jnp.einsum('bmt,nt->bmn', rows_bell, quad, precision=highest, preferred_element_type=jnp.float32)
    band_rows = lanczos_bands(band_offsets[:, 0], shifts[:, 0], side, matched_len)
    band_cols = lanczos_bands(band_offsets[:, 1], shifts[:, 1], side, matched_len)
    halfway = jnp.einsum('bim,bmn->bin', band_rows, matched, precision=highest, preferred_element_type=jnp.float32)
    return jnp.einsum('bin,bjn->bij', halfway, band_cols, precision=highest, preferred_element_type=jnp.float32)

def filter_band(taps, length, radius):
    row_index = jnp.arange(length, dtype=jnp.int32)[:, None]
    col_index = jnp.arange(length + 2 * radius, dtype=jnp.int32)[None, :]
    lag_index = col_index - row_index
    band = jnp.zeros((length, length + 2 * radius), jnp.float32)
    for tap_index in range(2 * radius + 1):
        band = band + jnp.where(lag_index == tap_index, taps[tap_index], 0.0)
    return band

def reference(stamps, variance, coefficients, band_offsets, shifts, destination, position, psf_taps):
    highest = lax.Precision.HIGHEST
    per_group = NB * OWNERS
    tables = factor_tables(S, KR)
    pieces = (stamps.reshape(GROUPS, per_group, S, S), variance.reshape(GROUPS, per_group, B, B), coefficients.reshape(GROUPS, per_group, NBASIS), band_offsets.reshape(GROUPS, per_group, 2), shifts.reshape(GROUPS, per_group, 2), destination.reshape(GROUPS, per_group), position.reshape(GROUPS, per_group))

    def one_group(carry, group_pieces):
        group_stamps, group_var, group_coef, group_off, group_shift, group_dest, group_pos = group_pieces
        warped = warp_blocks(group_stamps, group_coef, group_off, group_shift, tables, B)
        weight = 1.0 / group_var
        terms = jnp.stack([weight * warped, weight], axis=1)
        tile_index = (group_dest * (PB * PB) + group_pos).astype(jnp.int32)
        summed = jax.ops.segment_sum(terms, tile_index, num_segments=OWNERS * PB * PB)
        return (carry + summed, None)
    start = jnp.zeros((OWNERS * PB * PB, 2, B, B), jnp.float32)
    tile_sums, _ = lax.scan(one_group, start, pieces)
    grid = tile_sums.reshape(PROWS, PCOLS, PB, PB, 2, B, B).transpose(4, 0, 2, 5, 1, 3, 6).reshape(2, TROWS, TCOLS)
    coadd = grid[0] / (1.0 + grid[1])
    padded = jnp.pad(coadd, RF)
    row_band = filter_band(psf_taps, TROWS, RF)
    col_band = filter_band(psf_taps, TCOLS, RF)
    across = jnp.dot(row_band, padded, precision=highest, preferred_element_type=jnp.float32)
    detection = jnp.dot(across, col_band.T, precision=highest, preferred_element_type=jnp.float32)
    return (coadd, detection)
```

```python
import functools

import jax
import jax.numpy as jnp
import numpy as np
from jax import lax
from jax.experimental import pallas as pl
from jax.experimental.pallas import tpu as pltpu
from jax.sharding import PartitionSpec as P

S = 192
KR = 15
PB = 4
RF = 8


basis_widths = (1.0, 2.0, 4.0)


def extended(cells, sides, width):
    for axis, dim in sides:
        count = lax.axis_size(axis)
        ends = count - 1
        head = lax.slice_in_dim(cells, 0, width, axis=dim)
        tail = lax.slice_in_dim(cells, cells.shape[dim] - width, cells.shape[dim], axis=dim)
        cells = jnp.concatenate(
            [
                lax.ppermute(tail, axis, [(i, (i + 1) % count) for i in range(ends)]),
                cells,
                lax.ppermute(head, axis, [((i + 1) % count, i) for i in range(ends)]),
            ],
            axis=dim,
        )
    return cells


def factor_tables(span, radius):
    matched_len = span - 2 * radius
    row_index = jnp.arange(matched_len, dtype=jnp.int32)[:, None]
    col_index = jnp.arange(span, dtype=jnp.int32)[None, :]
    lag_index = col_index - row_index - radius
    inside = (jnp.abs(lag_index) <= radius).astype(jnp.float32)
    lagged = lag_index.astype(jnp.float32)
    offsets = jnp.arange(-radius, radius + 1, dtype=jnp.int32).astype(jnp.float32)
    result = []
    for width in basis_widths:
        scaled = offsets / width
        gauss_norm = jnp.sqrt(jnp.sum(jnp.exp(-scaled * scaled)))
        quad_norm = jnp.sqrt(jnp.sum(scaled**4 * jnp.exp(-scaled * scaled)))
        ratio = lagged / width
        bell = jnp.exp(-0.5 * ratio * ratio) * inside
        result.append(jnp.stack([bell / gauss_norm, ratio * ratio * bell / quad_norm]))
    return jnp.stack(result)


def lanczos_bands(offsets, fractions, out_len, in_len):
    row_index = jnp.arange(out_len, dtype=jnp.int32)[None, :, None]
    col_index = jnp.arange(in_len, dtype=jnp.int32)[None, None, :]
    start = offsets[:, None, None]
    distance = (col_index - row_index - start).astype(jnp.float32) - fractions[:, None, None]
    return jnp.where(jnp.abs(distance) < 3.0, jnp.sinc(distance) * jnp.sinc(distance / 3.0), 0.0)


def warp_blocks(stamps, coefficients, band_offsets, shifts, tables, side):
    highest = lax.Precision.HIGHEST
    count = stamps.shape[0]
    matched_len = tables.shape[2]
    matched = jnp.zeros((count, matched_len, matched_len), jnp.float32)
    for width_index in range(len(basis_widths)):
        bell = tables[width_index, 0]
        quad = tables[width_index, 1]
        rows_bell = jnp.einsum(
            "ms,bst->bmt", bell, stamps, precision=highest, preferred_element_type=jnp.float32
        )
        rows_quad = jnp.einsum(
            "ms,bst->bmt", quad, stamps, precision=highest, preferred_element_type=jnp.float32
        )
        first = coefficients[:, 3 * width_index][:, None, None]
        second = coefficients[:, 3 * width_index + 1][:, None, None]
        third = coefficients[:, 3 * width_index + 2][:, None, None]
        left = first * rows_bell + second * rows_quad
        matched = matched + jnp.einsum(
            "bmt,nt->bmn", left, bell, precision=highest, preferred_element_type=jnp.float32
        )
        matched = matched + third * jnp.einsum(
            "bmt,nt->bmn", rows_bell, quad, precision=highest, preferred_element_type=jnp.float32
        )
    band_rows = lanczos_bands(band_offsets[:, 0], shifts[:, 0], side, matched_len)
    band_cols = lanczos_bands(band_offsets[:, 1], shifts[:, 1], side, matched_len)
    halfway = jnp.einsum(
        "bim,bmn->bin", band_rows, matched, precision=highest, preferred_element_type=jnp.float32
    )
    return jnp.einsum(
        "bin,bjn->bij", halfway, band_cols, precision=highest, preferred_element_type=jnp.float32
    )


def filter_band(taps, length, radius):
    row_index = jnp.arange(length, dtype=jnp.int32)[:, None]
    col_index = jnp.arange(length + 2 * radius, dtype=jnp.int32)[None, :]
    lag_index = col_index - row_index
    band = jnp.zeros((length, length + 2 * radius), jnp.float32)
    for tap_index in range(2 * radius + 1):
        band = band + jnp.where(lag_index == tap_index, taps[tap_index], 0.0)
    return band


def owner_body(stamps, variance, coefficients, band_offsets, shifts, destination, position, psf_taps):
    highest = lax.Precision.HIGHEST
    count = stamps.shape[0]
    span = S
    side = variance.shape[1]
    row_owners = lax.axis_size("prow")
    col_owners = lax.axis_size("pcol")
    owners = row_owners * col_owners
    capacity = max(2, 2 * count // owners)
    tables = factor_tables(span, KR)
    images = stamps.reshape(count, span, span)
    warped = warp_blocks(images, coefficients, band_offsets, shifts, tables, side)
    weight = 1.0 / variance
    terms = jnp.stack([weight * warped, weight], axis=1)
    owner_ids = jnp.arange(owners, dtype=jnp.int32)
    onehot = (destination[:, None] == owner_ids[None, :]).astype(jnp.int32)
    block_ids = jnp.arange(count, dtype=jnp.int32)
    earlier = (block_ids[None, :] < block_ids[:, None]).astype(jnp.int32)
    before = jnp.sum(earlier[:, :, None] * onehot[None, :, :], axis=1)
    rank = jnp.sum(before * onehot, axis=1)
    slot_ids = jnp.arange(capacity, dtype=jnp.int32)
    select = onehot.T[:, None, :] * (rank[None, None, :] == slot_ids[None, :, None]).astype(
        jnp.int32
    )
    send_pos = jnp.sum(select * (position[None, None, :] + 1), axis=2) - 1
    outgoing = jnp.einsum(
        "okb,bxij->okxij",
        select.astype(jnp.float32),
        terms,
        precision=highest,
        preferred_element_type=jnp.float32,
    )
    incoming, arrived = (
        lax.all_to_all(outgoing, ("prow", "pcol"), split_axis=0, concat_axis=0, tiled=True),
        lax.all_to_all(send_pos, ("prow", "pcol"), split_axis=0, concat_axis=0, tiled=True),
    )
    flattened = incoming.reshape(owners * capacity, 2 * side * side)
    tile_ids = jnp.arange(PB * PB, dtype=jnp.int32)
    placing = (arrived.reshape(owners * capacity)[None, :] == tile_ids[:, None]).astype(jnp.float32)
    tile_sums = jnp.dot(placing, flattened, precision=highest, preferred_element_type=jnp.float32)
    patch_sums = (
        tile_sums.reshape(PB, PB, 2, side, side)
        .transpose(2, 0, 3, 1, 4)
        .reshape(2, PB * side, PB * side)
    )
    shares = lax.psum_scatter(patch_sums, "visit", scatter_dimension=1, tiled=True)
    coadd = lax.all_gather(shares[0] / (1.0 + shares[1]), "visit", axis=0, tiled=True)
    padded = extended(coadd, (("prow", 0), ("pcol", 1)), RF)
    band = filter_band(psf_taps, coadd.shape[0], RF)
    across = jnp.dot(band, padded, precision=highest, preferred_element_type=jnp.float32)
    detection = jnp.dot(across, band.T, precision=highest, preferred_element_type=jnp.float32)
    return (coadd, detection)


TAPS = 6
WRAP = 256


def halves(values):
    high = values.astype(jnp.bfloat16)
    return high, (values - high.astype(jnp.float32)).astype(jnp.bfloat16)


def dot(left, right, contract):
    return lax.dot_general(left, right, (contract, ((), ())), preferred_element_type=jnp.float32)


def toeplitz(row, rows):
    spread = jnp.broadcast_to(row, (rows, row.shape[1]))
    return pltpu.roll(spread, 0, 1, stride=1, stride_axis=0)


def lagged_tables(radius):
    lags = np.arange(-radius, radius + 1, dtype=np.float64)
    tables = np.zeros((TAPS, 8, WRAP), np.float64)
    for index, width in enumerate(basis_widths):
        ratio = lags / width
        bell = np.exp(-0.5 * ratio * ratio)
        quad = ratio * ratio * bell
        for kind, factor in enumerate((bell, quad)):
            normed = factor / np.sqrt(np.sum(factor * factor))
            for n in range(TAPS):
                places = (np.arange(2 * radius + 1) + n - 2) % WRAP
                tables[n, 2 * index + kind, places] = normed
    return tables.astype(np.float32)


def lanczos(distance):
    def sinc(x):
        angle = jnp.float32(np.pi) * x
        return jnp.where(x == 0.0, 1.0, jnp.sin(angle) / jnp.where(x == 0.0, 1.0, angle))

    return jnp.where(jnp.abs(distance) < 3.0, sinc(distance) * sinc(distance / 3.0), 0.0)


def warp_kernel(stamps, variance, coefs, offsets, shifts, dest, pos, tables, out, *, slices):
    k = pl.program_id(0)
    count = pl.num_programs(0)
    span = stamps.shape[1]
    side = variance.shape[1]
    depth = side // slices
    pitch = (2 * depth + 1) * count
    widths = len(basis_widths)
    lane = lax.broadcasted_iota(jnp.int32, (8, 128), 1)
    level = lax.broadcasted_iota(jnp.int32, (8, 128), 0)
    part = jnp.where(level == 0, shifts[k, 0], shifts[k, 1])
    values = lanczos((lane - 2).astype(jnp.float32) - part)
    rows = jnp.zeros(tables.shape[1:], jnp.float32)
    cols = jnp.zeros(tables.shape[1:], jnp.float32)
    for n in range(TAPS):
        rows = rows + values[0:1, n : n + 1] * tables[n]
        cols = cols + values[1:2, n : n + 1] * tables[n]
    rows = pltpu.roll(rows, offsets[k, 0], 1)
    cols = pltpu.roll(cols, offsets[k, 1], 1)
    image_high, image_low = halves(stamps[0])
    total = jnp.zeros((side, side), jnp.float32)
    for m in range(widths):
        bell = rows[2 * m : 2 * m + 1]
        quad = rows[2 * m + 1 : 2 * m + 2]
        lefts = (
            coefs[k, 3 * m] * bell + coefs[k, 3 * m + 1] * quad,
            coefs[k, 3 * m + 2] * bell,
        )
        for kind in range(2):
            right = toeplitz(cols[2 * m + kind : 2 * m + kind + 1], side)
            right_high, right_low = halves(right[:, :span])
            both = jnp.concatenate([right_high, right_low], axis=0)
            first = dot(image_high, both, ((1,), (1,)))
            across = first[:, :side] + first[:, side:] + dot(image_low, right_high, ((1,), (1,)))
            left_high, left_low = halves(toeplitz(lefts[kind], side)[:, :span])
            across_high, across_low = halves(across)
            pair = jnp.concatenate([across_high, across_low], axis=1)
            second = dot(left_high, pair, ((1,), (0,)))
            total = total + second[:, :side] + second[:, side:]
            total = total + dot(left_low, across_high, ((1,), (0,)))
    weight = 1.0 / variance[0]
    weighted = weight * total
    for r in range(depth):
        cut = slice(r * slices, (r + 1) * slices)
        out[pl.ds(r * count + k, slices, stride=pitch), :] = weighted[cut]
        out[pl.ds((depth + r) * count + k, slices, stride=pitch), :] = weight[cut]
    tile = (dest[k] * (PB * PB) + pos[k]).astype(jnp.float32)
    out[pl.ds(2 * depth * count + k, slices, stride=pitch), :] = jnp.full((slices, side), tile)


def tile_kernel(place, incoming, out, cells, strips, *, count, visits, prows, pcols):
    slices, pitch, side = incoming.shape
    depth = side // slices
    owners = prows * pcols
    per_patch = PB * PB
    tiles = owners * per_patch
    blocks = slices * count
    named = incoming[:, 2 * depth * count :, :].reshape(blocks, side)
    named = jnp.concatenate([named] * (tiles // side), axis=1) if tiles > side else named
    places = lax.broadcasted_iota(jnp.int32, (blocks, tiles), 1).astype(jnp.float32)
    chosen = jnp.where(named == places, 1.0, 0.0).T.astype(jnp.bfloat16)

    def summed(index):
        data = incoming[:, index * count : (index + 1) * count, :].reshape(blocks, side)
        high, low = halves(data)
        both = dot(chosen, jnp.concatenate([high, low], axis=1), ((1,), (0,)))
        return both[:, :side] + both[:, side:]

    for r in range(depth):
        cells[r * tiles : (r + 1) * tiles, :] = summed(r) / (1.0 + summed(depth + r))
    lane = lax.broadcasted_iota(jnp.int32, (PB, side), 1)
    for o in range(owners):
        for r in range(depth):
            strip = jnp.zeros((PB, side), jnp.float32)
            if o % pcols < pcols - 1:
                after = cells[pl.ds(r * tiles + (o + 1) * per_patch, PB, stride=PB), :]
                strip = jnp.where(lane < RF, after, strip)
            if o % pcols > 0:
                before = cells[pl.ds(r * tiles + (o - 1) * per_patch + PB - 1, PB, stride=PB), :]
                strip = jnp.where(lane >= side - RF, before, strip)
            strips[(o * depth + r) * PB : (o * depth + r + 1) * PB, :] = strip
    group = side // (2 * RF)
    packed = pltpu.roll(strips[...], RF, 1, stride=2 * RF, stride_axis=0)
    packed = jnp.sum(packed.reshape(owners * depth * PB // group, group, side), axis=1)
    lines = depth * PB // group
    upper = place[0] >= RF
    for o in range(owners):
        below = jnp.zeros((PB, side), jnp.float32)
        above = jnp.zeros((PB, side), jnp.float32)
        corner_below = jnp.zeros((1, side), jnp.float32)
        corner_above = jnp.zeros((1, side), jnp.float32)
        if o + pcols < owners:
            start = (o + pcols) * per_patch
            below = cells[start : start + PB, :]
            start = (o + pcols) * depth * PB
            corner_below = strips[start : start + 1, :]
        if o >= pcols:
            start = (depth - 1) * tiles + (o - pcols) * per_patch + per_patch - PB
            above = cells[start : start + PB, :]
            start = (o - pcols + 1) * depth * PB - 1
            corner_above = strips[start : start + 1, :]
        outer = jnp.where(upper, above, below)
        corner = jnp.where(upper, corner_above, corner_below)
        for v in range(visits):
            to = v * owners + o
            for r in range(depth):
                start = r * tiles + o * per_patch
                out[to, r * per_patch : (r + 1) * per_patch, :] = cells[start : start + per_patch, :]
            start = depth * per_patch
            out[to, start : start + lines, :] = packed[o * lines : (o + 1) * lines]
            start = start + lines
            out[to, start : start + PB, :] = outer
            start = start + PB
            out[to, start : start + 1, :] = corner


def filter_kernel(taps, incoming, coadd, detection, across, *, slices):
    pitch = incoming.shape[0] // slices
    side = incoming.shape[1]
    depth = side // slices
    per_patch = PB * PB
    group = side // (2 * RF)
    lines = depth * PB // group
    lane = lax.broadcasted_iota(jnp.int32, (8, WRAP), 1)
    centred = jnp.zeros((8, WRAP), jnp.float32)
    leading = jnp.zeros((8, WRAP), jnp.float32)
    for b in range(2 * RF + 1):
        centred = jnp.where(lane == (b - RF) % WRAP, taps[b], centred)
        leading = jnp.where(lane == b, taps[b], leading)
    across_band = toeplitz(centred[0:1], side)
    down_band = toeplitz(leading[0:1], side)
    across_high, across_low = halves(across_band)
    across_both = jnp.concatenate([across_high, across_low], axis=0)
    down_high, down_low = halves(down_band[:, : side + 2 * RF])

    def filtered(parts, ends, start):
        rows = ends.shape[0]
        left = lax.broadcasted_iota(jnp.int32, (rows, side), 1) < side // 2
        for c in range(PB):
            after = parts[c + 1] if c < PB - 1 else ends
            before = parts[c - 1] if c > 0 else ends
            beside = jnp.where(left, after, before)
            whole = jnp.concatenate([parts[c], beside], axis=1)
            high, low = halves(whole)
            both = dot(high, across_both, ((1,), (1,)))
            result = both[:, :side] + both[:, side:] + dot(low, across_high, ((1,), (1,)))
            across[start : start + rows, c * side : (c + 1) * side] = result

    def line(index, first, rows):
        return incoming[pl.ds(first * pitch + index, rows, stride=pitch), :]

    for p in range(PB):
        parts = []
        for c in range(PB):
            tile = jnp.concatenate(
                [line(r * per_patch + p * PB + c, 0, slices) for r in range(depth)], axis=0
            )
            coadd[p * side : (p + 1) * side, c * side : (c + 1) * side] = tile
            parts.append(tile)
        ends = []
        for r in range(depth):
            number = r * PB + p
            strip = line(depth * per_patch + number // group, 0, slices)
            turn = -(2 * RF * (number % group) + RF) % side
            ends.append(pltpu.roll(strip, turn, 1) if turn else strip)
        filtered(parts, jnp.concatenate(ends, axis=0), RF + p * side)
    start = depth * per_patch + lines
    for first, place in ((slices - RF, 0), (0, RF + PB * side)):
        parts = [line(start + c, first, RF) for c in range(PB)]
        filtered(parts, line(start + PB, first, RF), place)
    for p in range(PB):
        high, low = halves(across[p * side : (p + 1) * side + 2 * RF, :])
        result = dot(down_high, high, ((1,), (0,))) + dot(down_high, low, ((1,), (0,)))
        result = result + dot(down_low, high, ((1,), (0,)))
        detection[p * side : (p + 1) * side, :] = result


def sliced_body(
    stamps, variance, coefficients, band_offsets, shifts, destination, position, psf_taps
):
    axes = ("visit", "prow", "pcol")
    count = stamps.shape[0]
    side = variance.shape[1]
    slices = lax.axis_size(axes)
    depth = side // slices
    visits = lax.axis_size("visit")
    prows = lax.axis_size("prow")
    pcols = lax.axis_size("pcol")
    owners = prows * pcols
    tiles = owners * PB * PB
    span = S
    pitch = (2 * depth + 1) * count
    smem = pl.BlockSpec(memory_space=pltpu.SMEM)
    vmem = pl.BlockSpec(memory_space=pltpu.VMEM)
    tables = jnp.asarray(lagged_tables(KR))
    images = stamps.reshape(count, span, span)
    outgoing = pl.pallas_call(
        functools.partial(warp_kernel, slices=slices),
        grid=(count,),
        in_specs=[
            pl.BlockSpec((1, span, span), lambda k: (k, 0, 0)),
            pl.BlockSpec((1, side, side), lambda k: (k, 0, 0)),
            smem,
            smem,
            smem,
            smem,
            smem,
            pl.BlockSpec(tables.shape, lambda k: (0, 0, 0)),
        ],
        out_specs=pl.BlockSpec((slices * pitch, side), lambda k: (0, 0)),
        out_shape=jax.ShapeDtypeStruct((slices * pitch, side), jnp.float32),
    )(images, variance, coefficients, band_offsets, shifts, destination, position, tables)
    incoming = lax.all_to_all(
        outgoing.reshape(slices, pitch, side), axes, split_axis=0, concat_axis=0, tiled=True
    )
    group = side // (2 * RF)
    length = depth * PB * PB + depth * PB // group + PB + 1
    length = -(-length // 8) * 8
    place = lax.axis_index(axes).astype(jnp.int32).reshape(1)
    shares = pl.pallas_call(
        functools.partial(tile_kernel, count=count, visits=visits, prows=prows, pcols=pcols),
        in_specs=[smem, vmem],
        out_specs=vmem,
        out_shape=jax.ShapeDtypeStruct((slices, length, side), jnp.float32),
        scratch_shapes=[
            pltpu.VMEM((depth * tiles, side), jnp.float32),
            pltpu.VMEM((owners * depth * PB, side), jnp.float32),
        ],
    )(place, incoming)
    gathered = lax.all_to_all(shares, axes, split_axis=0, concat_axis=0, tiled=True)
    extent = PB * side
    return pl.pallas_call(
        functools.partial(filter_kernel, slices=slices),
        in_specs=[smem, vmem],
        out_specs=[vmem, vmem],
        out_shape=[jax.ShapeDtypeStruct((extent, extent), jnp.float32)] * 2,
        scratch_shapes=[pltpu.VMEM((extent + 2 * RF, extent), jnp.float32)],
    )(psf_taps, gathered.reshape(slices * length, side))


def slices_fit(mesh, side):
    total = mesh.shape["visit"] * mesh.shape["prow"] * mesh.shape["pcol"]
    tiles = mesh.shape["prow"] * mesh.shape["pcol"] * PB * PB
    group = side // (2 * RF)
    if side % total or total < RF or tiles % side:
        return False
    return (side // total * PB) % group == 0


def body(*args):
    mesh = jax.sharding.get_abstract_mesh()
    if slices_fit(mesh, args[1].shape[1]):
        return tuple(sliced_body(*args))
    return owner_body(*args)


def solution(mesh):
    placed = (
        P(("visit", "prow", "pcol"), None),
        P(("visit", "prow", "pcol"), None, None),
        P(("visit", "prow", "pcol"), None),
        P(("visit", "prow", "pcol"), None),
        P(("visit", "prow", "pcol"), None),
        P(("visit", "prow", "pcol")),
        P(("visit", "prow", "pcol")),
        P(),
    )
    return jax.shard_map(
        body,
        mesh=mesh,
        in_specs=placed,
        out_specs=(P("prow", "pcol"), P("prow", "pcol")),
        check_vma=False,
    )
```

```python
import functools

import jax
import jax.numpy as jnp
import numpy as np
from jax import lax
from jax.experimental import pallas as pl
from jax.experimental.pallas import tpu as pltpu
from jax.sharding import PartitionSpec as P

S = 192
KR = 15
PB = 4
RF = 8


basis_widths = (1.0, 2.0, 4.0)


def extended(cells, sides, width):
    for axis, dim in sides:
        count = lax.axis_size(axis)
        ends = count - 1
        head = lax.slice_in_dim(cells, 0, width, axis=dim)
        tail = lax.slice_in_dim(cells, cells.shape[dim] - width, cells.shape[dim], axis=dim)
        cells = jnp.concatenate(
            [
                lax.ppermute(tail, axis, [(i, (i + 1) % count) for i in range(ends)]),
                cells,
                lax.ppermute(head, axis, [((i + 1) % count, i) for i in range(ends)]),
            ],
            axis=dim,
        )
    return cells


def factor_tables(span, radius):
    matched_len = span - 2 * radius
    row_index = jnp.arange(matched_len, dtype=jnp.int32)[:, None]
    col_index = jnp.arange(span, dtype=jnp.int32)[None, :]
    lag_index = col_index - row_index - radius
    inside = (jnp.abs(lag_index) <= radius).astype(jnp.float32)
    lagged = lag_index.astype(jnp.float32)
    offsets = jnp.arange(-radius, radius + 1, dtype=jnp.int32).astype(jnp.float32)
    result = []
    for width in basis_widths:
        scaled = offsets / width
        gauss_norm = jnp.sqrt(jnp.sum(jnp.exp(-scaled * scaled)))
        quad_norm = jnp.sqrt(jnp.sum(scaled**4 * jnp.exp(-scaled * scaled)))
        ratio = lagged / width
        bell = jnp.exp(-0.5 * ratio * ratio) * inside
        result.append(jnp.stack([bell / gauss_norm, ratio * ratio * bell / quad_norm]))
    return jnp.stack(result)


def lanczos_bands(offsets, fractions, out_len, in_len):
    row_index = jnp.arange(out_len, dtype=jnp.int32)[None, :, None]
    col_index = jnp.arange(in_len, dtype=jnp.int32)[None, None, :]
    start = offsets[:, None, None]
    distance = (col_index - row_index - start).astype(jnp.float32) - fractions[:, None, None]
    return jnp.where(jnp.abs(distance) < 3.0, jnp.sinc(distance) * jnp.sinc(distance / 3.0), 0.0)


def warp_blocks(stamps, coefficients, band_offsets, shifts, tables, side):
    highest = lax.Precision.HIGHEST
    count = stamps.shape[0]
    matched_len = tables.shape[2]
    matched = jnp.zeros((count, matched_len, matched_len), jnp.float32)
    for width_index in range(len(basis_widths)):
        bell = tables[width_index, 0]
        quad = tables[width_index, 1]
        rows_bell = jnp.einsum(
            "ms,bst->bmt", bell, stamps, precision=highest, preferred_element_type=jnp.float32
        )
        rows_quad = jnp.einsum(
            "ms,bst->bmt", quad, stamps, precision=highest, preferred_element_type=jnp.float32
        )
        first = coefficients[:, 3 * width_index][:, None, None]
        second = coefficients[:, 3 * width_index + 1][:, None, None]
        third = coefficients[:, 3 * width_index + 2][:, None, None]
        left = first * rows_bell + second * rows_quad
        matched = matched + jnp.einsum(
            "bmt,nt->bmn", left, bell, precision=highest, preferred_element_type=jnp.float32
        )
        matched = matched + third * jnp.einsum(
            "bmt,nt->bmn", rows_bell, quad, precision=highest, preferred_element_type=jnp.float32
        )
    band_rows = lanczos_bands(band_offsets[:, 0], shifts[:, 0], side, matched_len)
    band_cols = lanczos_bands(band_offsets[:, 1], shifts[:, 1], side, matched_len)
    halfway = jnp.einsum(
        "bim,bmn->bin", band_rows, matched, precision=highest, preferred_element_type=jnp.float32
    )
    return jnp.einsum(
        "bin,bjn->bij", halfway, band_cols, precision=highest, preferred_element_type=jnp.float32
    )


def filter_band(taps, length, radius):
    row_index = jnp.arange(length, dtype=jnp.int32)[:, None]
    col_index = jnp.arange(length + 2 * radius, dtype=jnp.int32)[None, :]
    lag_index = col_index - row_index
    band = jnp.zeros((length, length + 2 * radius), jnp.float32)
    for tap_index in range(2 * radius + 1):
        band = band + jnp.where(lag_index == tap_index, taps[tap_index], 0.0)
    return band


def owner_body(stamps, variance, coefficients, band_offsets, shifts, destination, position, psf_taps):
    highest = lax.Precision.HIGHEST
    count = stamps.shape[0]
    span = S
    side = variance.shape[1]
    row_owners = lax.axis_size("prow")
    col_owners = lax.axis_size("pcol")
    owners = row_owners * col_owners
    capacity = max(2, 2 * count // owners)
    tables = factor_tables(span, KR)
    images = stamps.reshape(count, span, span)
    warped = warp_blocks(images, coefficients, band_offsets, shifts, tables, side)
    weight = 1.0 / variance
    terms = jnp.stack([weight * warped, weight], axis=1)
    owner_ids = jnp.arange(owners, dtype=jnp.int32)
    onehot = (destination[:, None] == owner_ids[None, :]).astype(jnp.int32)
    block_ids = jnp.arange(count, dtype=jnp.int32)
    earlier = (block_ids[None, :] < block_ids[:, None]).astype(jnp.int32)
    before = jnp.sum(earlier[:, :, None] * onehot[None, :, :], axis=1)
    rank = jnp.sum(before * onehot, axis=1)
    slot_ids = jnp.arange(capacity, dtype=jnp.int32)
    select = onehot.T[:, None, :] * (rank[None, None, :] == slot_ids[None, :, None]).astype(
        jnp.int32
    )
    send_pos = jnp.sum(select * (position[None, None, :] + 1), axis=2) - 1
    outgoing = jnp.einsum(
        "okb,bxij->okxij",
        select.astype(jnp.float32),
        terms,
        precision=highest,
        preferred_element_type=jnp.float32,
    )
    incoming, arrived = (
        lax.all_to_all(outgoing, ("prow", "pcol"), split_axis=0, concat_axis=0, tiled=True),
        lax.all_to_all(send_pos, ("prow", "pcol"), split_axis=0, concat_axis=0, tiled=True),
    )
    flattened = incoming.reshape(owners * capacity, 2 * side * side)
    tile_ids = jnp.arange(PB * PB, dtype=jnp.int32)
    placing = (arrived.reshape(owners * capacity)[None, :] == tile_ids[:, None]).astype(jnp.float32)
    tile_sums = jnp.dot(placing, flattened, precision=highest, preferred_element_type=jnp.float32)
    patch_sums = (
        tile_sums.reshape(PB, PB, 2, side, side)
        .transpose(2, 0, 3, 1, 4)
        .reshape(2, PB * side, PB * side)
    )
    shares = lax.psum_scatter(patch_sums, "visit", scatter_dimension=1, tiled=True)
    coadd = lax.all_gather(shares[0] / (1.0 + shares[1]), "visit", axis=0, tiled=True)
    padded = extended(coadd, (("prow", 0), ("pcol", 1)), RF)
    band = filter_band(psf_taps, coadd.shape[0], RF)
    across = jnp.dot(band, padded, precision=highest, preferred_element_type=jnp.float32)
    detection = jnp.dot(across, band.T, precision=highest, preferred_element_type=jnp.float32)
    return (coadd, detection)


TAPS = 6
AXES = ("visit", "prow", "pcol")
WRAP = 256


def halves(values):
    high = values.astype(jnp.bfloat16)
    return high, (values - high.astype(jnp.float32)).astype(jnp.bfloat16)


def dot(left, right, contract):
    return lax.dot_general(left, right, (contract, ((), ())), preferred_element_type=jnp.float32)


def toeplitz(row, rows):
    spread = jnp.broadcast_to(row, (rows, row.shape[1]))
    return pltpu.roll(spread, 0, 1, stride=1, stride_axis=0)


def lagged_tables(radius, period):
    lags = np.arange(-radius, radius + 1, dtype=np.float64)
    tables = np.zeros((2, TAPS, 8, period), np.float64)
    for index, width in enumerate(basis_widths):
        ratio = lags / width
        bell = np.exp(-0.5 * ratio * ratio)
        quad = ratio * ratio * bell
        for kind, factor in enumerate((bell, quad)):
            normed = factor / np.sqrt(np.sum(factor * factor))
            for n in range(TAPS):
                places = np.arange(2 * radius + 1) + n - 2
                tables[0, n, 2 * index + kind, places % period] = normed
                tables[1, n, 2 * index + kind, -places % period] = normed
    return tables.astype(np.float32)


def lanczos(distance):
    def sinc(x):
        angle = jnp.float32(np.pi) * x
        return jnp.where(x == 0.0, 1.0, jnp.sin(angle) / jnp.where(x == 0.0, 1.0, angle))

    return jnp.where(jnp.abs(distance) < 3.0, sinc(distance) * sinc(distance / 3.0), 0.0)


def weight_kernel(variance, dest, pos, out, *, slices):
    count, side = variance.shape[:2]
    depth = side // slices
    pitch = (depth + 1) * count
    for k in range(count):
        weight = 1.0 / variance[k]
        for r in range(depth):
            cut = slice(r * slices, (r + 1) * slices)
            out[pl.ds(r * count + k, slices, stride=pitch), :] = weight[cut]
        tile = (dest[k] * (PB * PB) + pos[k]).astype(jnp.float32)
        out[pl.ds(depth * count + k, slices, stride=pitch), :] = jnp.full((slices, side), tile)


def warp_kernel(
    stamps, variance, coefs, offsets, shifts, tables, out, image, masks, taps, *, slices, batch
):
    step = pl.program_id(0)
    count = pl.num_programs(0) * batch
    span = stamps.shape[1]
    side = variance.shape[1]
    depth = side // slices
    pitch = depth * count
    widths = len(basis_widths)

    @pl.when(step == 0)
    def _():
        image[...] = jnp.zeros(image.shape, image.dtype)
        row = lax.broadcasted_iota(jnp.int32, (side, side), 0)
        col = lax.broadcasted_iota(jnp.int32, (side, side), 1)
        for index, test in enumerate((col >= row, col < row, col <= row, col > row)):
            masks[index] = jnp.where(test, 1.0, 0.0).astype(jnp.bfloat16)
        lane = lax.broadcasted_iota(jnp.int32, (count, side), 1)
        level = lax.broadcasted_iota(jnp.int32, (count, side), 0)
        for axis in range(2):
            part = jnp.zeros((count, side), jnp.float32)
            for k in range(count):
                part = jnp.where(level == k, shifts[axis, k], part)
            taps[axis] = lanczos((lane - 2).astype(jnp.float32) - part)

    for b in range(batch):
        k = step * batch + b
        factors = []
        for axis in range(2):
            values = taps[axis, pl.ds(k, 1), :]
            total = jnp.zeros(tables.shape[2:], jnp.float32)
            for n in range(TAPS):
                total = total + values[:, n : n + 1] * tables[axis, n]
            offset = offsets[axis, k]
            factors.append(pltpu.roll(total, offset if axis == 0 else side - offset, 1))
        rows, cols = factors
        high, low = halves(stamps[b])
        image[b, 0:span, 0:span] = high
        image[b, 2 * side : 2 * side + span, 0:span] = low
        image_high = image[b, 0 : 2 * side, :]
        image_low = image[b, 2 * side : 4 * side, :]
        lefts = []
        rights = []
        for m in range(widths):
            bell = cols[2 * m : 2 * m + 1]
            quad = cols[2 * m + 1 : 2 * m + 2]
            mixed = (
                coefs[k, 3 * m] * bell + coefs[k, 3 * m + 2] * quad,
                coefs[k, 3 * m + 1] * bell,
            )
            for kind in range(2):
                q = 2 * m + kind
                high, low = halves(toeplitz(rows[q : q + 1], side))
                high = jnp.concatenate([high * masks[0], high * masks[1]], axis=1)
                low = jnp.concatenate([low * masks[0], low * masks[1]], axis=1)
                lefts.append(jnp.concatenate([high, high, low], axis=1))
                high, low = halves(toeplitz(mixed[kind], side))
                both = jnp.concatenate([high, low], axis=1)
                upper = jnp.concatenate([masks[2], masks[2]], axis=1)
                lower = jnp.concatenate([masks[3], masks[3]], axis=1)
                rights.append(jnp.concatenate([both * upper, both * lower], axis=0))
        images = jnp.concatenate([image_high, image_low, image_high], axis=0)
        total = jnp.zeros((2 * side, 2 * side), jnp.float32)
        for q in range(2 * widths):
            high, low = halves(dot(lefts[q], images, ((1,), (0,))))
            total = total + dot(jnp.concatenate([high, low], axis=0), rights[q], ((1,), (0,)))
        warped = total[:side, :side] + (total[:side, side:] + total[side:, :side])
        weighted = (1.0 / variance[b]) * warped
        for r in range(depth):
            cut = slice(r * slices, (r + 1) * slices)
            out[pl.ds(r * count + k, slices, stride=pitch), :] = weighted[cut]


def tile_kernel(weights, incoming, out, cells, strips, *, count, visits, prows, pcols):
    slices, pitch, side = incoming.shape
    depth = side // slices
    owners = prows * pcols
    per_patch = PB * PB
    tiles = owners * per_patch
    blocks = slices * count
    named = weights[:, depth * count :, :].reshape(blocks, side)
    named = jnp.concatenate([named] * (tiles // side), axis=1) if tiles > side else named
    places = lax.broadcasted_iota(jnp.int32, (blocks, tiles), 1).astype(jnp.float32)
    chosen = jnp.where(named == places, 1.0, 0.0).T.astype(jnp.bfloat16)

    def summed(source, index):
        data = source[:, index * count : (index + 1) * count, :].reshape(blocks, side)
        high, low = halves(data)
        both = dot(chosen, jnp.concatenate([high, low], axis=1), ((1,), (0,)))
        return both[:, :side] + both[:, side:]

    for r in range(depth):
        cells[r * tiles : (r + 1) * tiles, :] = summed(incoming, r) / (1.0 + summed(weights, r))
    lane = lax.broadcasted_iota(jnp.int32, (PB, side), 1)
    for o in range(owners):
        for r in range(depth):
            strip = jnp.zeros((PB, side), jnp.float32)
            if o % pcols < pcols - 1:
                after = cells[pl.ds(r * tiles + (o + 1) * per_patch, PB, stride=PB), :]
                strip = jnp.where(lane < RF, after, strip)
            if o % pcols > 0:
                before = cells[pl.ds(r * tiles + (o - 1) * per_patch + PB - 1, PB, stride=PB), :]
                strip = jnp.where(lane >= side - RF, before, strip)
            strips[(o * depth + r) * PB : (o * depth + r + 1) * PB, :] = strip
    group = side // (2 * RF)
    packed = pltpu.roll(strips[...], RF, 1, stride=2 * RF, stride_axis=0)
    packed = jnp.sum(packed.reshape(owners * depth * PB // group, group, side), axis=1)
    lines = depth * PB // group
    upper = lax.axis_index(AXES) >= RF
    for o in range(owners):
        below = jnp.zeros((PB, side), jnp.float32)
        above = jnp.zeros((PB, side), jnp.float32)
        corner_below = jnp.zeros((1, side), jnp.float32)
        corner_above = jnp.zeros((1, side), jnp.float32)
        if o + pcols < owners:
            start = (o + pcols) * per_patch
            below = cells[start : start + PB, :]
            start = (o + pcols) * depth * PB
            corner_below = strips[start : start + 1, :]
        if o >= pcols:
            start = (depth - 1) * tiles + (o - pcols) * per_patch + per_patch - PB
            above = cells[start : start + PB, :]
            start = (o - pcols + 1) * depth * PB - 1
            corner_above = strips[start : start + 1, :]
        outer = jnp.where(upper, above, below)
        corner = jnp.where(upper, corner_above, corner_below)
        for v in range(visits):
            to = v * owners + o
            for r in range(depth):
                start = r * tiles + o * per_patch
                out[to, r * per_patch : (r + 1) * per_patch, :] = cells[start : start + per_patch, :]
            start = depth * per_patch
            out[to, start : start + lines, :] = packed[o * lines : (o + 1) * lines]
            start = start + lines
            out[to, start : start + PB, :] = outer
            start = start + PB
            out[to, start : start + 1, :] = corner


def filter_kernel(taps, incoming, coadd, detection, across, *, slices):
    pitch = incoming.shape[0] // slices
    side = incoming.shape[1]
    depth = side // slices
    per_patch = PB * PB
    group = side // (2 * RF)
    lines = depth * PB // group
    lane = lax.broadcasted_iota(jnp.int32, (8, WRAP), 1)
    centred = jnp.zeros((8, WRAP), jnp.float32)
    leading = jnp.zeros((8, WRAP), jnp.float32)
    for b in range(2 * RF + 1):
        centred = jnp.where(lane == (b - RF) % WRAP, taps[b], centred)
        leading = jnp.where(lane == b, taps[b], leading)
    across_band = toeplitz(centred[0:1], side)
    down_band = toeplitz(leading[0:1], side)
    across_high, across_low = halves(across_band)
    across_both = jnp.concatenate([across_high, across_low], axis=0)
    down_high, down_low = halves(down_band[:, : side + 2 * RF])

    def filtered(parts, ends, start):
        rows = ends.shape[0]
        left = lax.broadcasted_iota(jnp.int32, (rows, side), 1) < side // 2
        for c in range(PB):
            after = parts[c + 1] if c < PB - 1 else ends
            before = parts[c - 1] if c > 0 else ends
            beside = jnp.where(left, after, before)
            whole = jnp.concatenate([parts[c], beside], axis=1)
            high, low = halves(whole)
            both = dot(high, across_both, ((1,), (1,)))
            result = both[:, :side] + both[:, side:] + dot(low, across_high, ((1,), (1,)))
            across[start : start + rows, c * side : (c + 1) * side] = result

    def line(index, first, rows):
        return incoming[pl.ds(first * pitch + index, rows, stride=pitch), :]

    for p in range(PB):
        parts = []
        for c in range(PB):
            tile = jnp.concatenate(
                [line(r * per_patch + p * PB + c, 0, slices) for r in range(depth)], axis=0
            )
            coadd[p * side : (p + 1) * side, c * side : (c + 1) * side] = tile
            parts.append(tile)
        ends = []
        for r in range(depth):
            number = r * PB + p
            strip = line(depth * per_patch + number // group, 0, slices)
            turn = -(2 * RF * (number % group) + RF) % side
            ends.append(pltpu.roll(strip, turn, 1) if turn else strip)
        filtered(parts, jnp.concatenate(ends, axis=0), RF + p * side)
    start = depth * per_patch + lines
    for first, place in ((slices - RF, 0), (0, RF + PB * side)):
        parts = [line(start + c, first, RF) for c in range(PB)]
        filtered(parts, line(start + PB, first, RF), place)
    for p in range(PB):
        high, low = halves(across[p * side : (p + 1) * side + 2 * RF, :])
        result = dot(down_high, high, ((1,), (0,))) + dot(down_high, low, ((1,), (0,)))
        result = result + dot(down_low, high, ((1,), (0,)))
        detection[p * side : (p + 1) * side, :] = result


def sliced_body(
    stamps, variance, coefficients, band_offsets, shifts, destination, position, psf_taps
):
    count = stamps.shape[0]
    side = variance.shape[1]
    slices = lax.axis_size(AXES)
    depth = side // slices
    visits = lax.axis_size("visit")
    prows = lax.axis_size("prow")
    pcols = lax.axis_size("pcol")
    owners = prows * pcols
    tiles = owners * PB * PB
    span = S
    batch = 2 if count % 2 == 0 else 1
    smem = pl.BlockSpec(memory_space=pltpu.SMEM)
    vmem = pl.BlockSpec(memory_space=pltpu.VMEM)
    pitch = (depth + 1) * count
    weights = pl.pallas_call(
        functools.partial(weight_kernel, slices=slices),
        in_specs=[vmem, smem, smem],
        out_specs=vmem,
        out_shape=jax.ShapeDtypeStruct((slices * pitch, side), jnp.float32),
    )(variance, destination, position)
    weights = lax.all_to_all(
        weights.reshape(slices, pitch, side), AXES, split_axis=0, concat_axis=0, tiled=True
    )
    tables = jnp.asarray(lagged_tables(KR, side))
    images = stamps.reshape(count, span, span)
    pitch = depth * count
    outgoing = pl.pallas_call(
        functools.partial(warp_kernel, slices=slices, batch=batch),
        grid=(count // batch,),
        in_specs=[
            pl.BlockSpec((batch, span, span), lambda k: (k, 0, 0)),
            pl.BlockSpec((batch, side, side), lambda k: (k, 0, 0)),
            smem,
            smem,
            smem,
            pl.BlockSpec(tables.shape, lambda k: (0, 0, 0, 0)),
        ],
        out_specs=pl.BlockSpec((slices * pitch, side), lambda k: (0, 0)),
        out_shape=jax.ShapeDtypeStruct((slices * pitch, side), jnp.float32),
        scratch_shapes=[
            pltpu.VMEM((batch, 4 * side, 2 * side), jnp.bfloat16),
            pltpu.VMEM((4, side, side), jnp.bfloat16),
            pltpu.VMEM((2, count, side), jnp.float32),
        ],
    )(images, variance, coefficients, band_offsets.T, shifts.T, tables)
    outgoing, weights = lax.optimization_barrier((outgoing, weights))
    incoming = lax.all_to_all(
        outgoing.reshape(slices, pitch, side), AXES, split_axis=0, concat_axis=0, tiled=True
    )
    group = side // (2 * RF)
    length = depth * PB * PB + depth * PB // group + PB + 1
    length = -(-length // 8) * 8
    shares = pl.pallas_call(
        functools.partial(tile_kernel, count=count, visits=visits, prows=prows, pcols=pcols),
        in_specs=[vmem, vmem],
        out_specs=vmem,
        out_shape=jax.ShapeDtypeStruct((slices, length, side), jnp.float32),
        scratch_shapes=[
            pltpu.VMEM((depth * tiles, side), jnp.float32),
            pltpu.VMEM((owners * depth * PB, side), jnp.float32),
        ],
    )(weights, incoming)
    gathered = lax.all_to_all(shares, AXES, split_axis=0, concat_axis=0, tiled=True)
    extent = PB * side
    return pl.pallas_call(
        functools.partial(filter_kernel, slices=slices),
        in_specs=[smem, vmem],
        out_specs=[vmem, vmem],
        out_shape=[jax.ShapeDtypeStruct((extent, extent), jnp.float32)] * 2,
        scratch_shapes=[pltpu.VMEM((extent + 2 * RF, extent), jnp.float32)],
    )(psf_taps, gathered.reshape(slices * length, side))


def slices_fit(mesh, side):
    total = mesh.shape["visit"] * mesh.shape["prow"] * mesh.shape["pcol"]
    tiles = mesh.shape["prow"] * mesh.shape["pcol"] * PB * PB
    group = side // (2 * RF)
    if side % total or total < RF or tiles % side:
        return False
    return (side // total * PB) % group == 0


def body(*args):
    mesh = jax.sharding.get_abstract_mesh()
    if slices_fit(mesh, args[1].shape[1]):
        return tuple(sliced_body(*args))
    return owner_body(*args)


def solution(mesh):
    placed = (
        P(("visit", "prow", "pcol"), None),
        P(("visit", "prow", "pcol"), None, None),
        P(("visit", "prow", "pcol"), None),
        P(("visit", "prow", "pcol"), None),
        P(("visit", "prow", "pcol"), None),
        P(("visit", "prow", "pcol")),
        P(("visit", "prow", "pcol")),
        P(),
    )
    return jax.shard_map(
        body,
        mesh=mesh,
        in_specs=placed,
        out_specs=(P("prow", "pcol"), P("prow", "pcol")),
        check_vma=False,
    )
```

```python
import functools

import jax
import jax.numpy as jnp
import numpy as np
from jax import lax
from jax.experimental import pallas as pl
from jax.experimental.pallas import tpu as pltpu
from jax.sharding import PartitionSpec as P

S = 192
KR = 15
PB = 4
RF = 8


basis_widths = (1.0, 2.0, 4.0)


def extended(cells, sides, width):
    for axis, dim in sides:
        count = lax.axis_size(axis)
        ends = count - 1
        head = lax.slice_in_dim(cells, 0, width, axis=dim)
        tail = lax.slice_in_dim(cells, cells.shape[dim] - width, cells.shape[dim], axis=dim)
        cells = jnp.concatenate(
            [
                lax.ppermute(tail, axis, [(i, (i + 1) % count) for i in range(ends)]),
                cells,
                lax.ppermute(head, axis, [((i + 1) % count, i) for i in range(ends)]),
            ],
            axis=dim,
        )
    return cells


def factor_tables(span, radius):
    matched_len = span - 2 * radius
    row_index = jnp.arange(matched_len, dtype=jnp.int32)[:, None]
    col_index = jnp.arange(span, dtype=jnp.int32)[None, :]
    lag_index = col_index - row_index - radius
    inside = (jnp.abs(lag_index) <= radius).astype(jnp.float32)
    lagged = lag_index.astype(jnp.float32)
    offsets = jnp.arange(-radius, radius + 1, dtype=jnp.int32).astype(jnp.float32)
    result = []
    for width in basis_widths:
        scaled = offsets / width
        gauss_norm = jnp.sqrt(jnp.sum(jnp.exp(-scaled * scaled)))
        quad_norm = jnp.sqrt(jnp.sum(scaled**4 * jnp.exp(-scaled * scaled)))
        ratio = lagged / width
        bell = jnp.exp(-0.5 * ratio * ratio) * inside
        result.append(jnp.stack([bell / gauss_norm, ratio * ratio * bell / quad_norm]))
    return jnp.stack(result)


def lanczos_bands(offsets, fractions, out_len, in_len):
    row_index = jnp.arange(out_len, dtype=jnp.int32)[None, :, None]
    col_index = jnp.arange(in_len, dtype=jnp.int32)[None, None, :]
    start = offsets[:, None, None]
    distance = (col_index - row_index - start).astype(jnp.float32) - fractions[:, None, None]
    return jnp.where(jnp.abs(distance) < 3.0, jnp.sinc(distance) * jnp.sinc(distance / 3.0), 0.0)


def warp_blocks(stamps, coefficients, band_offsets, shifts, tables, side):
    highest = lax.Precision.HIGHEST
    count = stamps.shape[0]
    matched_len = tables.shape[2]
    matched = jnp.zeros((count, matched_len, matched_len), jnp.float32)
    for width_index in range(len(basis_widths)):
        bell = tables[width_index, 0]
        quad = tables[width_index, 1]
        rows_bell = jnp.einsum(
            "ms,bst->bmt", bell, stamps, precision=highest, preferred_element_type=jnp.float32
        )
        rows_quad = jnp.einsum(
            "ms,bst->bmt", quad, stamps, precision=highest, preferred_element_type=jnp.float32
        )
        first = coefficients[:, 3 * width_index][:, None, None]
        second = coefficients[:, 3 * width_index + 1][:, None, None]
        third = coefficients[:, 3 * width_index + 2][:, None, None]
        left = first * rows_bell + second * rows_quad
        matched = matched + jnp.einsum(
            "bmt,nt->bmn", left, bell, precision=highest, preferred_element_type=jnp.float32
        )
        matched = matched + third * jnp.einsum(
            "bmt,nt->bmn", rows_bell, quad, precision=highest, preferred_element_type=jnp.float32
        )
    band_rows = lanczos_bands(band_offsets[:, 0], shifts[:, 0], side, matched_len)
    band_cols = lanczos_bands(band_offsets[:, 1], shifts[:, 1], side, matched_len)
    halfway = jnp.einsum(
        "bim,bmn->bin", band_rows, matched, precision=highest, preferred_element_type=jnp.float32
    )
    return jnp.einsum(
        "bin,bjn->bij", halfway, band_cols, precision=highest, preferred_element_type=jnp.float32
    )


def filter_band(taps, length, radius):
    row_index = jnp.arange(length, dtype=jnp.int32)[:, None]
    col_index = jnp.arange(length + 2 * radius, dtype=jnp.int32)[None, :]
    lag_index = col_index - row_index
    band = jnp.zeros((length, length + 2 * radius), jnp.float32)
    for tap_index in range(2 * radius + 1):
        band = band + jnp.where(lag_index == tap_index, taps[tap_index], 0.0)
    return band


def owner_body(stamps, variance, coefficients, band_offsets, shifts, destination, position, psf_taps):
    highest = lax.Precision.HIGHEST
    count = stamps.shape[0]
    span = S
    side = variance.shape[1]
    row_owners = lax.axis_size("prow")
    col_owners = lax.axis_size("pcol")
    owners = row_owners * col_owners
    capacity = max(2, 2 * count // owners)
    tables = factor_tables(span, KR)
    images = stamps.reshape(count, span, span)
    warped = warp_blocks(images, coefficients, band_offsets, shifts, tables, side)
    weight = 1.0 / variance
    terms = jnp.stack([weight * warped, weight], axis=1)
    owner_ids = jnp.arange(owners, dtype=jnp.int32)
    onehot = (destination[:, None] == owner_ids[None, :]).astype(jnp.int32)
    block_ids = jnp.arange(count, dtype=jnp.int32)
    earlier = (block_ids[None, :] < block_ids[:, None]).astype(jnp.int32)
    before = jnp.sum(earlier[:, :, None] * onehot[None, :, :], axis=1)
    rank = jnp.sum(before * onehot, axis=1)
    slot_ids = jnp.arange(capacity, dtype=jnp.int32)
    select = onehot.T[:, None, :] * (rank[None, None, :] == slot_ids[None, :, None]).astype(
        jnp.int32
    )
    send_pos = jnp.sum(select * (position[None, None, :] + 1), axis=2) - 1
    outgoing = jnp.einsum(
        "okb,bxij->okxij",
        select.astype(jnp.float32),
        terms,
        precision=highest,
        preferred_element_type=jnp.float32,
    )
    incoming, arrived = (
        lax.all_to_all(outgoing, ("prow", "pcol"), split_axis=0, concat_axis=0, tiled=True),
        lax.all_to_all(send_pos, ("prow", "pcol"), split_axis=0, concat_axis=0, tiled=True),
    )
    flattened = incoming.reshape(owners * capacity, 2 * side * side)
    tile_ids = jnp.arange(PB * PB, dtype=jnp.int32)
    placing = (arrived.reshape(owners * capacity)[None, :] == tile_ids[:, None]).astype(jnp.float32)
    tile_sums = jnp.dot(placing, flattened, precision=highest, preferred_element_type=jnp.float32)
    patch_sums = (
        tile_sums.reshape(PB, PB, 2, side, side)
        .transpose(2, 0, 3, 1, 4)
        .reshape(2, PB * side, PB * side)
    )
    shares = lax.psum_scatter(patch_sums, "visit", scatter_dimension=1, tiled=True)
    coadd = lax.all_gather(shares[0] / (1.0 + shares[1]), "visit", axis=0, tiled=True)
    padded = extended(coadd, (("prow", 0), ("pcol", 1)), RF)
    band = filter_band(psf_taps, coadd.shape[0], RF)
    across = jnp.dot(band, padded, precision=highest, preferred_element_type=jnp.float32)
    detection = jnp.dot(across, band.T, precision=highest, preferred_element_type=jnp.float32)
    return (coadd, detection)


TAPS = 6
AXES = ("visit", "prow", "pcol")
WRAP = 256


def halves(values):
    high = values.astype(jnp.bfloat16)
    return high, (values - high.astype(jnp.float32)).astype(jnp.bfloat16)


def dot(left, right, contract):
    return lax.dot_general(left, right, (contract, ((), ())), preferred_element_type=jnp.float32)


def toeplitz(row, rows):
    spread = jnp.broadcast_to(row, (rows, row.shape[1]))
    return pltpu.roll(spread, 0, 1, stride=1, stride_axis=0)


def lagged_tables(radius, period):
    lags = np.arange(-radius, radius + 1, dtype=np.float64)
    tables = np.zeros((2, TAPS, 8, period), np.float64)
    for index, width in enumerate(basis_widths):
        ratio = lags / width
        bell = np.exp(-0.5 * ratio * ratio)
        quad = ratio * ratio * bell
        for kind, factor in enumerate((bell, quad)):
            normed = factor / np.sqrt(np.sum(factor * factor))
            for n in range(TAPS):
                places = np.arange(2 * radius + 1) + n - 2
                tables[0, n, 2 * index + kind, places % period] = normed
                tables[1, n, 2 * index + kind, -places % period] = normed
    return tables.astype(np.float32)


def lanczos(distance):
    def sinc(x):
        angle = jnp.float32(np.pi) * x
        return jnp.where(x == 0.0, 1.0, jnp.sin(angle) / jnp.where(x == 0.0, 1.0, angle))

    return jnp.where(jnp.abs(distance) < 3.0, sinc(distance) * sinc(distance / 3.0), 0.0)


def weight_kernel(variance, dest, pos, out, *, slices):
    count, side = variance.shape[:2]
    depth = side // slices
    pitch = (depth + 1) * count
    for k in range(count):
        weight = 1.0 / variance[k]
        for r in range(depth):
            cut = slice(r * slices, (r + 1) * slices)
            out[pl.ds(r * count + k, slices, stride=pitch), :] = weight[cut]
        tile = (dest[k] * (PB * PB) + pos[k]).astype(jnp.float32)
        out[pl.ds(depth * count + k, slices, stride=pitch), :] = jnp.full((slices, side), tile)


def warp_kernel(
    stamps, variance, coefs, offsets, shifts, tables, out, image, masks, taps, *, slices, batch
):
    step = pl.program_id(0)
    count = pl.num_programs(0) * batch
    span = stamps.shape[1]
    side = variance.shape[1]
    depth = side // slices
    pitch = depth * count
    widths = len(basis_widths)

    @pl.when(step == 0)
    def _():
        image[...] = jnp.zeros(image.shape, image.dtype)
        row = lax.broadcasted_iota(jnp.int32, (side, side), 0)
        col = lax.broadcasted_iota(jnp.int32, (side, side), 1)
        for index, test in enumerate((col >= row, col < row, col <= row, col > row)):
            masks[index] = jnp.where(test, 1.0, 0.0).astype(jnp.bfloat16)
        lane = lax.broadcasted_iota(jnp.int32, (count, side), 1)
        level = lax.broadcasted_iota(jnp.int32, (count, side), 0)
        for axis in range(2):
            part = jnp.zeros((count, side), jnp.float32)
            for k in range(count):
                part = jnp.where(level == k, shifts[axis, k], part)
            taps[axis] = lanczos((lane - 2).astype(jnp.float32) - part)

    for b in range(batch):
        k = step * batch + b
        factors = []
        for axis in range(2):
            values = taps[axis, pl.ds(k, 1), :]
            total = jnp.zeros(tables.shape[2:], jnp.float32)
            for n in range(TAPS):
                total = total + values[:, n : n + 1] * tables[axis, n]
            offset = offsets[axis, k]
            factors.append(pltpu.roll(total, offset if axis == 0 else side - offset, 1))
        rows, cols = factors
        high, low = halves(stamps[b])
        image[b, 0:span, 0:span] = high
        image[b, 2 * side : 2 * side + span, 0:span] = low
        image_high = image[b, 0 : 2 * side, :]
        image_low = image[b, 2 * side : 4 * side, :]
        lefts = []
        rights = []
        for m in range(widths):
            bell = cols[2 * m : 2 * m + 1]
            quad = cols[2 * m + 1 : 2 * m + 2]
            mixed = (
                coefs[k, 3 * m] * bell + coefs[k, 3 * m + 2] * quad,
                coefs[k, 3 * m + 1] * bell,
            )
            for kind in range(2):
                q = 2 * m + kind
                high, low = halves(toeplitz(rows[q : q + 1], side))
                high = jnp.concatenate([high * masks[0], high * masks[1]], axis=1)
                low = jnp.concatenate([low * masks[0], low * masks[1]], axis=1)
                lefts.append(jnp.concatenate([high, high, low], axis=1))
                high, low = halves(toeplitz(mixed[kind], side))
                both = jnp.concatenate([high, low], axis=1)
                upper = jnp.concatenate([masks[2], masks[2]], axis=1)
                lower = jnp.concatenate([masks[3], masks[3]], axis=1)
                rights.append(jnp.concatenate([both * upper, both * lower], axis=0))
        images = jnp.concatenate([image_high, image_low, image_high], axis=0)
        total = jnp.zeros((2 * side, 2 * side), jnp.float32)
        for q in range(2 * widths):
            high, low = halves(dot(lefts[q], images, ((1,), (0,))))
            total = total + dot(jnp.concatenate([high, low], axis=0), rights[q], ((1,), (0,)))
        warped = total[:side, :side] + (total[:side, side:] + total[side:, :side])
        weighted = (1.0 / variance[b]) * warped
        for r in range(depth):
            cut = slice(r * slices, (r + 1) * slices)
            out[pl.ds(r * count + k, slices, stride=pitch), :] = weighted[cut]


def tile_kernel(weights, incoming, out, cells, strips, *, count, visits, prows, pcols):
    slices, pitch, side = incoming.shape
    depth = side // slices
    owners = prows * pcols
    per_patch = PB * PB
    tiles = owners * per_patch
    blocks = slices * count
    named = weights[:, depth * count :, :].reshape(blocks, side)
    named = jnp.concatenate([named] * (tiles // side), axis=1) if tiles > side else named
    places = lax.broadcasted_iota(jnp.int32, (blocks, tiles), 1).astype(jnp.float32)
    chosen = jnp.where(named == places, 1.0, 0.0).T.astype(jnp.bfloat16)

    def summed(source, index):
        data = source[:, index * count : (index + 1) * count, :].reshape(blocks, side)
        high, low = halves(data)
        both = dot(chosen, jnp.concatenate([high, low], axis=1), ((1,), (0,)))
        return both[:, :side] + both[:, side:]

    for r in range(depth):
        cells[r * tiles : (r + 1) * tiles, :] = summed(incoming, r) / (1.0 + summed(weights, r))
    lane = lax.broadcasted_iota(jnp.int32, (PB, side), 1)
    for o in range(owners):
        for r in range(depth):
            strip = jnp.zeros((PB, side), jnp.float32)
            if o % pcols < pcols - 1:
                after = cells[pl.ds(r * tiles + (o + 1) * per_patch, PB, stride=PB), :]
                strip = jnp.where(lane < RF, after, strip)
            if o % pcols > 0:
                before = cells[pl.ds(r * tiles + (o - 1) * per_patch + PB - 1, PB, stride=PB), :]
                strip = jnp.where(lane >= side - RF, before, strip)
            strips[(o * depth + r) * PB : (o * depth + r + 1) * PB, :] = strip
    group = side // (2 * RF)
    packed = pltpu.roll(strips[...], RF, 1, stride=2 * RF, stride_axis=0)
    packed = jnp.sum(packed.reshape(owners * depth * PB // group, group, side), axis=1)
    lines = depth * PB // group
    upper = lax.axis_index(AXES) >= RF
    for o in range(owners):
        below = jnp.zeros((PB, side), jnp.float32)
        above = jnp.zeros((PB, side), jnp.float32)
        corner_below = jnp.zeros((1, side), jnp.float32)
        corner_above = jnp.zeros((1, side), jnp.float32)
        if o + pcols < owners:
            start = (o + pcols) * per_patch
            below = cells[start : start + PB, :]
            start = (o + pcols) * depth * PB
            corner_below = strips[start : start + 1, :]
        if o >= pcols:
            start = (depth - 1) * tiles + (o - pcols) * per_patch + per_patch - PB
            above = cells[start : start + PB, :]
            start = (o - pcols + 1) * depth * PB - 1
            corner_above = strips[start : start + 1, :]
        outer = jnp.where(upper, above, below)
        corner = jnp.where(upper, corner_above, corner_below)
        for v in range(visits):
            to = v * owners + o
            for r in range(depth):
                start = r * tiles + o * per_patch
                out[to, r * per_patch : (r + 1) * per_patch, :] = cells[start : start + per_patch, :]
            start = depth * per_patch
            out[to, start : start + lines, :] = packed[o * lines : (o + 1) * lines]
            start = start + lines
            out[to, start : start + PB, :] = outer
            start = start + PB
            out[to, start : start + 1, :] = corner


def filter_kernel(taps, incoming, coadd, detection, across, *, slices):
    pitch = incoming.shape[0] // slices
    side = incoming.shape[1]
    depth = side // slices
    per_patch = PB * PB
    group = side // (2 * RF)
    lines = depth * PB // group
    lane = lax.broadcasted_iota(jnp.int32, (8, WRAP), 1)
    centred = jnp.zeros((8, WRAP), jnp.float32)
    leading = jnp.zeros((8, WRAP), jnp.float32)
    for b in range(2 * RF + 1):
        centred = jnp.where(lane == (b - RF) % WRAP, taps[b], centred)
        leading = jnp.where(lane == b, taps[b], leading)
    across_band = toeplitz(centred[0:1], side)
    down_band = toeplitz(leading[0:1], side)
    across_high, across_low = halves(across_band)
    across_both = jnp.concatenate([across_high, across_low], axis=0)
    down_high, down_low = halves(down_band[:, : side + 2 * RF])

    def filtered(parts, ends, start):
        rows = ends.shape[0]
        left = lax.broadcasted_iota(jnp.int32, (rows, side), 1) < side // 2
        for c in range(PB):
            after = parts[c + 1] if c < PB - 1 else ends
            before = parts[c - 1] if c > 0 else ends
            beside = jnp.where(left, after, before)
            whole = jnp.concatenate([parts[c], beside], axis=1)
            high, low = halves(whole)
            both = dot(high, across_both, ((1,), (1,)))
            result = both[:, :side] + both[:, side:] + dot(low, across_high, ((1,), (1,)))
            across[start : start + rows, c * side : (c + 1) * side] = result

    def line(index, first, rows):
        return incoming[pl.ds(first * pitch + index, rows, stride=pitch), :]

    for p in range(PB):
        parts = []
        for c in range(PB):
            tile = jnp.concatenate(
                [line(r * per_patch + p * PB + c, 0, slices) for r in range(depth)], axis=0
            )
            coadd[p * side : (p + 1) * side, c * side : (c + 1) * side] = tile
            parts.append(tile)
        ends = []
        for r in range(depth):
            number = r * PB + p
            strip = line(depth * per_patch + number // group, 0, slices)
            turn = -(2 * RF * (number % group) + RF) % side
            ends.append(pltpu.roll(strip, turn, 1) if turn else strip)
        filtered(parts, jnp.concatenate(ends, axis=0), RF + p * side)
    start = depth * per_patch + lines
    for first, place in ((slices - RF, 0), (0, RF + PB * side)):
        parts = [line(start + c, first, RF) for c in range(PB)]
        filtered(parts, line(start + PB, first, RF), place)
    for p in range(PB):
        high, low = halves(across[p * side : (p + 1) * side + 2 * RF, :])
        result = dot(down_high, high, ((1,), (0,))) + dot(down_high, low, ((1,), (0,)))
        result = result + dot(down_low, high, ((1,), (0,)))
        detection[p * side : (p + 1) * side, :] = result


def sliced_body(
    stamps, variance, coefficients, band_offsets, shifts, destination, position, psf_taps
):
    count = stamps.shape[0]
    side = variance.shape[1]
    slices = lax.axis_size(AXES)
    depth = side // slices
    visits = lax.axis_size("visit")
    prows = lax.axis_size("prow")
    pcols = lax.axis_size("pcol")
    owners = prows * pcols
    tiles = owners * PB * PB
    span = S
    batch = 2 if count % 2 == 0 else 1
    smem = pl.BlockSpec(memory_space=pltpu.SMEM)
    vmem = pl.BlockSpec(memory_space=pltpu.VMEM)
    pitch = (depth + 1) * count
    weights = pl.pallas_call(
        functools.partial(weight_kernel, slices=slices),
        in_specs=[vmem, smem, smem],
        out_specs=vmem,
        out_shape=pltpu.VMEM((slices * pitch, side), jnp.float32),
    )(variance, destination, position)
    weights = lax.all_to_all(
        weights.reshape(slices, pitch, side), AXES, split_axis=0, concat_axis=0, tiled=True
    )
    tables = jnp.asarray(lagged_tables(KR, side))
    images = stamps.reshape(count, span, span)
    pitch = depth * count
    outgoing = pl.pallas_call(
        functools.partial(warp_kernel, slices=slices, batch=batch),
        grid=(count // batch,),
        in_specs=[
            pl.BlockSpec((batch, span, span), lambda k: (k, 0, 0)),
            pl.BlockSpec((batch, side, side), lambda k: (k, 0, 0)),
            smem,
            smem,
            smem,
            pl.BlockSpec(tables.shape, lambda k: (0, 0, 0, 0)),
        ],
        out_specs=pl.BlockSpec((slices * pitch, side), lambda k: (0, 0)),
        out_shape=jax.ShapeDtypeStruct((slices * pitch, side), jnp.float32),
        scratch_shapes=[
            pltpu.VMEM((batch, 4 * side, 2 * side), jnp.bfloat16),
            pltpu.VMEM((4, side, side), jnp.bfloat16),
            pltpu.VMEM((2, count, side), jnp.float32),
        ],
    )(images, variance, coefficients, band_offsets.T, shifts.T, tables)
    outgoing, weights = lax.optimization_barrier((outgoing, weights))
    incoming = lax.all_to_all(
        outgoing.reshape(slices, pitch, side), AXES, split_axis=0, concat_axis=0, tiled=True
    )
    group = side // (2 * RF)
    length = depth * PB * PB + depth * PB // group + PB + 1
    length = -(-length // 8) * 8
    shares = pl.pallas_call(
        functools.partial(tile_kernel, count=count, visits=visits, prows=prows, pcols=pcols),
        in_specs=[vmem, vmem],
        out_specs=vmem,
        out_shape=pltpu.VMEM((slices, length, side), jnp.float32),
        scratch_shapes=[
            pltpu.VMEM((depth * tiles, side), jnp.float32),
            pltpu.VMEM((owners * depth * PB, side), jnp.float32),
        ],
    )(kept(weights), kept(incoming))
    gathered = lax.all_to_all(shares, AXES, split_axis=0, concat_axis=0, tiled=True)
    extent = PB * side
    return pl.pallas_call(
        functools.partial(filter_kernel, slices=slices),
        in_specs=[smem, vmem],
        out_specs=[vmem, vmem],
        out_shape=[jax.ShapeDtypeStruct((extent, extent), jnp.float32)] * 2,
        scratch_shapes=[pltpu.VMEM((extent + 2 * RF, extent), jnp.float32)],
    )(psf_taps, kept(gathered.reshape(slices * length, side)))


def kept(values):
    return pltpu.with_memory_space_constraint(values, pltpu.VMEM)


def slices_fit(mesh, side):
    total = mesh.shape["visit"] * mesh.shape["prow"] * mesh.shape["pcol"]
    tiles = mesh.shape["prow"] * mesh.shape["pcol"] * PB * PB
    group = side // (2 * RF)
    if side % total or total < RF or tiles % side:
        return False
    return (side // total * PB) % group == 0


def body(*args):
    mesh = jax.sharding.get_abstract_mesh()
    if slices_fit(mesh, args[1].shape[1]):
        return tuple(sliced_body(*args))
    return owner_body(*args)


def solution(mesh):
    placed = (
        P(("visit", "prow", "pcol"), None),
        P(("visit", "prow", "pcol"), None, None),
        P(("visit", "prow", "pcol"), None),
        P(("visit", "prow", "pcol"), None),
        P(("visit", "prow", "pcol"), None),
        P(("visit", "prow", "pcol")),
        P(("visit", "prow", "pcol")),
        P(),
    )
    return jax.shard_map(
        body,
        mesh=mesh,
        in_specs=placed,
        out_specs=(P("prow", "pcol"), P("prow", "pcol")),
        check_vma=False,
    )
```

```python
import functools

import jax
import jax.numpy as jnp
import numpy as np
from jax import lax
from jax.experimental import pallas as pl
from jax.experimental.pallas import tpu as pltpu
from jax.sharding import PartitionSpec as P

S = 192
KR = 15
PB = 4
RF = 8


basis_widths = (1.0, 2.0, 4.0)


def extended(cells, sides, width):
    for axis, dim in sides:
        count = lax.axis_size(axis)
        ends = count - 1
        head = lax.slice_in_dim(cells, 0, width, axis=dim)
        tail = lax.slice_in_dim(cells, cells.shape[dim] - width, cells.shape[dim], axis=dim)
        cells = jnp.concatenate(
            [
                lax.ppermute(tail, axis, [(i, (i + 1) % count) for i in range(ends)]),
                cells,
                lax.ppermute(head, axis, [((i + 1) % count, i) for i in range(ends)]),
            ],
            axis=dim,
        )
    return cells


def factor_tables(span, radius):
    matched_len = span - 2 * radius
    row_index = jnp.arange(matched_len, dtype=jnp.int32)[:, None]
    col_index = jnp.arange(span, dtype=jnp.int32)[None, :]
    lag_index = col_index - row_index - radius
    inside = (jnp.abs(lag_index) <= radius).astype(jnp.float32)
    lagged = lag_index.astype(jnp.float32)
    offsets = jnp.arange(-radius, radius + 1, dtype=jnp.int32).astype(jnp.float32)
    result = []
    for width in basis_widths:
        scaled = offsets / width
        gauss_norm = jnp.sqrt(jnp.sum(jnp.exp(-scaled * scaled)))
        quad_norm = jnp.sqrt(jnp.sum(scaled**4 * jnp.exp(-scaled * scaled)))
        ratio = lagged / width
        bell = jnp.exp(-0.5 * ratio * ratio) * inside
        result.append(jnp.stack([bell / gauss_norm, ratio * ratio * bell / quad_norm]))
    return jnp.stack(result)


def lanczos_bands(offsets, fractions, out_len, in_len):
    row_index = jnp.arange(out_len, dtype=jnp.int32)[None, :, None]
    col_index = jnp.arange(in_len, dtype=jnp.int32)[None, None, :]
    start = offsets[:, None, None]
    distance = (col_index - row_index - start).astype(jnp.float32) - fractions[:, None, None]
    return jnp.where(jnp.abs(distance) < 3.0, jnp.sinc(distance) * jnp.sinc(distance / 3.0), 0.0)


def warp_blocks(stamps, coefficients, band_offsets, shifts, tables, side):
    highest = lax.Precision.HIGHEST
    count = stamps.shape[0]
    matched_len = tables.shape[2]
    matched = jnp.zeros((count, matched_len, matched_len), jnp.float32)
    for width_index in range(len(basis_widths)):
        bell = tables[width_index, 0]
        quad = tables[width_index, 1]
        rows_bell = jnp.einsum(
            "ms,bst->bmt", bell, stamps, precision=highest, preferred_element_type=jnp.float32
        )
        rows_quad = jnp.einsum(
            "ms,bst->bmt", quad, stamps, precision=highest, preferred_element_type=jnp.float32
        )
        first = coefficients[:, 3 * width_index][:, None, None]
        second = coefficients[:, 3 * width_index + 1][:, None, None]
        third = coefficients[:, 3 * width_index + 2][:, None, None]
        left = first * rows_bell + second * rows_quad
        matched = matched + jnp.einsum(
            "bmt,nt->bmn", left, bell, precision=highest, preferred_element_type=jnp.float32
        )
        matched = matched + third * jnp.einsum(
            "bmt,nt->bmn", rows_bell, quad, precision=highest, preferred_element_type=jnp.float32
        )
    band_rows = lanczos_bands(band_offsets[:, 0], shifts[:, 0], side, matched_len)
    band_cols = lanczos_bands(band_offsets[:, 1], shifts[:, 1], side, matched_len)
    halfway = jnp.einsum(
        "bim,bmn->bin", band_rows, matched, precision=highest, preferred_element_type=jnp.float32
    )
    return jnp.einsum(
        "bin,bjn->bij", halfway, band_cols, precision=highest, preferred_element_type=jnp.float32
    )


def filter_band(taps, length, radius):
    row_index = jnp.arange(length, dtype=jnp.int32)[:, None]
    col_index = jnp.arange(length + 2 * radius, dtype=jnp.int32)[None, :]
    lag_index = col_index - row_index
    band = jnp.zeros((length, length + 2 * radius), jnp.float32)
    for tap_index in range(2 * radius + 1):
        band = band + jnp.where(lag_index == tap_index, taps[tap_index], 0.0)
    return band


def owner_body(stamps, variance, coefficients, band_offsets, shifts, destination, position, psf_taps):
    highest = lax.Precision.HIGHEST
    count = stamps.shape[0]
    span = S
    side = variance.shape[1]
    row_owners = lax.axis_size("prow")
    col_owners = lax.axis_size("pcol")
    owners = row_owners * col_owners
    capacity = max(2, 2 * count // owners)
    tables = factor_tables(span, KR)
    images = stamps.reshape(count, span, span)
    warped = warp_blocks(images, coefficients, band_offsets, shifts, tables, side)
    weight = 1.0 / variance
    terms = jnp.stack([weight * warped, weight], axis=1)
    owner_ids = jnp.arange(owners, dtype=jnp.int32)
    onehot = (destination[:, None] == owner_ids[None, :]).astype(jnp.int32)
    block_ids = jnp.arange(count, dtype=jnp.int32)
    earlier = (block_ids[None, :] < block_ids[:, None]).astype(jnp.int32)
    before = jnp.sum(earlier[:, :, None] * onehot[None, :, :], axis=1)
    rank = jnp.sum(before * onehot, axis=1)
    slot_ids = jnp.arange(capacity, dtype=jnp.int32)
    select = onehot.T[:, None, :] * (rank[None, None, :] == slot_ids[None, :, None]).astype(
        jnp.int32
    )
    send_pos = jnp.sum(select * (position[None, None, :] + 1), axis=2) - 1
    outgoing = jnp.einsum(
        "okb,bxij->okxij",
        select.astype(jnp.float32),
        terms,
        precision=highest,
        preferred_element_type=jnp.float32,
    )
    incoming, arrived = (
        lax.all_to_all(outgoing, ("prow", "pcol"), split_axis=0, concat_axis=0, tiled=True),
        lax.all_to_all(send_pos, ("prow", "pcol"), split_axis=0, concat_axis=0, tiled=True),
    )
    flattened = incoming.reshape(owners * capacity, 2 * side * side)
    tile_ids = jnp.arange(PB * PB, dtype=jnp.int32)
    placing = (arrived.reshape(owners * capacity)[None, :] == tile_ids[:, None]).astype(jnp.float32)
    tile_sums = jnp.dot(placing, flattened, precision=highest, preferred_element_type=jnp.float32)
    patch_sums = (
        tile_sums.reshape(PB, PB, 2, side, side)
        .transpose(2, 0, 3, 1, 4)
        .reshape(2, PB * side, PB * side)
    )
    shares = lax.psum_scatter(patch_sums, "visit", scatter_dimension=1, tiled=True)
    coadd = lax.all_gather(shares[0] / (1.0 + shares[1]), "visit", axis=0, tiled=True)
    padded = extended(coadd, (("prow", 0), ("pcol", 1)), RF)
    band = filter_band(psf_taps, coadd.shape[0], RF)
    across = jnp.dot(band, padded, precision=highest, preferred_element_type=jnp.float32)
    detection = jnp.dot(across, band.T, precision=highest, preferred_element_type=jnp.float32)
    return (coadd, detection)


TAPS = 6
AXES = ("visit", "prow", "pcol")
WRAP = 256


def halves(values):
    high = values.astype(jnp.bfloat16)
    return high, (values - high.astype(jnp.float32)).astype(jnp.bfloat16)


def dot(left, right, contract):
    return lax.dot_general(left, right, (contract, ((), ())), preferred_element_type=jnp.float32)


def toeplitz(row, rows):
    spread = jnp.broadcast_to(row, (rows, row.shape[1]))
    return pltpu.roll(spread, 0, 1, stride=1, stride_axis=0)


def lagged_tables(radius, period):
    lags = np.arange(-radius, radius + 1, dtype=np.float64)
    tables = np.zeros((2, TAPS, 8, period), np.float64)
    for index, width in enumerate(basis_widths):
        ratio = lags / width
        bell = np.exp(-0.5 * ratio * ratio)
        quad = ratio * ratio * bell
        for kind, factor in enumerate((bell, quad)):
            normed = factor / np.sqrt(np.sum(factor * factor))
            for n in range(TAPS):
                places = np.arange(2 * radius + 1) + n - 2
                tables[0, n, 2 * index + kind, places % period] = normed
                tables[1, n, 2 * index + kind, -places % period] = normed
    return tables.astype(np.float32)


def lanczos(distance):
    def sinc(x):
        angle = jnp.float32(np.pi) * x
        return jnp.where(x == 0.0, 1.0, jnp.sin(angle) / jnp.where(x == 0.0, 1.0, angle))

    return jnp.where(jnp.abs(distance) < 3.0, sinc(distance) * sinc(distance / 3.0), 0.0)


def weight_kernel(variance, dest, pos, out, *, slices):
    count, side = variance.shape[:2]
    depth = side // slices
    pitch = depth * count + 1
    lane = lax.broadcasted_iota(jnp.int32, (slices, side), 1)
    names = jnp.zeros((slices, side), jnp.float32)
    for k in range(count):
        weight = 1.0 / variance[k]
        for r in range(depth):
            cut = slice(r * slices, (r + 1) * slices)
            out[pl.ds(r * count + k, slices, stride=pitch), :] = weight[cut]
        tile = (dest[k] * (PB * PB) + pos[k]).astype(jnp.float32)
        names = jnp.where(lane == k, tile, names)
    out[pl.ds(depth * count, slices, stride=pitch), :] = names


def warp_kernel(
    stamps, variance, coefs, offsets, shifts, tables, out, image, masks, taps, *, slices, batch
):
    step = pl.program_id(0)
    count = pl.num_programs(0) * batch
    span = stamps.shape[1]
    side = variance.shape[1]
    depth = side // slices
    pitch = depth * count
    widths = len(basis_widths)

    @pl.when(step == 0)
    def _():
        image[...] = jnp.zeros(image.shape, image.dtype)
        row = lax.broadcasted_iota(jnp.int32, (side, side), 0)
        col = lax.broadcasted_iota(jnp.int32, (side, side), 1)
        for index, test in enumerate((col >= row, col < row, col <= row, col > row)):
            masks[index] = jnp.where(test, 1.0, 0.0).astype(jnp.bfloat16)
        lane = lax.broadcasted_iota(jnp.int32, (count, side), 1)
        level = lax.broadcasted_iota(jnp.int32, (count, side), 0)
        for axis in range(2):
            part = jnp.zeros((count, side), jnp.float32)
            for k in range(count):
                part = jnp.where(level == k, shifts[axis, k], part)
            taps[axis] = lanczos((lane - 2).astype(jnp.float32) - part)

    for b in range(batch):
        k = step * batch + b
        factors = []
        for axis in range(2):
            values = taps[axis, pl.ds(k, 1), :]
            total = jnp.zeros(tables.shape[2:], jnp.float32)
            for n in range(TAPS):
                total = total + values[:, n : n + 1] * tables[axis, n]
            offset = offsets[axis, k]
            factors.append(pltpu.roll(total, offset if axis == 0 else side - offset, 1))
        rows, cols = factors
        high, low = halves(stamps[b])
        image[b, 0:span, 0:span] = high
        image[b, 2 * side : 2 * side + span, 0:span] = low
        image_high = image[b, 0 : 2 * side, :]
        image_low = image[b, 2 * side : 4 * side, :]
        lefts = []
        rights = []
        for m in range(widths):
            bell = cols[2 * m : 2 * m + 1]
            quad = cols[2 * m + 1 : 2 * m + 2]
            mixed = (
                coefs[k, 3 * m] * bell + coefs[k, 3 * m + 2] * quad,
                coefs[k, 3 * m + 1] * bell,
            )
            for kind in range(2):
                q = 2 * m + kind
                high, low = halves(toeplitz(rows[q : q + 1], side))
                high = jnp.concatenate([high * masks[0], high * masks[1]], axis=1)
                low = jnp.concatenate([low * masks[0], low * masks[1]], axis=1)
                lefts.append(jnp.concatenate([high, high, low], axis=1))
                high, low = halves(toeplitz(mixed[kind], side))
                both = jnp.concatenate([high, low], axis=1)
                upper = jnp.concatenate([masks[2], masks[2]], axis=1)
                lower = jnp.concatenate([masks[3], masks[3]], axis=1)
                rights.append(jnp.concatenate([both * upper, both * lower], axis=0))
        images = jnp.concatenate([image_high, image_low, image_high], axis=0)
        total = jnp.zeros((2 * side, 2 * side), jnp.float32)
        for q in range(2 * widths):
            high, low = halves(dot(lefts[q], images, ((1,), (0,))))
            total = total + dot(jnp.concatenate([high, low], axis=0), rights[q], ((1,), (0,)))
        warped = total[:side, :side] + (total[:side, side:] + total[side:, :side])
        weighted = (1.0 / variance[b]) * warped
        for r in range(depth):
            cut = slice(r * slices, (r + 1) * slices)
            out[pl.ds(r * count + k, slices, stride=pitch), :] = weighted[cut]


def tile_kernel(weights, incoming, out, cells, strips, *, count, visits, prows, pcols):
    slices, pitch, side = incoming.shape
    depth = side // slices
    owners = prows * pcols
    per_patch = PB * PB
    tiles = owners * per_patch
    blocks = slices * count
    names = weights[pl.ds(pitch, slices, stride=pitch + 1), :]
    names = pltpu.roll(names, 0, 1, stride=count, stride_axis=0)
    per_row = side // count
    named = jnp.concatenate(
        [
            jnp.sum(names[first : first + per_row], axis=0, keepdims=True)
            for first in range(0, slices, per_row)
        ],
        axis=1,
    )
    places = lax.broadcasted_iota(jnp.int32, (tiles, blocks), 0).astype(jnp.float32)
    chosen = jnp.where(named == places, 1.0, 0.0).astype(jnp.bfloat16)

    def summed(data):
        high, low = halves(data)
        both = dot(chosen, jnp.concatenate([high, low], axis=1), ((1,), (0,)))
        return both[:, :side] + both[:, side:]

    for r in range(depth):
        flux = summed(incoming[:, r * count : (r + 1) * count, :].reshape(blocks, side))
        starts = [j * (pitch + 1) + r * count for j in range(slices)]
        weight = summed(
            jnp.concatenate([weights[start : start + count, :] for start in starts], axis=0)
        )
        cells[r * tiles : (r + 1) * tiles, :] = flux / (1.0 + weight)
    lane = lax.broadcasted_iota(jnp.int32, (PB, side), 1)
    for o in range(owners):
        for r in range(depth):
            strip = jnp.zeros((PB, side), jnp.float32)
            if o % pcols < pcols - 1:
                after = cells[pl.ds(r * tiles + (o + 1) * per_patch, PB, stride=PB), :]
                strip = jnp.where(lane < RF, after, strip)
            if o % pcols > 0:
                before = cells[pl.ds(r * tiles + (o - 1) * per_patch + PB - 1, PB, stride=PB), :]
                strip = jnp.where(lane >= side - RF, before, strip)
            strips[(o * depth + r) * PB : (o * depth + r + 1) * PB, :] = strip
    group = side // (2 * RF)
    packed = pltpu.roll(strips[...], RF, 1, stride=2 * RF, stride_axis=0)
    packed = jnp.sum(packed.reshape(owners * depth * PB // group, group, side), axis=1)
    lines = depth * PB // group
    upper = lax.axis_index(AXES) >= RF
    for o in range(owners):
        below = jnp.zeros((PB, side), jnp.float32)
        above = jnp.zeros((PB, side), jnp.float32)
        corner_below = jnp.zeros((1, side), jnp.float32)
        corner_above = jnp.zeros((1, side), jnp.float32)
        if o + pcols < owners:
            start = (o + pcols) * per_patch
            below = cells[start : start + PB, :]
            start = (o + pcols) * depth * PB
            corner_below = strips[start : start + 1, :]
        if o >= pcols:
            start = (depth - 1) * tiles + (o - pcols) * per_patch + per_patch - PB
            above = cells[start : start + PB, :]
            start = (o - pcols + 1) * depth * PB - 1
            corner_above = strips[start : start + 1, :]
        outer = jnp.where(upper, above, below)
        corner = jnp.where(upper, corner_above, corner_below)
        for v in range(visits):
            to = v * owners + o
            for r in range(depth):
                start = r * tiles + o * per_patch
                out[to, r * per_patch : (r + 1) * per_patch, :] = cells[start : start + per_patch, :]
            start = depth * per_patch
            out[to, start : start + lines, :] = packed[o * lines : (o + 1) * lines]
            start = start + lines
            out[to, start : start + PB, :] = outer
            start = start + PB
            out[to, start : start + 1, :] = corner


def filter_kernel(
    taps, incoming, coadd, detection, across, coadd_part, detection_part, sems, *, slices
):
    pitch = incoming.shape[0] // slices
    side = incoming.shape[1]
    depth = side // slices
    per_patch = PB * PB
    group = side // (2 * RF)
    lines = depth * PB // group
    lane = lax.broadcasted_iota(jnp.int32, (8, WRAP), 1)
    centred = jnp.zeros((8, WRAP), jnp.float32)
    leading = jnp.zeros((8, WRAP), jnp.float32)
    for b in range(2 * RF + 1):
        centred = jnp.where(lane == (RF - b) % WRAP, taps[b], centred)
        leading = jnp.where(lane == b, taps[b], leading)
    across_band = toeplitz(centred[0:1], WRAP)[:, :side]
    down_band = toeplitz(leading[0:1], side)
    across_high, across_low = halves(across_band)
    across_both = jnp.concatenate([across_high, across_low], axis=1)
    down_high, down_low = halves(down_band[:, : side + 2 * RF])
    down_both = jnp.concatenate([down_high, down_low], axis=0)

    def filtered(parts, ends, start):
        rows = ends.shape[0]
        left = lax.broadcasted_iota(jnp.int32, (rows, side), 1) < side // 2
        whole = []
        for c in range(PB):
            after = parts[c + 1] if c < PB - 1 else ends
            before = parts[c - 1] if c > 0 else ends
            beside = jnp.where(left, after, before)
            whole.append(jnp.concatenate([parts[c], beside], axis=1))
        high, low = halves(jnp.concatenate(whole, axis=0))
        both = dot(high, across_both, ((1,), (0,)))
        result = both[:, :side] + both[:, side:] + dot(low, across_high, ((1,), (0,)))
        for c in range(PB):
            cut = result[c * rows : (c + 1) * rows]
            across[start : start + rows, c * side : (c + 1) * side] = cut

    def line(index, first, rows):
        return incoming[pl.ds(first * pitch + index, rows, stride=pitch), :]

    def leave(part, whole, p, index):
        cut = pl.ds(p * side, side)
        copy = pltpu.make_async_copy(part.at[cut], whole.at[cut], sems.at[index, p])
        copy.start()
        return copy

    def down(p):
        high, low = halves(across[p * side : (p + 1) * side + 2 * RF, :])
        both = dot(down_both, high, ((1,), (0,)))
        result = both[:side] + both[side:] + dot(down_high, low, ((1,), (0,)))
        detection_part[p * side : (p + 1) * side, :] = result
        return leave(detection_part, detection, p, 1)

    copies = []
    start = depth * per_patch + lines
    for first, place in ((slices - RF, 0), (0, RF + PB * side)):
        parts = [line(start + c, first, RF) for c in range(PB)]
        filtered(parts, line(start + PB, first, RF), place)
    for p in range(PB):
        parts = []
        for c in range(PB):
            tile = jnp.concatenate(
                [line(r * per_patch + p * PB + c, 0, slices) for r in range(depth)], axis=0
            )
            coadd_part[p * side : (p + 1) * side, c * side : (c + 1) * side] = tile
            parts.append(tile)
        copies.append(leave(coadd_part, coadd, p, 0))
        ends = []
        for r in range(depth):
            number = r * PB + p
            strip = line(depth * per_patch + number // group, 0, slices)
            turn = -(2 * RF * (number % group) + RF) % side
            ends.append(pltpu.roll(strip, turn, 1) if turn else strip)
        filtered(parts, jnp.concatenate(ends, axis=0), RF + p * side)
        if p > 0:
            copies.append(down(p - 1))
    copies.append(down(PB - 1))
    for copy in copies:
        copy.wait()


def sliced_body(
    stamps, variance, coefficients, band_offsets, shifts, destination, position, psf_taps
):
    count = stamps.shape[0]
    side = variance.shape[1]
    slices = lax.axis_size(AXES)
    depth = side // slices
    visits = lax.axis_size("visit")
    prows = lax.axis_size("prow")
    pcols = lax.axis_size("pcol")
    owners = prows * pcols
    tiles = owners * PB * PB
    span = S
    batch = 2 if count % 2 == 0 else 1
    smem = pl.BlockSpec(memory_space=pltpu.SMEM)
    vmem = pl.BlockSpec(memory_space=pltpu.VMEM)
    pitch = depth * count + 1
    weights = pl.pallas_call(
        functools.partial(weight_kernel, slices=slices),
        in_specs=[vmem, smem, smem],
        out_specs=vmem,
        out_shape=jax.ShapeDtypeStruct((slices * pitch, side), jnp.float32),
    )(variance, destination, position)
    weights = lax.all_to_all(
        weights.reshape(slices, pitch, 1, side), AXES, split_axis=0, concat_axis=0, tiled=True
    )
    tables = jnp.asarray(lagged_tables(KR, side))
    images = stamps.reshape(count, span, span)
    pitch = depth * count
    outgoing = pl.pallas_call(
        functools.partial(warp_kernel, slices=slices, batch=batch),
        grid=(count // batch,),
        in_specs=[
            pl.BlockSpec((batch, span, span), lambda k: (k, 0, 0)),
            pl.BlockSpec((batch, side, side), lambda k: (k, 0, 0)),
            smem,
            smem,
            smem,
            pl.BlockSpec(tables.shape, lambda k: (0, 0, 0, 0)),
        ],
        out_specs=pl.BlockSpec((slices * pitch, side), lambda k: (0, 0)),
        out_shape=jax.ShapeDtypeStruct((slices * pitch, side), jnp.float32),
        scratch_shapes=[
            pltpu.VMEM((batch, 4 * side, 2 * side), jnp.bfloat16),
            pltpu.VMEM((4, side, side), jnp.bfloat16),
            pltpu.VMEM((2, count, side), jnp.float32),
        ],
    )(images, variance, coefficients, band_offsets.T, shifts.T, tables)
    outgoing, weights = lax.optimization_barrier((outgoing, weights))
    incoming = lax.all_to_all(
        outgoing.reshape(slices, pitch, side), AXES, split_axis=0, concat_axis=0, tiled=True
    )
    group = side // (2 * RF)
    length = depth * PB * PB + depth * PB // group + PB + 1
    length = -(-length // 8) * 8
    shares = pl.pallas_call(
        functools.partial(tile_kernel, count=count, visits=visits, prows=prows, pcols=pcols),
        in_specs=[vmem, vmem],
        out_specs=vmem,
        out_shape=pltpu.VMEM((slices, length, side), jnp.float32),
        scratch_shapes=[
            pltpu.VMEM((depth * tiles, side), jnp.float32),
            pltpu.VMEM((owners * depth * PB, side), jnp.float32),
        ],
    )(kept(weights.reshape(-1, side)), kept(incoming))
    gathered = lax.all_to_all(shares, AXES, split_axis=0, concat_axis=0, tiled=True)
    extent = PB * side
    return pl.pallas_call(
        functools.partial(filter_kernel, slices=slices),
        in_specs=[smem, vmem],
        out_specs=[pl.BlockSpec(memory_space=pl.ANY)] * 2,
        out_shape=[jax.ShapeDtypeStruct((extent, extent), jnp.float32)] * 2,
        scratch_shapes=[
            pltpu.VMEM((extent + 2 * RF, extent), jnp.float32),
            pltpu.VMEM((extent, extent), jnp.float32),
            pltpu.VMEM((extent, extent), jnp.float32),
            pltpu.SemaphoreType.DMA((2, PB)),
        ],
    )(psf_taps, kept(gathered.reshape(slices * length, side)))


def kept(values):
    return pltpu.with_memory_space_constraint(values, pltpu.VMEM)


def slices_fit(mesh, count, side):
    total = mesh.shape["visit"] * mesh.shape["prow"] * mesh.shape["pcol"]
    tiles = mesh.shape["prow"] * mesh.shape["pcol"] * PB * PB
    group = side // (2 * RF)
    if side % total or total < RF or tiles % side or WRAP != 2 * side:
        return False
    return (side // total * PB) % group == 0 and total * count % side == 0


def body(*args):
    mesh = jax.sharding.get_abstract_mesh()
    if slices_fit(mesh, *args[1].shape[:2]):
        return tuple(sliced_body(*args))
    return owner_body(*args)


def solution(mesh):
    placed = (
        P(("visit", "prow", "pcol"), None),
        P(("visit", "prow", "pcol"), None, None),
        P(("visit", "prow", "pcol"), None),
        P(("visit", "prow", "pcol"), None),
        P(("visit", "prow", "pcol"), None),
        P(("visit", "prow", "pcol")),
        P(("visit", "prow", "pcol")),
        P(),
    )
    return jax.shard_map(
        body,
        mesh=mesh,
        in_specs=placed,
        out_specs=(P("prow", "pcol"), P("prow", "pcol")),
        check_vma=False,
    )
```

```python
import functools

import jax
import jax.numpy as jnp
import numpy as np
from jax import lax
from jax.experimental import pallas as pl
from jax.experimental.pallas import tpu as pltpu
from jax.sharding import PartitionSpec as P

S = 192
KR = 15
PB = 4
RF = 8


basis_widths = (1.0, 2.0, 4.0)


def extended(cells, sides, width):
    for axis, dim in sides:
        count = lax.axis_size(axis)
        ends = count - 1
        head = lax.slice_in_dim(cells, 0, width, axis=dim)
        tail = lax.slice_in_dim(cells, cells.shape[dim] - width, cells.shape[dim], axis=dim)
        cells = jnp.concatenate(
            [
                lax.ppermute(tail, axis, [(i, (i + 1) % count) for i in range(ends)]),
                cells,
                lax.ppermute(head, axis, [((i + 1) % count, i) for i in range(ends)]),
            ],
            axis=dim,
        )
    return cells


def factor_tables(span, radius):
    matched_len = span - 2 * radius
    row_index = jnp.arange(matched_len, dtype=jnp.int32)[:, None]
    col_index = jnp.arange(span, dtype=jnp.int32)[None, :]
    lag_index = col_index - row_index - radius
    inside = (jnp.abs(lag_index) <= radius).astype(jnp.float32)
    lagged = lag_index.astype(jnp.float32)
    offsets = jnp.arange(-radius, radius + 1, dtype=jnp.int32).astype(jnp.float32)
    result = []
    for width in basis_widths:
        scaled = offsets / width
        gauss_norm = jnp.sqrt(jnp.sum(jnp.exp(-scaled * scaled)))
        quad_norm = jnp.sqrt(jnp.sum(scaled**4 * jnp.exp(-scaled * scaled)))
        ratio = lagged / width
        bell = jnp.exp(-0.5 * ratio * ratio) * inside
        result.append(jnp.stack([bell / gauss_norm, ratio * ratio * bell / quad_norm]))
    return jnp.stack(result)


def lanczos_bands(offsets, fractions, out_len, in_len):
    row_index = jnp.arange(out_len, dtype=jnp.int32)[None, :, None]
    col_index = jnp.arange(in_len, dtype=jnp.int32)[None, None, :]
    start = offsets[:, None, None]
    distance = (col_index - row_index - start).astype(jnp.float32) - fractions[:, None, None]
    return jnp.where(jnp.abs(distance) < 3.0, jnp.sinc(distance) * jnp.sinc(distance / 3.0), 0.0)


def warp_blocks(stamps, coefficients, band_offsets, shifts, tables, side):
    highest = lax.Precision.HIGHEST
    count = stamps.shape[0]
    matched_len = tables.shape[2]
    matched = jnp.zeros((count, matched_len, matched_len), jnp.float32)
    for width_index in range(len(basis_widths)):
        bell = tables[width_index, 0]
        quad = tables[width_index, 1]
        rows_bell = jnp.einsum(
            "ms,bst->bmt", bell, stamps, precision=highest, preferred_element_type=jnp.float32
        )
        rows_quad = jnp.einsum(
            "ms,bst->bmt", quad, stamps, precision=highest, preferred_element_type=jnp.float32
        )
        first = coefficients[:, 3 * width_index][:, None, None]
        second = coefficients[:, 3 * width_index + 1][:, None, None]
        third = coefficients[:, 3 * width_index + 2][:, None, None]
        left = first * rows_bell + second * rows_quad
        matched = matched + jnp.einsum(
            "bmt,nt->bmn", left, bell, precision=highest, preferred_element_type=jnp.float32
        )
        matched = matched + third * jnp.einsum(
            "bmt,nt->bmn", rows_bell, quad, precision=highest, preferred_element_type=jnp.float32
        )
    band_rows = lanczos_bands(band_offsets[:, 0], shifts[:, 0], side, matched_len)
    band_cols = lanczos_bands(band_offsets[:, 1], shifts[:, 1], side, matched_len)
    halfway = jnp.einsum(
        "bim,bmn->bin", band_rows, matched, precision=highest, preferred_element_type=jnp.float32
    )
    return jnp.einsum(
        "bin,bjn->bij", halfway, band_cols, precision=highest, preferred_element_type=jnp.float32
    )


def filter_band(taps, length, radius):
    row_index = jnp.arange(length, dtype=jnp.int32)[:, None]
    col_index = jnp.arange(length + 2 * radius, dtype=jnp.int32)[None, :]
    lag_index = col_index - row_index
    band = jnp.zeros((length, length + 2 * radius), jnp.float32)
    for tap_index in range(2 * radius + 1):
        band = band + jnp.where(lag_index == tap_index, taps[tap_index], 0.0)
    return band


def owner_body(stamps, variance, coefficients, band_offsets, shifts, destination, position, psf_taps):
    highest = lax.Precision.HIGHEST
    count = stamps.shape[0]
    span = S
    side = variance.shape[1]
    row_owners = lax.axis_size("prow")
    col_owners = lax.axis_size("pcol")
    owners = row_owners * col_owners
    capacity = max(2, 2 * count // owners)
    tables = factor_tables(span, KR)
    images = stamps.reshape(count, span, span)
    warped = warp_blocks(images, coefficients, band_offsets, shifts, tables, side)
    weight = 1.0 / variance
    terms = jnp.stack([weight * warped, weight], axis=1)
    owner_ids = jnp.arange(owners, dtype=jnp.int32)
    onehot = (destination[:, None] == owner_ids[None, :]).astype(jnp.int32)
    block_ids = jnp.arange(count, dtype=jnp.int32)
    earlier = (block_ids[None, :] < block_ids[:, None]).astype(jnp.int32)
    before = jnp.sum(earlier[:, :, None] * onehot[None, :, :], axis=1)
    rank = jnp.sum(before * onehot, axis=1)
    slot_ids = jnp.arange(capacity, dtype=jnp.int32)
    select = onehot.T[:, None, :] * (rank[None, None, :] == slot_ids[None, :, None]).astype(
        jnp.int32
    )
    send_pos = jnp.sum(select * (position[None, None, :] + 1), axis=2) - 1
    outgoing = jnp.einsum(
        "okb,bxij->okxij",
        select.astype(jnp.float32),
        terms,
        precision=highest,
        preferred_element_type=jnp.float32,
    )
    incoming, arrived = (
        lax.all_to_all(outgoing, ("prow", "pcol"), split_axis=0, concat_axis=0, tiled=True),
        lax.all_to_all(send_pos, ("prow", "pcol"), split_axis=0, concat_axis=0, tiled=True),
    )
    flattened = incoming.reshape(owners * capacity, 2 * side * side)
    tile_ids = jnp.arange(PB * PB, dtype=jnp.int32)
    placing = (arrived.reshape(owners * capacity)[None, :] == tile_ids[:, None]).astype(jnp.float32)
    tile_sums = jnp.dot(placing, flattened, precision=highest, preferred_element_type=jnp.float32)
    patch_sums = (
        tile_sums.reshape(PB, PB, 2, side, side)
        .transpose(2, 0, 3, 1, 4)
        .reshape(2, PB * side, PB * side)
    )
    shares = lax.psum_scatter(patch_sums, "visit", scatter_dimension=1, tiled=True)
    coadd = lax.all_gather(shares[0] / (1.0 + shares[1]), "visit", axis=0, tiled=True)
    padded = extended(coadd, (("prow", 0), ("pcol", 1)), RF)
    band = filter_band(psf_taps, coadd.shape[0], RF)
    across = jnp.dot(band, padded, precision=highest, preferred_element_type=jnp.float32)
    detection = jnp.dot(across, band.T, precision=highest, preferred_element_type=jnp.float32)
    return (coadd, detection)


TAPS = 6
AXES = ("visit", "prow", "pcol")
WRAP = 256
WINDOW = 80
BATCH = 2


def halves(values):
    high = values.astype(jnp.bfloat16)
    return high, (values - high.astype(jnp.float32)).astype(jnp.bfloat16)


def dot(left, right, contract):
    return lax.dot_general(left, right, (contract, ((), ())), preferred_element_type=jnp.float32)


def toeplitz(row, rows):
    spread = jnp.broadcast_to(row, (rows, row.shape[1]))
    return pltpu.roll(spread, 0, 1, stride=1, stride_axis=0)


def lagged_tables(radius, period, sign):
    lags = np.arange(-radius, radius + 1, dtype=np.float64)
    tables = np.zeros((TAPS, 8, period), np.float64)
    for index, width in enumerate(basis_widths):
        ratio = lags / width
        bell = np.exp(-0.5 * ratio * ratio)
        quad = ratio * ratio * bell
        for kind, factor in enumerate((bell, quad)):
            normed = factor / np.sqrt(np.sum(factor * factor))
            for n in range(TAPS):
                places = sign * (np.arange(2 * radius + 1) + n - 2)
                tables[n, 2 * index + kind, places % period] = normed
    return jnp.asarray(tables.astype(np.float32))


def lanczos(distance):
    def sinc(x):
        angle = jnp.float32(np.pi) * x
        return jnp.where(x == 0.0, 1.0, jnp.sin(angle) / jnp.where(x == 0.0, 1.0, angle))

    return jnp.where(jnp.abs(distance) < 3.0, sinc(distance) * sinc(distance / 3.0), 0.0)


def warp_kernel(
    stamps,
    variance,
    coefs,
    offsets,
    shifts,
    dest,
    pos,
    row_tables,
    col_tables,
    out,
    image,
    masks,
    taps,
    *,
    slices,
    span,
    batch,
):
    count, side = variance.shape[:2]
    depth = side // slices
    pitch = 2 * depth * count + 1
    widths = len(basis_widths)
    rows_even = span // 2
    rest = span - side
    step = 3 * count
    image[...] = jnp.zeros(image.shape, image.dtype)
    row = lax.broadcasted_iota(jnp.int32, (side, side), 0)
    col = lax.broadcasted_iota(jnp.int32, (side, side), 1)
    for index, test in enumerate((col <= row, col > row)):
        mask = jnp.where(test, 1.0, 0.0).astype(jnp.bfloat16)
        masks[index] = jnp.concatenate([mask, mask], axis=1)
    lane = lax.broadcasted_iota(jnp.int32, (count, side), 1)
    level = lax.broadcasted_iota(jnp.int32, (count, side), 0)
    for axis in range(2):
        part = jnp.zeros((count, side), jnp.float32)
        for k in range(count):
            part = jnp.where(level == k, shifts[axis, k], part)
        taps[axis] = lanczos((lane - 2).astype(jnp.float32) - part)
    lane = lax.broadcasted_iota(jnp.int32, (slices, side), 1)
    names = jnp.zeros((slices, side), jnp.float32)
    for k in range(count):
        tile = (dest[k] * (PB * PB) + pos[k]).astype(jnp.float32)
        names = jnp.where(lane == k, tile, names)
    out[pl.ds(pitch - 1, slices, stride=pitch), :] = names
    early = lax.broadcasted_iota(jnp.int32, (rows_even, side), 1) < rest

    def mixed(axis, k, tables):
        values = taps[axis, pl.ds(k, 1), :]
        total = jnp.zeros(tables.shape[1:], jnp.float32)
        for n in range(TAPS):
            total = total + values[:, n : n + 1] * tables[n]
        return total

    def one_block(k, b):
        first = stamps[pl.ds(k, rows_even, stride=step), :]
        second = stamps[pl.ds(count + k, rows_even, stride=step), :]
        third = stamps[pl.ds(2 * count + k, rows_even, stride=step), :]
        second_turned = pltpu.roll(second, rest, 1)
        third_turned = pltpu.roll(third, rest, 1)
        image[b, 0, pl.ds(0, rows_even, stride=2), :] = first
        image[b, 1, pl.ds(0, rows_even, stride=2), :] = second
        image[b, 0, pl.ds(1, rows_even, stride=2), :] = jnp.where(
            early, second_turned, third_turned
        )
        image[b, 1, pl.ds(1, rows_even, stride=2), :] = third_turned
        offset = offsets[0, k]
        base = lax.div(offset - 2, 8) * 8
        row_taps = pltpu.roll(mixed(0, k, row_tables), offset - base, 1)
        high = row_taps.astype(jnp.bfloat16).astype(jnp.float32)
        low = (row_taps - high).astype(jnp.bfloat16).astype(jnp.float32)
        lined = high + pltpu.roll(high, WINDOW, 1) + pltpu.roll(low, 2 * WINDOW, 1)
        left = jnp.concatenate(
            [toeplitz(lined[q : q + 1], slices) for q in range(2 * widths)], axis=0
        ).astype(jnp.bfloat16)
        across = []
        for w in range(depth):
            start = pl.multiple_of(w * slices + base, 8)
            window = jnp.concatenate(
                [image[b, half, pl.ds(start, WINDOW), :] for half in range(2)], axis=1
            )
            high, low = halves(window)
            none = jnp.zeros((WRAP - 3 * WINDOW, 2 * side), jnp.bfloat16)
            right = jnp.concatenate([high, low, high, none], axis=0)
            across.append(dot(left, right, ((1,), (0,)))[:, :span])
        offset = offsets[1, k]
        col_taps = pltpu.roll(mixed(1, k, col_tables), side - offset, 1)
        total = jnp.zeros((2 * side, 2 * side), jnp.float32)
        for m in range(widths):
            bell = col_taps[2 * m : 2 * m + 1]
            quad = col_taps[2 * m + 1 : 2 * m + 2]
            pair = (
                coefs[k, 3 * m] * bell + coefs[k, 3 * m + 2] * quad,
                coefs[k, 3 * m + 1] * bell,
            )
            for kind in range(2):
                q = 2 * m + kind
                high, low = halves(toeplitz(pair[kind], side))
                both = jnp.concatenate([high, low], axis=1)
                right = jnp.concatenate([both * masks[0], both[:rest] * masks[1, :rest]], axis=0)
                cut = slice(q * slices, (q + 1) * slices)
                high, low = halves(jnp.concatenate([part[cut] for part in across], axis=0))
                total = total + dot(jnp.concatenate([high, low], axis=0), right, ((1,), (0,)))
        warped = total[:side, :side] + (total[:side, side:] + total[side:, :side])
        weight = 1.0 / variance[k]
        weighted = weight * warped
        for r in range(depth):
            cut = slice(r * slices, (r + 1) * slices)
            out[pl.ds(r * count + k, slices, stride=pitch), :] = weighted[cut]
            out[pl.ds((depth + r) * count + k, slices, stride=pitch), :] = weight[cut]

    def some_blocks(index, carry):
        for b in range(batch):
            one_block(index * batch + b, b)
        return carry

    lax.fori_loop(0, count // batch, some_blocks, 0)


def tile_kernel(incoming, out, cells, strips, *, slices, count, visits, prows, pcols):
    pitch = incoming.shape[0] // slices
    side = incoming.shape[1]
    depth = side // slices
    owners = prows * pcols
    per_patch = PB * PB
    tiles = owners * per_patch
    blocks = slices * count
    names = incoming[pl.ds(pitch - 1, slices, stride=pitch), :]
    names = pltpu.roll(names, 0, 1, stride=count, stride_axis=0)
    per_row = side // count
    named = jnp.concatenate(
        [
            jnp.sum(names[first : first + per_row], axis=0, keepdims=True)
            for first in range(0, slices, per_row)
        ],
        axis=1,
    )
    places = lax.broadcasted_iota(jnp.int32, (tiles, blocks), 0).astype(jnp.float32)
    chosen = jnp.where(named == places, 1.0, 0.0).astype(jnp.bfloat16)

    def summed(index):
        starts = [j * pitch + index * count for j in range(slices)]
        data = jnp.concatenate([incoming[start : start + count, :] for start in starts], axis=0)
        high, low = halves(data)
        both = dot(chosen, jnp.concatenate([high, low], axis=1), ((1,), (0,)))
        return both[:, :side] + both[:, side:]

    for r in range(depth):
        cells[r * tiles : (r + 1) * tiles, :] = summed(r) / (1.0 + summed(depth + r))
    lane = lax.broadcasted_iota(jnp.int32, (PB, side), 1)
    for o in range(owners):
        for r in range(depth):
            strip = jnp.zeros((PB, side), jnp.float32)
            if o % pcols < pcols - 1:
                after = cells[pl.ds(r * tiles + (o + 1) * per_patch, PB, stride=PB), :]
                strip = jnp.where(lane < RF, after, strip)
            if o % pcols > 0:
                before = cells[pl.ds(r * tiles + (o - 1) * per_patch + PB - 1, PB, stride=PB), :]
                strip = jnp.where(lane >= side - RF, before, strip)
            strips[(o * depth + r) * PB : (o * depth + r + 1) * PB, :] = strip
    group = side // (2 * RF)
    packed = pltpu.roll(strips[...], RF, 1, stride=2 * RF, stride_axis=0)
    packed = jnp.sum(packed.reshape(owners * depth * PB // group, group, side), axis=1)
    lines = depth * PB // group
    upper = lax.axis_index(AXES) >= RF
    for o in range(owners):
        below = jnp.zeros((PB, side), jnp.float32)
        above = jnp.zeros((PB, side), jnp.float32)
        corner_below = jnp.zeros((1, side), jnp.float32)
        corner_above = jnp.zeros((1, side), jnp.float32)
        if o + pcols < owners:
            start = (o + pcols) * per_patch
            below = cells[start : start + PB, :]
            start = (o + pcols) * depth * PB
            corner_below = strips[start : start + 1, :]
        if o >= pcols:
            start = (depth - 1) * tiles + (o - pcols) * per_patch + per_patch - PB
            above = cells[start : start + PB, :]
            start = (o - pcols + 1) * depth * PB - 1
            corner_above = strips[start : start + 1, :]
        outer = jnp.where(upper, above, below)
        corner = jnp.where(upper, corner_above, corner_below)
        for v in range(visits):
            to = v * owners + o
            for r in range(depth):
                start = r * tiles + o * per_patch
                out[to, r * per_patch : (r + 1) * per_patch, :] = cells[start : start + per_patch, :]
            start = depth * per_patch
            out[to, start : start + lines, :] = packed[o * lines : (o + 1) * lines]
            start = start + lines
            out[to, start : start + PB, :] = outer
            start = start + PB
            out[to, start : start + 1, :] = corner


def filter_kernel(
    taps, incoming, coadd, detection, across, coadd_part, detection_part, sems, *, slices
):
    pitch = incoming.shape[0] // slices
    side = incoming.shape[1]
    depth = side // slices
    per_patch = PB * PB
    group = side // (2 * RF)
    lines = depth * PB // group
    lane = lax.broadcasted_iota(jnp.int32, (8, WRAP), 1)
    centred = jnp.zeros((8, WRAP), jnp.float32)
    leading = jnp.zeros((8, WRAP), jnp.float32)
    for b in range(2 * RF + 1):
        centred = jnp.where(lane == (RF - b) % WRAP, taps[b], centred)
        leading = jnp.where(lane == b, taps[b], leading)
    across_band = toeplitz(centred[0:1], WRAP)[:, :side]
    down_band = toeplitz(leading[0:1], side)
    across_high, across_low = halves(across_band)
    across_both = jnp.concatenate([across_high, across_low], axis=1)
    down_high, down_low = halves(down_band[:, : side + 2 * RF])
    down_both = jnp.concatenate([down_high, down_low], axis=0)

    def filtered(parts, ends, start):
        rows = ends.shape[0]
        left = lax.broadcasted_iota(jnp.int32, (rows, side), 1) < side // 2
        whole = []
        for c in range(PB):
            after = parts[c + 1] if c < PB - 1 else ends
            before = parts[c - 1] if c > 0 else ends
            beside = jnp.where(left, after, before)
            whole.append(jnp.concatenate([parts[c], beside], axis=1))
        high, low = halves(jnp.concatenate(whole, axis=0))
        both = dot(high, across_both, ((1,), (0,)))
        result = both[:, :side] + both[:, side:] + dot(low, across_high, ((1,), (0,)))
        for c in range(PB):
            cut = result[c * rows : (c + 1) * rows]
            across[start : start + rows, c * side : (c + 1) * side] = cut

    def line(index, first, rows):
        return incoming[pl.ds(first * pitch + index, rows, stride=pitch), :]

    def leave(part, whole, p, index):
        cut = pl.ds(p * side, side)
        copy = pltpu.make_async_copy(part.at[cut], whole.at[cut], sems.at[index, p])
        copy.start()
        return copy

    def down(p):
        high, low = halves(across[p * side : (p + 1) * side + 2 * RF, :])
        both = dot(down_both, high, ((1,), (0,)))
        result = both[:side] + both[side:] + dot(down_high, low, ((1,), (0,)))
        detection_part[p * side : (p + 1) * side, :] = result
        return leave(detection_part, detection, p, 1)

    copies = []
    start = depth * per_patch + lines
    for first, place in ((slices - RF, 0), (0, RF + PB * side)):
        parts = [line(start + c, first, RF) for c in range(PB)]
        filtered(parts, line(start + PB, first, RF), place)
    for p in range(PB):
        parts = []
        for c in range(PB):
            tile = jnp.concatenate(
                [line(r * per_patch + p * PB + c, 0, slices) for r in range(depth)], axis=0
            )
            coadd_part[p * side : (p + 1) * side, c * side : (c + 1) * side] = tile
            parts.append(tile)
        copies.append(leave(coadd_part, coadd, p, 0))
        ends = []
        for r in range(depth):
            number = r * PB + p
            strip = line(depth * per_patch + number // group, 0, slices)
            turn = -(2 * RF * (number % group) + RF) % side
            ends.append(pltpu.roll(strip, turn, 1) if turn else strip)
        filtered(parts, jnp.concatenate(ends, axis=0), RF + p * side)
        if p > 0:
            copies.append(down(p - 1))
    copies.append(down(PB - 1))
    for copy in copies:
        copy.wait()


def sliced_body(
    stamps, variance, coefficients, band_offsets, shifts, destination, position, psf_taps
):
    count = stamps.shape[0]
    side = variance.shape[1]
    slices = lax.axis_size(AXES)
    depth = side // slices
    visits = lax.axis_size("visit")
    prows = lax.axis_size("prow")
    pcols = lax.axis_size("pcol")
    owners = prows * pcols
    tiles = owners * PB * PB
    span = S
    batch = BATCH if count % BATCH == 0 else 1
    smem = pl.BlockSpec(memory_space=pltpu.SMEM)
    vmem = pl.BlockSpec(memory_space=pltpu.VMEM)
    pitch = 2 * depth * count + 1
    lines = stamps.reshape(count, -1, side).transpose(1, 0, 2).reshape(-1, side)
    outgoing = pl.pallas_call(
        functools.partial(warp_kernel, slices=slices, span=span, batch=batch),
        in_specs=[vmem, vmem, smem, smem, smem, smem, smem, vmem, vmem],
        out_specs=vmem,
        out_shape=pltpu.VMEM((slices * pitch, side), jnp.float32),
        scratch_shapes=[
            pltpu.VMEM((batch, 2, span + 16, side), jnp.float32),
            pltpu.VMEM((2, side, 2 * side), jnp.bfloat16),
            pltpu.VMEM((2, count, side), jnp.float32),
        ],
    )(
        lines,
        variance,
        coefficients,
        band_offsets.T,
        shifts.T,
        destination,
        position,
        lagged_tables(KR, WRAP, 1),
        lagged_tables(KR, side, -1),
    )
    incoming = lax.all_to_all(
        outgoing.reshape(slices, pitch, 1, side), AXES, split_axis=0, concat_axis=0, tiled=True
    )
    group = side // (2 * RF)
    length = depth * PB * PB + depth * PB // group + PB + 1
    length = -(-length // 8) * 8
    shares = pl.pallas_call(
        functools.partial(
            tile_kernel, slices=slices, count=count, visits=visits, prows=prows, pcols=pcols
        ),
        in_specs=[vmem],
        out_specs=vmem,
        out_shape=pltpu.VMEM((slices, length, side), jnp.float32),
        scratch_shapes=[
            pltpu.VMEM((depth * tiles, side), jnp.float32),
            pltpu.VMEM((owners * depth * PB, side), jnp.float32),
        ],
    )(kept(incoming.reshape(-1, side)))
    gathered = lax.all_to_all(shares, AXES, split_axis=0, concat_axis=0, tiled=True)
    extent = PB * side
    return pl.pallas_call(
        functools.partial(filter_kernel, slices=slices),
        in_specs=[smem, vmem],
        out_specs=[pl.BlockSpec(memory_space=pl.ANY)] * 2,
        out_shape=[jax.ShapeDtypeStruct((extent, extent), jnp.float32)] * 2,
        scratch_shapes=[
            pltpu.VMEM((extent + 2 * RF, extent), jnp.float32),
            pltpu.VMEM((extent, extent), jnp.float32),
            pltpu.VMEM((extent, extent), jnp.float32),
            pltpu.SemaphoreType.DMA((2, PB)),
        ],
    )(psf_taps, kept(gathered.reshape(slices * length, side)))


def kept(values):
    return pltpu.with_memory_space_constraint(values, pltpu.VMEM)


def slices_fit(mesh, count, side):
    total = mesh.shape["visit"] * mesh.shape["prow"] * mesh.shape["pcol"]
    tiles = mesh.shape["prow"] * mesh.shape["pcol"] * PB * PB
    group = side // (2 * RF)
    if side % total or total < RF or tiles % side or WRAP != 2 * side:
        return False
    if total + 2 * KR + TAPS + 8 > WINDOW or (side // total * PB) % group:
        return False
    return total * count % side == 0 and 2 * S == 3 * side


def body(*args):
    mesh = jax.sharding.get_abstract_mesh()
    if slices_fit(mesh, *args[1].shape[:2]):
        return tuple(sliced_body(*args))
    return owner_body(*args)


def solution(mesh):
    placed = (
        P(("visit", "prow", "pcol"), None),
        P(("visit", "prow", "pcol"), None, None),
        P(("visit", "prow", "pcol"), None),
        P(("visit", "prow", "pcol"), None),
        P(("visit", "prow", "pcol"), None),
        P(("visit", "prow", "pcol")),
        P(("visit", "prow", "pcol")),
        P(),
    )
    return jax.shard_map(
        body,
        mesh=mesh,
        in_specs=placed,
        out_specs=(P("prow", "pcol"), P("prow", "pcol")),
        check_vma=False,
    )
```

```python
import functools

import jax
import jax.numpy as jnp
import numpy as np
from jax import lax
from jax.experimental import pallas as pl
from jax.experimental.pallas import tpu as pltpu
from jax.sharding import PartitionSpec as P

S = 192
KR = 15
PB = 4
RF = 8


basis_widths = (1.0, 2.0, 4.0)


def extended(cells, sides, width):
    for axis, dim in sides:
        count = lax.axis_size(axis)
        ends = count - 1
        head = lax.slice_in_dim(cells, 0, width, axis=dim)
        tail = lax.slice_in_dim(cells, cells.shape[dim] - width, cells.shape[dim], axis=dim)
        cells = jnp.concatenate(
            [
                lax.ppermute(tail, axis, [(i, (i + 1) % count) for i in range(ends)]),
                cells,
                lax.ppermute(head, axis, [((i + 1) % count, i) for i in range(ends)]),
            ],
            axis=dim,
        )
    return cells


def factor_tables(span, radius):
    matched_len = span - 2 * radius
    row_index = jnp.arange(matched_len, dtype=jnp.int32)[:, None]
    col_index = jnp.arange(span, dtype=jnp.int32)[None, :]
    lag_index = col_index - row_index - radius
    inside = (jnp.abs(lag_index) <= radius).astype(jnp.float32)
    lagged = lag_index.astype(jnp.float32)
    offsets = jnp.arange(-radius, radius + 1, dtype=jnp.int32).astype(jnp.float32)
    result = []
    for width in basis_widths:
        scaled = offsets / width
        gauss_norm = jnp.sqrt(jnp.sum(jnp.exp(-scaled * scaled)))
        quad_norm = jnp.sqrt(jnp.sum(scaled**4 * jnp.exp(-scaled * scaled)))
        ratio = lagged / width
        bell = jnp.exp(-0.5 * ratio * ratio) * inside
        result.append(jnp.stack([bell / gauss_norm, ratio * ratio * bell / quad_norm]))
    return jnp.stack(result)


def lanczos_bands(offsets, fractions, out_len, in_len):
    row_index = jnp.arange(out_len, dtype=jnp.int32)[None, :, None]
    col_index = jnp.arange(in_len, dtype=jnp.int32)[None, None, :]
    start = offsets[:, None, None]
    distance = (col_index - row_index - start).astype(jnp.float32) - fractions[:, None, None]
    return jnp.where(jnp.abs(distance) < 3.0, jnp.sinc(distance) * jnp.sinc(distance / 3.0), 0.0)


def warp_blocks(stamps, coefficients, band_offsets, shifts, tables, side):
    highest = lax.Precision.HIGHEST
    count = stamps.shape[0]
    matched_len = tables.shape[2]
    matched = jnp.zeros((count, matched_len, matched_len), jnp.float32)
    for width_index in range(len(basis_widths)):
        bell = tables[width_index, 0]
        quad = tables[width_index, 1]
        rows_bell = jnp.einsum(
            "ms,bst->bmt", bell, stamps, precision=highest, preferred_element_type=jnp.float32
        )
        rows_quad = jnp.einsum(
            "ms,bst->bmt", quad, stamps, precision=highest, preferred_element_type=jnp.float32
        )
        first = coefficients[:, 3 * width_index][:, None, None]
        second = coefficients[:, 3 * width_index + 1][:, None, None]
        third = coefficients[:, 3 * width_index + 2][:, None, None]
        left = first * rows_bell + second * rows_quad
        matched = matched + jnp.einsum(
            "bmt,nt->bmn", left, bell, precision=highest, preferred_element_type=jnp.float32
        )
        matched = matched + third * jnp.einsum(
            "bmt,nt->bmn", rows_bell, quad, precision=highest, preferred_element_type=jnp.float32
        )
    band_rows = lanczos_bands(band_offsets[:, 0], shifts[:, 0], side, matched_len)
    band_cols = lanczos_bands(band_offsets[:, 1], shifts[:, 1], side, matched_len)
    halfway = jnp.einsum(
        "bim,bmn->bin", band_rows, matched, precision=highest, preferred_element_type=jnp.float32
    )
    return jnp.einsum(
        "bin,bjn->bij", halfway, band_cols, precision=highest, preferred_element_type=jnp.float32
    )


def filter_band(taps, length, radius):
    row_index = jnp.arange(length, dtype=jnp.int32)[:, None]
    col_index = jnp.arange(length + 2 * radius, dtype=jnp.int32)[None, :]
    lag_index = col_index - row_index
    band = jnp.zeros((length, length + 2 * radius), jnp.float32)
    for tap_index in range(2 * radius + 1):
        band = band + jnp.where(lag_index == tap_index, taps[tap_index], 0.0)
    return band


def owner_body(stamps, variance, coefficients, band_offsets, shifts, destination, position, psf_taps):
    highest = lax.Precision.HIGHEST
    count = stamps.shape[0]
    span = S
    side = variance.shape[1]
    row_owners = lax.axis_size("prow")
    col_owners = lax.axis_size("pcol")
    owners = row_owners * col_owners
    capacity = max(2, 2 * count // owners)
    tables = factor_tables(span, KR)
    images = stamps.reshape(count, span, span)
    warped = warp_blocks(images, coefficients, band_offsets, shifts, tables, side)
    weight = 1.0 / variance
    terms = jnp.stack([weight * warped, weight], axis=1)
    owner_ids = jnp.arange(owners, dtype=jnp.int32)
    onehot = (destination[:, None] == owner_ids[None, :]).astype(jnp.int32)
    block_ids = jnp.arange(count, dtype=jnp.int32)
    earlier = (block_ids[None, :] < block_ids[:, None]).astype(jnp.int32)
    before = jnp.sum(earlier[:, :, None] * onehot[None, :, :], axis=1)
    rank = jnp.sum(before * onehot, axis=1)
    slot_ids = jnp.arange(capacity, dtype=jnp.int32)
    select = onehot.T[:, None, :] * (rank[None, None, :] == slot_ids[None, :, None]).astype(
        jnp.int32
    )
    send_pos = jnp.sum(select * (position[None, None, :] + 1), axis=2) - 1
    outgoing = jnp.einsum(
        "okb,bxij->okxij",
        select.astype(jnp.float32),
        terms,
        precision=highest,
        preferred_element_type=jnp.float32,
    )
    incoming, arrived = (
        lax.all_to_all(outgoing, ("prow", "pcol"), split_axis=0, concat_axis=0, tiled=True),
        lax.all_to_all(send_pos, ("prow", "pcol"), split_axis=0, concat_axis=0, tiled=True),
    )
    flattened = incoming.reshape(owners * capacity, 2 * side * side)
    tile_ids = jnp.arange(PB * PB, dtype=jnp.int32)
    placing = (arrived.reshape(owners * capacity)[None, :] == tile_ids[:, None]).astype(jnp.float32)
    tile_sums = jnp.dot(placing, flattened, precision=highest, preferred_element_type=jnp.float32)
    patch_sums = (
        tile_sums.reshape(PB, PB, 2, side, side)
        .transpose(2, 0, 3, 1, 4)
        .reshape(2, PB * side, PB * side)
    )
    shares = lax.psum_scatter(patch_sums, "visit", scatter_dimension=1, tiled=True)
    coadd = lax.all_gather(shares[0] / (1.0 + shares[1]), "visit", axis=0, tiled=True)
    padded = extended(coadd, (("prow", 0), ("pcol", 1)), RF)
    band = filter_band(psf_taps, coadd.shape[0], RF)
    across = jnp.dot(band, padded, precision=highest, preferred_element_type=jnp.float32)
    detection = jnp.dot(across, band.T, precision=highest, preferred_element_type=jnp.float32)
    return (coadd, detection)


TAPS = 6
AXES = ("visit", "prow", "pcol")
WRAP = 256
WINDOW = 80


def halves(values):
    high = values.astype(jnp.bfloat16)
    return high, (values - high.astype(jnp.float32)).astype(jnp.bfloat16)


def dot(left, right, contract):
    return lax.dot_general(left, right, (contract, ((), ())), preferred_element_type=jnp.float32)


def toeplitz(row, rows):
    spread = jnp.broadcast_to(row, (rows, row.shape[1]))
    return pltpu.roll(spread, 0, 1, stride=1, stride_axis=0)


def lagged_tables(radius, period, sign):
    lags = np.arange(-radius, radius + 1, dtype=np.float64)
    tables = np.zeros((TAPS, 8, period), np.float64)
    for index, width in enumerate(basis_widths):
        ratio = lags / width
        bell = np.exp(-0.5 * ratio * ratio)
        quad = ratio * ratio * bell
        for kind, factor in enumerate((bell, quad)):
            normed = factor / np.sqrt(np.sum(factor * factor))
            for n in range(TAPS):
                places = sign * (np.arange(2 * radius + 1) + n - 2)
                tables[n, 2 * index + kind, places % period] = normed
    return jnp.asarray(tables.astype(np.float32))


def lanczos(distance):
    def sinc(x):
        angle = jnp.float32(np.pi) * x
        return jnp.where(x == 0.0, 1.0, jnp.sin(angle) / jnp.where(x == 0.0, 1.0, angle))

    return jnp.where(jnp.abs(distance) < 3.0, sinc(distance) * sinc(distance / 3.0), 0.0)


def warp_kernel(
    stamps,
    variance,
    coefs,
    offsets,
    shifts,
    dest,
    pos,
    row_tables,
    col_tables,
    out,
    image,
    masks,
    taps,
    *,
    slices,
    span,
    batch,
):
    count, side = variance.shape[:2]
    depth = side // slices
    pitch = 2 * depth * count + 1
    widths = len(basis_widths)
    rows_even = span // 2
    rest = span - side
    step = 3 * count
    image[...] = jnp.zeros(image.shape, image.dtype)
    row = lax.broadcasted_iota(jnp.int32, (side, side), 0)
    col = lax.broadcasted_iota(jnp.int32, (side, side), 1)
    for index, test in enumerate((col <= row, col > row)):
        mask = jnp.where(test, 1.0, 0.0).astype(jnp.bfloat16)
        masks[index] = jnp.concatenate([mask, mask], axis=1)
    lane = lax.broadcasted_iota(jnp.int32, (count, side), 1)
    level = lax.broadcasted_iota(jnp.int32, (count, side), 0)
    for axis in range(2):
        part = jnp.zeros((count, side), jnp.float32)
        for k in range(count):
            part = jnp.where(level == k, shifts[axis, k], part)
        taps[axis] = lanczos((lane - 2).astype(jnp.float32) - part)
    lane = lax.broadcasted_iota(jnp.int32, (slices, side), 1)
    names = jnp.zeros((slices, side), jnp.float32)
    for k in range(count):
        tile = (dest[k] * (PB * PB) + pos[k]).astype(jnp.float32)
        names = jnp.where(lane == k, tile, names)
    out[pl.ds(pitch - 1, slices, stride=pitch), :] = names
    early = lax.broadcasted_iota(jnp.int32, (rows_even, side), 1) < rest

    def mixed(axis, k, tables):
        values = taps[axis, pl.ds(k, 1), :]
        total = jnp.zeros(tables.shape[1:], jnp.float32)
        for n in range(TAPS):
            total = total + values[:, n : n + 1] * tables[n]
        return total

    def one_block(k, b):
        first = stamps[pl.ds(k, rows_even, stride=step), :]
        second = stamps[pl.ds(count + k, rows_even, stride=step), :]
        third = stamps[pl.ds(2 * count + k, rows_even, stride=step), :]
        second_turned = pltpu.roll(second, rest, 1)
        third_turned = pltpu.roll(third, rest, 1)
        image[b, 0, pl.ds(0, rows_even, stride=2), :] = first
        image[b, 1, pl.ds(0, rows_even, stride=2), :] = second
        image[b, 0, pl.ds(1, rows_even, stride=2), :] = jnp.where(
            early, second_turned, third_turned
        )
        image[b, 1, pl.ds(1, rows_even, stride=2), :] = third_turned
        offset = offsets[0, k]
        base = lax.div(offset - 2, 8) * 8
        row_taps = pltpu.roll(mixed(0, k, row_tables), offset - base, 1)
        high = row_taps.astype(jnp.bfloat16).astype(jnp.float32)
        low = (row_taps - high).astype(jnp.bfloat16).astype(jnp.float32)
        lined = high + pltpu.roll(high, WINDOW, 1) + pltpu.roll(low, 2 * WINDOW, 1)
        left = jnp.concatenate(
            [toeplitz(lined[q : q + 1], slices) for q in range(2 * widths)], axis=0
        ).astype(jnp.bfloat16)
        across = []
        for w in range(depth):
            start = pl.multiple_of(w * slices + base, 8)
            window = jnp.concatenate(
                [image[b, half, pl.ds(start, WINDOW), :] for half in range(2)], axis=1
            )
            high, low = halves(window)
            none = jnp.zeros((WRAP - 3 * WINDOW, 2 * side), jnp.bfloat16)
            right = jnp.concatenate([high, low, high, none], axis=0)
            across.append(dot(left, right, ((1,), (0,)))[:, :span])
        offset = offsets[1, k]
        col_taps = pltpu.roll(mixed(1, k, col_tables), side - offset, 1)
        total = jnp.zeros((2 * side, 2 * side), jnp.float32)
        for m in range(widths):
            bell = col_taps[2 * m : 2 * m + 1]
            quad = col_taps[2 * m + 1 : 2 * m + 2]
            pair = (
                coefs[k, 3 * m] * bell + coefs[k, 3 * m + 2] * quad,
                coefs[k, 3 * m + 1] * bell,
            )
            for kind in range(2):
                q = 2 * m + kind
                high, low = halves(toeplitz(pair[kind], side))
                both = jnp.concatenate([high, low], axis=1)
                right = jnp.concatenate([both * masks[0], both[:rest] * masks[1, :rest]], axis=0)
                cut = slice(q * slices, (q + 1) * slices)
                high, low = halves(jnp.concatenate([part[cut] for part in across], axis=0))
                total = total + dot(jnp.concatenate([high, low], axis=0), right, ((1,), (0,)))
        warped = total[:side, :side] + (total[:side, side:] + total[side:, :side])
        weight = 1.0 / variance[k]
        weighted = weight * warped
        for r in range(depth):
            cut = slice(r * slices, (r + 1) * slices)
            out[pl.ds(r * count + k, slices, stride=pitch), :] = weighted[cut]
            out[pl.ds((depth + r) * count + k, slices, stride=pitch), :] = weight[cut]

    for k in range(count):
        one_block(k, k)


def tile_kernel(incoming, out, cells, strips, *, slices, count, visits, prows, pcols):
    pitch = incoming.shape[0] // slices
    side = incoming.shape[1]
    depth = side // slices
    owners = prows * pcols
    per_patch = PB * PB
    tiles = owners * per_patch
    blocks = slices * count
    names = incoming[pl.ds(pitch - 1, slices, stride=pitch), :]
    names = pltpu.roll(names, 0, 1, stride=count, stride_axis=0)
    per_row = side // count
    named = jnp.concatenate(
        [
            jnp.sum(names[first : first + per_row], axis=0, keepdims=True)
            for first in range(0, slices, per_row)
        ],
        axis=1,
    )
    places = lax.broadcasted_iota(jnp.int32, (tiles, blocks), 0).astype(jnp.float32)
    chosen = jnp.where(named == places, 1.0, 0.0).astype(jnp.bfloat16)

    def summed(index):
        starts = [j * pitch + index * count for j in range(slices)]
        data = jnp.concatenate([incoming[start : start + count, :] for start in starts], axis=0)
        high, low = halves(data)
        both = dot(chosen, jnp.concatenate([high, low], axis=1), ((1,), (0,)))
        return both[:, :side] + both[:, side:]

    for r in range(depth):
        cells[r * tiles : (r + 1) * tiles, :] = summed(r) / (1.0 + summed(depth + r))
    lane = lax.broadcasted_iota(jnp.int32, (PB, side), 1)
    for o in range(owners):
        for r in range(depth):
            strip = jnp.zeros((PB, side), jnp.float32)
            if o % pcols < pcols - 1:
                after = cells[pl.ds(r * tiles + (o + 1) * per_patch, PB, stride=PB), :]
                strip = jnp.where(lane < RF, after, strip)
            if o % pcols > 0:
                before = cells[pl.ds(r * tiles + (o - 1) * per_patch + PB - 1, PB, stride=PB), :]
                strip = jnp.where(lane >= side - RF, before, strip)
            strips[(o * depth + r) * PB : (o * depth + r + 1) * PB, :] = strip
    group = side // (2 * RF)
    packed = pltpu.roll(strips[...], RF, 1, stride=2 * RF, stride_axis=0)
    packed = jnp.sum(packed.reshape(owners * depth * PB // group, group, side), axis=1)
    lines = depth * PB // group
    upper = lax.axis_index(AXES) >= RF
    for o in range(owners):
        below = jnp.zeros((PB, side), jnp.float32)
        above = jnp.zeros((PB, side), jnp.float32)
        corner_below = jnp.zeros((1, side), jnp.float32)
        corner_above = jnp.zeros((1, side), jnp.float32)
        if o + pcols < owners:
            start = (o + pcols) * per_patch
            below = cells[start : start + PB, :]
            start = (o + pcols) * depth * PB
            corner_below = strips[start : start + 1, :]
        if o >= pcols:
            start = (depth - 1) * tiles + (o - pcols) * per_patch + per_patch - PB
            above = cells[start : start + PB, :]
            start = (o - pcols + 1) * depth * PB - 1
            corner_above = strips[start : start + 1, :]
        outer = jnp.where(upper, above, below)
        corner = jnp.where(upper, corner_above, corner_below)
        for v in range(visits):
            to = v * owners + o
            for r in range(depth):
                start = r * tiles + o * per_patch
                out[to, r * per_patch : (r + 1) * per_patch, :] = cells[start : start + per_patch, :]
            start = depth * per_patch
            out[to, start : start + lines, :] = packed[o * lines : (o + 1) * lines]
            start = start + lines
            out[to, start : start + PB, :] = outer
            start = start + PB
            out[to, start : start + 1, :] = corner


def filter_kernel(
    taps, incoming, coadd, detection, across, coadd_part, detection_part, sems, *, slices
):
    pitch = incoming.shape[0] // slices
    side = incoming.shape[1]
    depth = side // slices
    per_patch = PB * PB
    group = side // (2 * RF)
    lines = depth * PB // group
    lane = lax.broadcasted_iota(jnp.int32, (8, WRAP), 1)
    centred = jnp.zeros((8, WRAP), jnp.float32)
    leading = jnp.zeros((8, WRAP), jnp.float32)
    for b in range(2 * RF + 1):
        centred = jnp.where(lane == (RF - b) % WRAP, taps[b], centred)
        leading = jnp.where(lane == b, taps[b], leading)
    across_band = toeplitz(centred[0:1], WRAP)[:, :side]
    down_band = toeplitz(leading[0:1], side)
    across_high, across_low = halves(across_band)
    across_both = jnp.concatenate([across_high, across_low], axis=1)
    down_high, down_low = halves(down_band[:, : side + 2 * RF])
    down_both = jnp.concatenate([down_high, down_low], axis=0)

    def filtered(parts, ends, start):
        rows = ends.shape[0]
        left = lax.broadcasted_iota(jnp.int32, (rows, side), 1) < side // 2
        whole = []
        for c in range(PB):
            after = parts[c + 1] if c < PB - 1 else ends
            before = parts[c - 1] if c > 0 else ends
            beside = jnp.where(left, after, before)
            whole.append(jnp.concatenate([parts[c], beside], axis=1))
        return [(start, c, part) for c, part in enumerate(whole)]

    def product(pieces):
        high, low = halves(jnp.concatenate([part for _, _, part in pieces], axis=0))
        both = dot(high, across_both, ((1,), (0,)))
        result = both[:, :side] + both[:, side:] + dot(low, across_high, ((1,), (0,)))
        first = 0
        for start, c, part in pieces:
            cut = result[first : first + part.shape[0]]
            across[start : start + part.shape[0], c * side : (c + 1) * side] = cut
            first += part.shape[0]

    def line(index, first, rows):
        return incoming[pl.ds(first * pitch + index, rows, stride=pitch), :]

    def leave(part, whole, p, index):
        cut = pl.ds(p * side, side)
        copy = pltpu.make_async_copy(part.at[cut], whole.at[cut], sems.at[index, p])
        copy.start()
        return copy

    def down(p):
        high, low = halves(across[p * side : (p + 1) * side + 2 * RF, :])
        both = dot(down_both, high, ((1,), (0,)))
        result = both[:side] + both[side:] + dot(down_high, low, ((1,), (0,)))
        detection_part[p * side : (p + 1) * side, :] = result
        return leave(detection_part, detection, p, 1)

    copies = []
    pieces = []
    start = depth * per_patch + lines
    for first, place in ((slices - RF, 0), (0, RF + PB * side)):
        parts = [line(start + c, first, RF) for c in range(PB)]
        pieces += filtered(parts, line(start + PB, first, RF), place)
    for p in range(PB):
        parts = []
        for c in range(PB):
            tile = jnp.concatenate(
                [line(r * per_patch + p * PB + c, 0, slices) for r in range(depth)], axis=0
            )
            coadd_part[p * side : (p + 1) * side, c * side : (c + 1) * side] = tile
            parts.append(tile)
        copies.append(leave(coadd_part, coadd, p, 0))
        ends = []
        for r in range(depth):
            number = r * PB + p
            strip = line(depth * per_patch + number // group, 0, slices)
            turn = -(2 * RF * (number % group) + RF) % side
            ends.append(pltpu.roll(strip, turn, 1) if turn else strip)
        pieces += filtered(parts, jnp.concatenate(ends, axis=0), RF + p * side)
        if p % 2:
            product(pieces)
            pieces = []
            copies += [down(q) for q in range(max(p - 2, 0), p)]
    copies.append(down(PB - 1))
    for copy in copies:
        copy.wait()


def sliced_body(
    stamps, variance, coefficients, band_offsets, shifts, destination, position, psf_taps
):
    count = stamps.shape[0]
    side = variance.shape[1]
    slices = lax.axis_size(AXES)
    depth = side // slices
    visits = lax.axis_size("visit")
    prows = lax.axis_size("prow")
    pcols = lax.axis_size("pcol")
    owners = prows * pcols
    tiles = owners * PB * PB
    span = S
    batch = count
    smem = pl.BlockSpec(memory_space=pltpu.SMEM)
    vmem = pl.BlockSpec(memory_space=pltpu.VMEM)
    pitch = 2 * depth * count + 1
    lines = stamps.reshape(count, -1, side).transpose(1, 0, 2).reshape(-1, side)
    outgoing = pl.pallas_call(
        functools.partial(warp_kernel, slices=slices, span=span, batch=batch),
        in_specs=[vmem, vmem, smem, smem, smem, smem, smem, vmem, vmem],
        out_specs=vmem,
        out_shape=pltpu.VMEM((slices * pitch, side), jnp.float32),
        scratch_shapes=[
            pltpu.VMEM((batch, 2, span + 16, side), jnp.float32),
            pltpu.VMEM((2, side, 2 * side), jnp.bfloat16),
            pltpu.VMEM((2, count, side), jnp.float32),
        ],
    )(
        lines,
        variance,
        coefficients,
        band_offsets.T,
        shifts.T,
        destination,
        position,
        lagged_tables(KR, WRAP, 1),
        lagged_tables(KR, side, -1),
    )
    incoming = lax.all_to_all(
        outgoing.reshape(slices, pitch, 1, side), AXES, split_axis=0, concat_axis=0, tiled=True
    )
    group = side // (2 * RF)
    length = depth * PB * PB + depth * PB // group + PB + 1
    length = -(-length // 8) * 8
    shares = pl.pallas_call(
        functools.partial(
            tile_kernel, slices=slices, count=count, visits=visits, prows=prows, pcols=pcols
        ),
        in_specs=[vmem],
        out_specs=vmem,
        out_shape=pltpu.VMEM((slices, length, side), jnp.float32),
        scratch_shapes=[
            pltpu.VMEM((depth * tiles, side), jnp.float32),
            pltpu.VMEM((owners * depth * PB, side), jnp.float32),
        ],
    )(kept(incoming.reshape(-1, side)))
    gathered = lax.all_to_all(shares, AXES, split_axis=0, concat_axis=0, tiled=True)
    extent = PB * side
    return pl.pallas_call(
        functools.partial(filter_kernel, slices=slices),
        in_specs=[smem, vmem],
        out_specs=[pl.BlockSpec(memory_space=pl.ANY)] * 2,
        out_shape=[jax.ShapeDtypeStruct((extent, extent), jnp.float32)] * 2,
        scratch_shapes=[
            pltpu.VMEM((extent + 2 * RF, extent), jnp.float32),
            pltpu.VMEM((extent, extent), jnp.float32),
            pltpu.VMEM((extent, extent), jnp.float32),
            pltpu.SemaphoreType.DMA((2, PB)),
        ],
    )(psf_taps, kept(gathered.reshape(slices * length, side)))


def kept(values):
    return pltpu.with_memory_space_constraint(values, pltpu.VMEM)


def slices_fit(mesh, count, side):
    total = mesh.shape["visit"] * mesh.shape["prow"] * mesh.shape["pcol"]
    tiles = mesh.shape["prow"] * mesh.shape["pcol"] * PB * PB
    group = side // (2 * RF)
    if side % total or total < RF or tiles % side or WRAP != 2 * side:
        return False
    if total + 2 * KR + TAPS + 8 > WINDOW or (side // total * PB) % group:
        return False
    return total * count % side == 0 and 2 * S == 3 * side


def body(*args):
    mesh = jax.sharding.get_abstract_mesh()
    if slices_fit(mesh, *args[1].shape[:2]):
        return tuple(sliced_body(*args))
    return owner_body(*args)


def solution(mesh):
    placed = (
        P(("visit", "prow", "pcol"), None),
        P(("visit", "prow", "pcol"), None, None),
        P(("visit", "prow", "pcol"), None),
        P(("visit", "prow", "pcol"), None),
        P(("visit", "prow", "pcol"), None),
        P(("visit", "prow", "pcol")),
        P(("visit", "prow", "pcol")),
        P(),
    )
    return jax.shard_map(
        body,
        mesh=mesh,
        in_specs=placed,
        out_specs=(P("prow", "pcol"), P("prow", "pcol")),
        check_vma=False,
    )
```

```python
import functools

import jax
import jax.numpy as jnp
import numpy as np
from jax import lax
from jax.experimental import pallas as pl
from jax.experimental.pallas import tpu as pltpu
from jax.sharding import PartitionSpec as P

S = 192
KR = 15
PB = 4
RF = 8


basis_widths = (1.0, 2.0, 4.0)


def extended(cells, sides, width):
    for axis, dim in sides:
        count = lax.axis_size(axis)
        ends = count - 1
        head = lax.slice_in_dim(cells, 0, width, axis=dim)
        tail = lax.slice_in_dim(cells, cells.shape[dim] - width, cells.shape[dim], axis=dim)
        cells = jnp.concatenate(
            [
                lax.ppermute(tail, axis, [(i, (i + 1) % count) for i in range(ends)]),
                cells,
                lax.ppermute(head, axis, [((i + 1) % count, i) for i in range(ends)]),
            ],
            axis=dim,
        )
    return cells


def factor_tables(span, radius):
    matched_len = span - 2 * radius
    row_index = jnp.arange(matched_len, dtype=jnp.int32)[:, None]
    col_index = jnp.arange(span, dtype=jnp.int32)[None, :]
    lag_index = col_index - row_index - radius
    inside = (jnp.abs(lag_index) <= radius).astype(jnp.float32)
    lagged = lag_index.astype(jnp.float32)
    offsets = jnp.arange(-radius, radius + 1, dtype=jnp.int32).astype(jnp.float32)
    result = []
    for width in basis_widths:
        scaled = offsets / width
        gauss_norm = jnp.sqrt(jnp.sum(jnp.exp(-scaled * scaled)))
        quad_norm = jnp.sqrt(jnp.sum(scaled**4 * jnp.exp(-scaled * scaled)))
        ratio = lagged / width
        bell = jnp.exp(-0.5 * ratio * ratio) * inside
        result.append(jnp.stack([bell / gauss_norm, ratio * ratio * bell / quad_norm]))
    return jnp.stack(result)


def lanczos_bands(offsets, fractions, out_len, in_len):
    row_index = jnp.arange(out_len, dtype=jnp.int32)[None, :, None]
    col_index = jnp.arange(in_len, dtype=jnp.int32)[None, None, :]
    start = offsets[:, None, None]
    distance = (col_index - row_index - start).astype(jnp.float32) - fractions[:, None, None]
    return jnp.where(jnp.abs(distance) < 3.0, jnp.sinc(distance) * jnp.sinc(distance / 3.0), 0.0)


def warp_blocks(stamps, coefficients, band_offsets, shifts, tables, side):
    highest = lax.Precision.HIGHEST
    count = stamps.shape[0]
    matched_len = tables.shape[2]
    matched = jnp.zeros((count, matched_len, matched_len), jnp.float32)
    for width_index in range(len(basis_widths)):
        bell = tables[width_index, 0]
        quad = tables[width_index, 1]
        rows_bell = jnp.einsum(
            "ms,bst->bmt", bell, stamps, precision=highest, preferred_element_type=jnp.float32
        )
        rows_quad = jnp.einsum(
            "ms,bst->bmt", quad, stamps, precision=highest, preferred_element_type=jnp.float32
        )
        first = coefficients[:, 3 * width_index][:, None, None]
        second = coefficients[:, 3 * width_index + 1][:, None, None]
        third = coefficients[:, 3 * width_index + 2][:, None, None]
        left = first * rows_bell + second * rows_quad
        matched = matched + jnp.einsum(
            "bmt,nt->bmn", left, bell, precision=highest, preferred_element_type=jnp.float32
        )
        matched = matched + third * jnp.einsum(
            "bmt,nt->bmn", rows_bell, quad, precision=highest, preferred_element_type=jnp.float32
        )
    band_rows = lanczos_bands(band_offsets[:, 0], shifts[:, 0], side, matched_len)
    band_cols = lanczos_bands(band_offsets[:, 1], shifts[:, 1], side, matched_len)
    halfway = jnp.einsum(
        "bim,bmn->bin", band_rows, matched, precision=highest, preferred_element_type=jnp.float32
    )
    return jnp.einsum(
        "bin,bjn->bij", halfway, band_cols, precision=highest, preferred_element_type=jnp.float32
    )


def filter_band(taps, length, radius):
    row_index = jnp.arange(length, dtype=jnp.int32)[:, None]
    col_index = jnp.arange(length + 2 * radius, dtype=jnp.int32)[None, :]
    lag_index = col_index - row_index
    band = jnp.zeros((length, length + 2 * radius), jnp.float32)
    for tap_index in range(2 * radius + 1):
        band = band + jnp.where(lag_index == tap_index, taps[tap_index], 0.0)
    return band


def owner_body(stamps, variance, coefficients, band_offsets, shifts, destination, position, psf_taps):
    highest = lax.Precision.HIGHEST
    count = stamps.shape[0]
    span = S
    side = variance.shape[1]
    row_owners = lax.axis_size("prow")
    col_owners = lax.axis_size("pcol")
    owners = row_owners * col_owners
    capacity = max(2, 2 * count // owners)
    tables = factor_tables(span, KR)
    images = stamps.reshape(count, span, span)
    warped = warp_blocks(images, coefficients, band_offsets, shifts, tables, side)
    weight = 1.0 / variance
    terms = jnp.stack([weight * warped, weight], axis=1)
    owner_ids = jnp.arange(owners, dtype=jnp.int32)
    onehot = (destination[:, None] == owner_ids[None, :]).astype(jnp.int32)
    block_ids = jnp.arange(count, dtype=jnp.int32)
    earlier = (block_ids[None, :] < block_ids[:, None]).astype(jnp.int32)
    before = jnp.sum(earlier[:, :, None] * onehot[None, :, :], axis=1)
    rank = jnp.sum(before * onehot, axis=1)
    slot_ids = jnp.arange(capacity, dtype=jnp.int32)
    select = onehot.T[:, None, :] * (rank[None, None, :] == slot_ids[None, :, None]).astype(
        jnp.int32
    )
    send_pos = jnp.sum(select * (position[None, None, :] + 1), axis=2) - 1
    outgoing = jnp.einsum(
        "okb,bxij->okxij",
        select.astype(jnp.float32),
        terms,
        precision=highest,
        preferred_element_type=jnp.float32,
    )
    incoming, arrived = (
        lax.all_to_all(outgoing, ("prow", "pcol"), split_axis=0, concat_axis=0, tiled=True),
        lax.all_to_all(send_pos, ("prow", "pcol"), split_axis=0, concat_axis=0, tiled=True),
    )
    flattened = incoming.reshape(owners * capacity, 2 * side * side)
    tile_ids = jnp.arange(PB * PB, dtype=jnp.int32)
    placing = (arrived.reshape(owners * capacity)[None, :] == tile_ids[:, None]).astype(jnp.float32)
    tile_sums = jnp.dot(placing, flattened, precision=highest, preferred_element_type=jnp.float32)
    patch_sums = (
        tile_sums.reshape(PB, PB, 2, side, side)
        .transpose(2, 0, 3, 1, 4)
        .reshape(2, PB * side, PB * side)
    )
    shares = lax.psum_scatter(patch_sums, "visit", scatter_dimension=1, tiled=True)
    coadd = lax.all_gather(shares[0] / (1.0 + shares[1]), "visit", axis=0, tiled=True)
    padded = extended(coadd, (("prow", 0), ("pcol", 1)), RF)
    band = filter_band(psf_taps, coadd.shape[0], RF)
    across = jnp.dot(band, padded, precision=highest, preferred_element_type=jnp.float32)
    detection = jnp.dot(across, band.T, precision=highest, preferred_element_type=jnp.float32)
    return (coadd, detection)


TAPS = 6
AXES = ("prow", "pcol", "visit")
WRAP = 256
WINDOW = 80


def halves(values):
    high = values.astype(jnp.bfloat16)
    return high, (values - high.astype(jnp.float32)).astype(jnp.bfloat16)


def dot(left, right, contract):
    return lax.dot_general(left, right, (contract, ((), ())), preferred_element_type=jnp.float32)


def toeplitz(row, rows):
    spread = jnp.broadcast_to(row, (rows, row.shape[1]))
    return pltpu.roll(spread, 0, 1, stride=1, stride_axis=0)


def lagged_tables(radius, period, sign):
    lags = np.arange(-radius, radius + 1, dtype=np.float64)
    tables = np.zeros((TAPS, 8, period), np.float64)
    for index, width in enumerate(basis_widths):
        ratio = lags / width
        bell = np.exp(-0.5 * ratio * ratio)
        quad = ratio * ratio * bell
        for kind, factor in enumerate((bell, quad)):
            normed = factor / np.sqrt(np.sum(factor * factor))
            for n in range(TAPS):
                places = sign * (np.arange(2 * radius + 1) + n - 2)
                tables[n, 2 * index + kind, places % period] = normed
    return jnp.asarray(tables.astype(np.float32))


def lanczos(distance):
    def sinc(x):
        angle = jnp.float32(np.pi) * x
        return jnp.where(x == 0.0, 1.0, jnp.sin(angle) / jnp.where(x == 0.0, 1.0, angle))

    return jnp.where(jnp.abs(distance) < 3.0, sinc(distance) * sinc(distance / 3.0), 0.0)


def warp_kernel(
    stamps,
    variance,
    coefs,
    offsets,
    shifts,
    dest,
    pos,
    row_tables,
    col_tables,
    out,
    image,
    masks,
    taps,
    *,
    slices,
    span,
    batch,
):
    count, side = variance.shape[:2]
    depth = side // slices
    pitch = 2 * depth * count + 1
    widths = len(basis_widths)
    rows_even = span // 2
    rest = span - side
    step = 3 * count
    image[...] = jnp.zeros(image.shape, image.dtype)
    row = lax.broadcasted_iota(jnp.int32, (side, side), 0)
    col = lax.broadcasted_iota(jnp.int32, (side, side), 1)
    for index, test in enumerate((col <= row, col > row)):
        mask = jnp.where(test, 1.0, 0.0).astype(jnp.bfloat16)
        masks[index] = jnp.concatenate([mask, mask], axis=1)
    lane = lax.broadcasted_iota(jnp.int32, (count, side), 1)
    level = lax.broadcasted_iota(jnp.int32, (count, side), 0)
    for axis in range(2):
        part = jnp.zeros((count, side), jnp.float32)
        for k in range(count):
            part = jnp.where(level == k, shifts[axis, k], part)
        taps[axis] = lanczos((lane - 2).astype(jnp.float32) - part)
    lane = lax.broadcasted_iota(jnp.int32, (slices, side), 1)
    names = jnp.zeros((slices, side), jnp.float32)
    for k in range(count):
        tile = (dest[k] * (PB * PB) + pos[k]).astype(jnp.float32)
        names = jnp.where(lane == k, tile, names)
    out[pl.ds(pitch - 1, slices, stride=pitch), :] = names
    early = lax.broadcasted_iota(jnp.int32, (rows_even, side), 1) < rest

    def mixed(axis, k, tables):
        values = taps[axis, pl.ds(k, 1), :]
        total = jnp.zeros(tables.shape[1:], jnp.float32)
        for n in range(TAPS):
            total = total + values[:, n : n + 1] * tables[n]
        return total

    def one_block(k, b):
        first = stamps[pl.ds(k, rows_even, stride=step), :]
        second = stamps[pl.ds(count + k, rows_even, stride=step), :]
        third = stamps[pl.ds(2 * count + k, rows_even, stride=step), :]
        second_turned = pltpu.roll(second, rest, 1)
        third_turned = pltpu.roll(third, rest, 1)
        image[b, 0, pl.ds(0, rows_even, stride=2), :] = first
        image[b, 1, pl.ds(0, rows_even, stride=2), :] = second
        image[b, 0, pl.ds(1, rows_even, stride=2), :] = jnp.where(
            early, second_turned, third_turned
        )
        image[b, 1, pl.ds(1, rows_even, stride=2), :] = third_turned
        offset = offsets[0, k]
        base = lax.div(offset - 2, 8) * 8
        row_taps = pltpu.roll(mixed(0, k, row_tables), offset - base, 1)
        high = row_taps.astype(jnp.bfloat16).astype(jnp.float32)
        low = (row_taps - high).astype(jnp.bfloat16).astype(jnp.float32)
        lined = high + pltpu.roll(high, WINDOW, 1) + pltpu.roll(low, 2 * WINDOW, 1)
        left = jnp.concatenate(
            [toeplitz(lined[q : q + 1], slices) for q in range(2 * widths)], axis=0
        ).astype(jnp.bfloat16)
        across = []
        for w in range(depth):
            start = pl.multiple_of(w * slices + base, 8)
            window = jnp.concatenate(
                [image[b, half, pl.ds(start, WINDOW), :] for half in range(2)], axis=1
            )
            high, low = halves(window)
            none = jnp.zeros((WRAP - 3 * WINDOW, 2 * side), jnp.bfloat16)
            right = jnp.concatenate([high, low, high, none], axis=0)
            across.append(dot(left, right, ((1,), (0,)))[:, :span])
        offset = offsets[1, k]
        col_taps = pltpu.roll(mixed(1, k, col_tables), side - offset, 1)
        total = jnp.zeros((2 * side, 2 * side), jnp.float32)
        for m in range(widths):
            bell = col_taps[2 * m : 2 * m + 1]
            quad = col_taps[2 * m + 1 : 2 * m + 2]
            pair = (
                coefs[k, 3 * m] * bell + coefs[k, 3 * m + 2] * quad,
                coefs[k, 3 * m + 1] * bell,
            )
            for kind in range(2):
                q = 2 * m + kind
                high, low = halves(toeplitz(pair[kind], side))
                both = jnp.concatenate([high, low], axis=1)
                right = jnp.concatenate([both * masks[0], both[:rest] * masks[1, :rest]], axis=0)
                cut = slice(q * slices, (q + 1) * slices)
                high, low = halves(jnp.concatenate([part[cut] for part in across], axis=0))
                total = total + dot(jnp.concatenate([high, low], axis=0), right, ((1,), (0,)))
        warped = total[:side, :side] + (total[:side, side:] + total[side:, :side])
        weight = 1.0 / variance[k]
        weighted = weight * warped
        for r in range(depth):
            cut = slice(r * slices, (r + 1) * slices)
            out[pl.ds(r * count + k, slices, stride=pitch), :] = weighted[cut]
            out[pl.ds((depth + r) * count + k, slices, stride=pitch), :] = weight[cut]

    for k in range(count):
        one_block(k, k)


def tile_kernel(incoming, out, cells, strips, *, slices, count, visits, prows, pcols):
    pitch = incoming.shape[0] // slices
    side = incoming.shape[1]
    depth = side // slices
    owners = prows * pcols
    per_patch = PB * PB
    tiles = owners * per_patch
    blocks = slices * count
    names = incoming[pl.ds(pitch - 1, slices, stride=pitch), :]
    names = pltpu.roll(names, 0, 1, stride=count, stride_axis=0)
    per_row = side // count
    named = jnp.concatenate(
        [
            jnp.sum(names[first : first + per_row], axis=0, keepdims=True)
            for first in range(0, slices, per_row)
        ],
        axis=1,
    )
    places = lax.broadcasted_iota(jnp.int32, (tiles, blocks), 0).astype(jnp.float32)
    chosen = jnp.where(named == places, 1.0, 0.0).astype(jnp.bfloat16)

    def summed(index):
        starts = [j * pitch + index * count for j in range(slices)]
        data = jnp.concatenate([incoming[start : start + count, :] for start in starts], axis=0)
        high, low = halves(data)
        both = dot(chosen, jnp.concatenate([high, low], axis=1), ((1,), (0,)))
        return both[:, :side] + both[:, side:]

    for r in range(depth):
        cells[r * tiles : (r + 1) * tiles, :] = summed(r) / (1.0 + summed(depth + r))
    lane = lax.broadcasted_iota(jnp.int32, (PB, side), 1)
    for o in range(owners):
        for r in range(depth):
            strip = jnp.zeros((PB, side), jnp.float32)
            if o % pcols < pcols - 1:
                after = cells[pl.ds(r * tiles + (o + 1) * per_patch, PB, stride=PB), :]
                strip = jnp.where(lane < RF, after, strip)
            if o % pcols > 0:
                before = cells[pl.ds(r * tiles + (o - 1) * per_patch + PB - 1, PB, stride=PB), :]
                strip = jnp.where(lane >= side - RF, before, strip)
            strips[(o * depth + r) * PB : (o * depth + r + 1) * PB, :] = strip
    group = side // (2 * RF)
    packed = pltpu.roll(strips[...], RF, 1, stride=2 * RF, stride_axis=0)
    packed = jnp.sum(packed.reshape(owners * depth * PB // group, group, side), axis=1)
    lines = depth * PB // group
    upper = lax.axis_index(AXES) >= RF
    for o in range(owners):
        below = jnp.zeros((PB, side), jnp.float32)
        above = jnp.zeros((PB, side), jnp.float32)
        corner_below = jnp.zeros((1, side), jnp.float32)
        corner_above = jnp.zeros((1, side), jnp.float32)
        if o + pcols < owners:
            start = (o + pcols) * per_patch
            below = cells[start : start + PB, :]
            start = (o + pcols) * depth * PB
            corner_below = strips[start : start + 1, :]
        if o >= pcols:
            start = (depth - 1) * tiles + (o - pcols) * per_patch + per_patch - PB
            above = cells[start : start + PB, :]
            start = (o - pcols + 1) * depth * PB - 1
            corner_above = strips[start : start + 1, :]
        outer = jnp.where(upper, above, below)
        corner = jnp.where(upper, corner_above, corner_below)
        for v in range(visits):
            to = o * visits + v
            for r in range(depth):
                start = r * tiles + o * per_patch
                out[to, r * per_patch : (r + 1) * per_patch, :] = cells[start : start + per_patch, :]
            start = depth * per_patch
            out[to, start : start + lines, :] = packed[o * lines : (o + 1) * lines]
            start = start + lines
            out[to, start : start + PB, :] = outer
            start = start + PB
            out[to, start : start + 1, :] = corner


def filter_kernel(
    taps, incoming, coadd, detection, across, coadd_part, detection_part, sems, *, slices
):
    pitch = incoming.shape[0] // slices
    side = incoming.shape[1]
    depth = side // slices
    per_patch = PB * PB
    group = side // (2 * RF)
    lines = depth * PB // group
    lane = lax.broadcasted_iota(jnp.int32, (8, WRAP), 1)
    centred = jnp.zeros((8, WRAP), jnp.float32)
    leading = jnp.zeros((8, WRAP), jnp.float32)
    for b in range(2 * RF + 1):
        centred = jnp.where(lane == (RF - b) % WRAP, taps[b], centred)
        leading = jnp.where(lane == b, taps[b], leading)
    across_band = toeplitz(centred[0:1], WRAP)[:, :side]
    down_band = toeplitz(leading[0:1], side)
    across_high, across_low = halves(across_band)
    across_both = jnp.concatenate([across_high, across_low], axis=1)
    down_high, down_low = halves(down_band[:, : side + 2 * RF])
    down_both = jnp.concatenate([down_high, down_low], axis=0)

    def filtered(parts, ends, start):
        rows = ends.shape[0]
        left = lax.broadcasted_iota(jnp.int32, (rows, side), 1) < side // 2
        whole = []
        for c in range(PB):
            after = parts[c + 1] if c < PB - 1 else ends
            before = parts[c - 1] if c > 0 else ends
            beside = jnp.where(left, after, before)
            whole.append(jnp.concatenate([parts[c], beside], axis=1))
        return [(start, c, part) for c, part in enumerate(whole)]

    def product(pieces):
        high, low = halves(jnp.concatenate([part for _, _, part in pieces], axis=0))
        both = dot(high, across_both, ((1,), (0,)))
        result = both[:, :side] + both[:, side:] + dot(low, across_high, ((1,), (0,)))
        first = 0
        for start, c, part in pieces:
            cut = result[first : first + part.shape[0]]
            across[start : start + part.shape[0], c * side : (c + 1) * side] = cut
            first += part.shape[0]

    def line(index, first, rows):
        return incoming[pl.ds(first * pitch + index, rows, stride=pitch), :]

    def leave(part, whole, p, index):
        cut = pl.ds(p * side, side)
        copy = pltpu.make_async_copy(part.at[cut], whole.at[cut], sems.at[index, p])
        copy.start()
        return copy

    def down(p):
        high, low = halves(across[p * side : (p + 1) * side + 2 * RF, :])
        both = dot(down_both, high, ((1,), (0,)))
        result = both[:side] + both[side:] + dot(down_high, low, ((1,), (0,)))
        detection_part[p * side : (p + 1) * side, :] = result
        return leave(detection_part, detection, p, 1)

    copies = []
    pieces = []
    start = depth * per_patch + lines
    for first, place in ((slices - RF, 0), (0, RF + PB * side)):
        parts = [line(start + c, first, RF) for c in range(PB)]
        pieces += filtered(parts, line(start + PB, first, RF), place)
    for p in range(PB):
        parts = []
        for c in range(PB):
            tile = jnp.concatenate(
                [line(r * per_patch + p * PB + c, 0, slices) for r in range(depth)], axis=0
            )
            coadd_part[p * side : (p + 1) * side, c * side : (c + 1) * side] = tile
            parts.append(tile)
        copies.append(leave(coadd_part, coadd, p, 0))
        ends = []
        for r in range(depth):
            number = r * PB + p
            strip = line(depth * per_patch + number // group, 0, slices)
            turn = -(2 * RF * (number % group) + RF) % side
            ends.append(pltpu.roll(strip, turn, 1) if turn else strip)
        pieces += filtered(parts, jnp.concatenate(ends, axis=0), RF + p * side)
        if p % 2:
            product(pieces)
            pieces = []
            copies += [down(q) for q in range(max(p - 2, 0), p)]
    copies.append(down(PB - 1))
    for copy in copies:
        copy.wait()


def sliced_body(
    stamps, variance, coefficients, band_offsets, shifts, destination, position, psf_taps
):
    count = stamps.shape[0]
    side = variance.shape[1]
    slices = lax.axis_size(AXES)
    depth = side // slices
    visits = lax.axis_size("visit")
    prows = lax.axis_size("prow")
    pcols = lax.axis_size("pcol")
    owners = prows * pcols
    tiles = owners * PB * PB
    span = S
    batch = count
    smem = pl.BlockSpec(memory_space=pltpu.SMEM)
    vmem = pl.BlockSpec(memory_space=pltpu.VMEM)
    pitch = 2 * depth * count + 1
    lines = stamps.reshape(count, -1, side).transpose(1, 0, 2).reshape(-1, side)
    outgoing = pl.pallas_call(
        functools.partial(warp_kernel, slices=slices, span=span, batch=batch),
        in_specs=[vmem, vmem, smem, smem, smem, smem, smem, vmem, vmem],
        out_specs=vmem,
        out_shape=pltpu.VMEM((slices * pitch, side), jnp.float32),
        scratch_shapes=[
            pltpu.VMEM((batch, 2, span + 16, side), jnp.float32),
            pltpu.VMEM((2, side, 2 * side), jnp.bfloat16),
            pltpu.VMEM((2, count, side), jnp.float32),
        ],
    )(
        lines,
        variance,
        coefficients,
        band_offsets.T,
        shifts.T,
        destination,
        position,
        lagged_tables(KR, WRAP, 1),
        lagged_tables(KR, side, -1),
    )
    incoming = lax.all_to_all(
        outgoing.reshape(slices, pitch, 1, side), AXES, split_axis=0, concat_axis=0, tiled=True
    )
    group = side // (2 * RF)
    length = depth * PB * PB + depth * PB // group + PB + 1
    length = -(-length // 8) * 8
    shares = pl.pallas_call(
        functools.partial(
            tile_kernel, slices=slices, count=count, visits=visits, prows=prows, pcols=pcols
        ),
        in_specs=[vmem],
        out_specs=vmem,
        out_shape=pltpu.VMEM((slices, length, side), jnp.float32),
        scratch_shapes=[
            pltpu.VMEM((depth * tiles, side), jnp.float32),
            pltpu.VMEM((owners * depth * PB, side), jnp.float32),
        ],
    )(kept(incoming.reshape(-1, side)))
    gathered = lax.all_to_all(shares, AXES, split_axis=0, concat_axis=0, tiled=True)
    extent = PB * side
    return pl.pallas_call(
        functools.partial(filter_kernel, slices=slices),
        in_specs=[smem, vmem],
        out_specs=[pl.BlockSpec(memory_space=pl.ANY)] * 2,
        out_shape=[jax.ShapeDtypeStruct((extent, extent), jnp.float32)] * 2,
        scratch_shapes=[
            pltpu.VMEM((extent + 2 * RF, extent), jnp.float32),
            pltpu.VMEM((extent, extent), jnp.float32),
            pltpu.VMEM((extent, extent), jnp.float32),
            pltpu.SemaphoreType.DMA((2, PB)),
        ],
    )(psf_taps, kept(gathered.reshape(slices * length, side)))


def kept(values):
    return pltpu.with_memory_space_constraint(values, pltpu.VMEM)


def slices_fit(mesh, count, side):
    total = mesh.shape["visit"] * mesh.shape["prow"] * mesh.shape["pcol"]
    tiles = mesh.shape["prow"] * mesh.shape["pcol"] * PB * PB
    group = side // (2 * RF)
    if side % total or total < RF or tiles % side or WRAP != 2 * side:
        return False
    if total + 2 * KR + TAPS + 8 > WINDOW or (side // total * PB) % group:
        return False
    return total * count % side == 0 and 2 * S == 3 * side


def body(*args):
    mesh = jax.sharding.get_abstract_mesh()
    if slices_fit(mesh, *args[1].shape[:2]):
        return tuple(sliced_body(*args))
    return owner_body(*args)


def solution(mesh):
    placed = (
        P(("visit", "prow", "pcol"), None),
        P(("visit", "prow", "pcol"), None, None),
        P(("visit", "prow", "pcol"), None),
        P(("visit", "prow", "pcol"), None),
        P(("visit", "prow", "pcol"), None),
        P(("visit", "prow", "pcol")),
        P(("visit", "prow", "pcol")),
        P(),
    )
    return jax.shard_map(
        body,
        mesh=mesh,
        in_specs=placed,
        out_specs=(P("prow", "pcol"), P("prow", "pcol")),
        check_vma=False,
    )
```

```python
import functools

import jax
import jax.numpy as jnp
import numpy as np
from jax import lax
from jax.experimental import pallas as pl
from jax.experimental.pallas import tpu as pltpu
from jax.sharding import PartitionSpec as P

S = 192
KR = 15
PB = 4
RF = 8


basis_widths = (1.0, 2.0, 4.0)


def extended(cells, sides, width):
    for axis, dim in sides:
        count = lax.axis_size(axis)
        ends = count - 1
        head = lax.slice_in_dim(cells, 0, width, axis=dim)
        tail = lax.slice_in_dim(cells, cells.shape[dim] - width, cells.shape[dim], axis=dim)
        cells = jnp.concatenate(
            [
                lax.ppermute(tail, axis, [(i, (i + 1) % count) for i in range(ends)]),
                cells,
                lax.ppermute(head, axis, [((i + 1) % count, i) for i in range(ends)]),
            ],
            axis=dim,
        )
    return cells


def factor_tables(span, radius):
    matched_len = span - 2 * radius
    row_index = jnp.arange(matched_len, dtype=jnp.int32)[:, None]
    col_index = jnp.arange(span, dtype=jnp.int32)[None, :]
    lag_index = col_index - row_index - radius
    inside = (jnp.abs(lag_index) <= radius).astype(jnp.float32)
    lagged = lag_index.astype(jnp.float32)
    offsets = jnp.arange(-radius, radius + 1, dtype=jnp.int32).astype(jnp.float32)
    result = []
    for width in basis_widths:
        scaled = offsets / width
        gauss_norm = jnp.sqrt(jnp.sum(jnp.exp(-scaled * scaled)))
        quad_norm = jnp.sqrt(jnp.sum(scaled**4 * jnp.exp(-scaled * scaled)))
        ratio = lagged / width
        bell = jnp.exp(-0.5 * ratio * ratio) * inside
        result.append(jnp.stack([bell / gauss_norm, ratio * ratio * bell / quad_norm]))
    return jnp.stack(result)


def lanczos_bands(offsets, fractions, out_len, in_len):
    row_index = jnp.arange(out_len, dtype=jnp.int32)[None, :, None]
    col_index = jnp.arange(in_len, dtype=jnp.int32)[None, None, :]
    start = offsets[:, None, None]
    distance = (col_index - row_index - start).astype(jnp.float32) - fractions[:, None, None]
    return jnp.where(jnp.abs(distance) < 3.0, jnp.sinc(distance) * jnp.sinc(distance / 3.0), 0.0)


def warp_blocks(stamps, coefficients, band_offsets, shifts, tables, side):
    highest = lax.Precision.HIGHEST
    count = stamps.shape[0]
    matched_len = tables.shape[2]
    matched = jnp.zeros((count, matched_len, matched_len), jnp.float32)
    for width_index in range(len(basis_widths)):
        bell = tables[width_index, 0]
        quad = tables[width_index, 1]
        rows_bell = jnp.einsum(
            "ms,bst->bmt", bell, stamps, precision=highest, preferred_element_type=jnp.float32
        )
        rows_quad = jnp.einsum(
            "ms,bst->bmt", quad, stamps, precision=highest, preferred_element_type=jnp.float32
        )
        first = coefficients[:, 3 * width_index][:, None, None]
        second = coefficients[:, 3 * width_index + 1][:, None, None]
        third = coefficients[:, 3 * width_index + 2][:, None, None]
        left = first * rows_bell + second * rows_quad
        matched = matched + jnp.einsum(
            "bmt,nt->bmn", left, bell, precision=highest, preferred_element_type=jnp.float32
        )
        matched = matched + third * jnp.einsum(
            "bmt,nt->bmn", rows_bell, quad, precision=highest, preferred_element_type=jnp.float32
        )
    band_rows = lanczos_bands(band_offsets[:, 0], shifts[:, 0], side, matched_len)
    band_cols = lanczos_bands(band_offsets[:, 1], shifts[:, 1], side, matched_len)
    halfway = jnp.einsum(
        "bim,bmn->bin", band_rows, matched, precision=highest, preferred_element_type=jnp.float32
    )
    return jnp.einsum(
        "bin,bjn->bij", halfway, band_cols, precision=highest, preferred_element_type=jnp.float32
    )


def filter_band(taps, length, radius):
    row_index = jnp.arange(length, dtype=jnp.int32)[:, None]
    col_index = jnp.arange(length + 2 * radius, dtype=jnp.int32)[None, :]
    lag_index = col_index - row_index
    band = jnp.zeros((length, length + 2 * radius), jnp.float32)
    for tap_index in range(2 * radius + 1):
        band = band + jnp.where(lag_index == tap_index, taps[tap_index], 0.0)
    return band


def owner_body(stamps, variance, coefficients, band_offsets, shifts, destination, position, psf_taps):
    highest = lax.Precision.HIGHEST
    count = stamps.shape[0]
    span = S
    side = variance.shape[1]
    row_owners = lax.axis_size("prow")
    col_owners = lax.axis_size("pcol")
    owners = row_owners * col_owners
    capacity = max(2, 2 * count // owners)
    tables = factor_tables(span, KR)
    images = stamps.reshape(count, span, span)
    warped = warp_blocks(images, coefficients, band_offsets, shifts, tables, side)
    weight = 1.0 / variance
    terms = jnp.stack([weight * warped, weight], axis=1)
    owner_ids = jnp.arange(owners, dtype=jnp.int32)
    onehot = (destination[:, None] == owner_ids[None, :]).astype(jnp.int32)
    block_ids = jnp.arange(count, dtype=jnp.int32)
    earlier = (block_ids[None, :] < block_ids[:, None]).astype(jnp.int32)
    before = jnp.sum(earlier[:, :, None] * onehot[None, :, :], axis=1)
    rank = jnp.sum(before * onehot, axis=1)
    slot_ids = jnp.arange(capacity, dtype=jnp.int32)
    select = onehot.T[:, None, :] * (rank[None, None, :] == slot_ids[None, :, None]).astype(
        jnp.int32
    )
    send_pos = jnp.sum(select * (position[None, None, :] + 1), axis=2) - 1
    outgoing = jnp.einsum(
        "okb,bxij->okxij",
        select.astype(jnp.float32),
        terms,
        precision=highest,
        preferred_element_type=jnp.float32,
    )
    incoming, arrived = (
        lax.all_to_all(outgoing, ("prow", "pcol"), split_axis=0, concat_axis=0, tiled=True),
        lax.all_to_all(send_pos, ("prow", "pcol"), split_axis=0, concat_axis=0, tiled=True),
    )
    flattened = incoming.reshape(owners * capacity, 2 * side * side)
    tile_ids = jnp.arange(PB * PB, dtype=jnp.int32)
    placing = (arrived.reshape(owners * capacity)[None, :] == tile_ids[:, None]).astype(jnp.float32)
    tile_sums = jnp.dot(placing, flattened, precision=highest, preferred_element_type=jnp.float32)
    patch_sums = (
        tile_sums.reshape(PB, PB, 2, side, side)
        .transpose(2, 0, 3, 1, 4)
        .reshape(2, PB * side, PB * side)
    )
    shares = lax.psum_scatter(patch_sums, "visit", scatter_dimension=1, tiled=True)
    coadd = lax.all_gather(shares[0] / (1.0 + shares[1]), "visit", axis=0, tiled=True)
    padded = extended(coadd, (("prow", 0), ("pcol", 1)), RF)
    band = filter_band(psf_taps, coadd.shape[0], RF)
    across = jnp.dot(band, padded, precision=highest, preferred_element_type=jnp.float32)
    detection = jnp.dot(across, band.T, precision=highest, preferred_element_type=jnp.float32)
    return (coadd, detection)


TAPS = 6
AXES = ("prow", "pcol", "visit")
WRAP = 256
WINDOW = 80


def halves(values):
    high = values.astype(jnp.bfloat16)
    return high, (values - high.astype(jnp.float32)).astype(jnp.bfloat16)


def dot(left, right, contract):
    return lax.dot_general(left, right, (contract, ((), ())), preferred_element_type=jnp.float32)


def toeplitz(row, rows):
    spread = jnp.broadcast_to(row, (rows, row.shape[1]))
    return pltpu.roll(spread, 0, 1, stride=1, stride_axis=0)


def lagged_tables(radius, period, sign):
    lags = np.arange(-radius, radius + 1, dtype=np.float64)
    tables = np.zeros((TAPS, 8, period), np.float64)
    for index, width in enumerate(basis_widths):
        ratio = lags / width
        bell = np.exp(-0.5 * ratio * ratio)
        quad = ratio * ratio * bell
        for kind, factor in enumerate((bell, quad)):
            normed = factor / np.sqrt(np.sum(factor * factor))
            for n in range(TAPS):
                places = sign * (np.arange(2 * radius + 1) + n - 2)
                tables[n, 2 * index + kind, places % period] = normed
    return jnp.asarray(tables.astype(np.float32))


def lanczos(distance):
    def sinc(x):
        angle = jnp.float32(np.pi) * x
        return jnp.where(x == 0.0, 1.0, jnp.sin(angle) / jnp.where(x == 0.0, 1.0, angle))

    return jnp.where(jnp.abs(distance) < 3.0, sinc(distance) * sinc(distance / 3.0), 0.0)


def warp_kernel(
    stamps,
    variance,
    coefs,
    offsets,
    shifts,
    dest,
    pos,
    row_tables,
    col_tables,
    out,
    image,
    masks,
    taps,
    *,
    slices,
    span,
    batch,
):
    count, side = variance.shape[:2]
    depth = side // slices
    pitch = 2 * depth * count + 1
    widths = len(basis_widths)
    rows_even = span // 2
    rest = span - side
    step = 3 * count
    image[...] = jnp.zeros(image.shape, image.dtype)
    row = lax.broadcasted_iota(jnp.int32, (side, side), 0)
    col = lax.broadcasted_iota(jnp.int32, (side, side), 1)
    for index, test in enumerate((col <= row, col > row)):
        mask = jnp.where(test, 1.0, 0.0).astype(jnp.bfloat16)
        masks[index] = jnp.concatenate([mask, mask], axis=1)
    lane = lax.broadcasted_iota(jnp.int32, (count, side), 1)
    level = lax.broadcasted_iota(jnp.int32, (count, side), 0)
    for axis in range(2):
        part = jnp.zeros((count, side), jnp.float32)
        for k in range(count):
            part = jnp.where(level == k, shifts[axis, k], part)
        taps[axis] = lanczos((lane - 2).astype(jnp.float32) - part)
    lane = lax.broadcasted_iota(jnp.int32, (slices, side), 1)
    names = jnp.zeros((slices, side), jnp.float32)
    for k in range(count):
        tile = (dest[k] * (PB * PB) + pos[k]).astype(jnp.float32)
        names = jnp.where(lane == k, tile, names)
    out[pl.ds(pitch - 1, slices, stride=pitch), :] = names
    early = lax.broadcasted_iota(jnp.int32, (rows_even, side), 1) < rest

    def mixed(axis, k, tables):
        values = taps[axis, pl.ds(k, 1), :]
        total = jnp.zeros(tables.shape[1:], jnp.float32)
        for n in range(TAPS):
            total = total + values[:, n : n + 1] * tables[n]
        return total

    def one_block(k, b):
        first = stamps[pl.ds(k, rows_even, stride=step), :]
        second = stamps[pl.ds(count + k, rows_even, stride=step), :]
        third = stamps[pl.ds(2 * count + k, rows_even, stride=step), :]
        second_turned = pltpu.roll(second, rest, 1)
        third_turned = pltpu.roll(third, rest, 1)
        image[b, 0, pl.ds(0, rows_even, stride=2), :] = first
        image[b, 1, pl.ds(0, rows_even, stride=2), :] = second
        image[b, 0, pl.ds(1, rows_even, stride=2), :] = jnp.where(
            early, second_turned, third_turned
        )
        image[b, 1, pl.ds(1, rows_even, stride=2), :] = third_turned
        offset = offsets[0, k]
        base = lax.div(offset - 2, 8) * 8
        row_taps = pltpu.roll(mixed(0, k, row_tables), offset - base, 1)
        high = row_taps.astype(jnp.bfloat16).astype(jnp.float32)
        low = (row_taps - high).astype(jnp.bfloat16).astype(jnp.float32)
        lined = high + pltpu.roll(high, WINDOW, 1) + pltpu.roll(low, 2 * WINDOW, 1)
        left = jnp.concatenate(
            [toeplitz(lined[q : q + 1], slices) for q in range(2 * widths)], axis=0
        ).astype(jnp.bfloat16)
        across = []
        for w in range(depth):
            start = pl.multiple_of(w * slices + base, 8)
            window = jnp.concatenate(
                [image[b, half, pl.ds(start, WINDOW), :] for half in range(2)], axis=1
            )
            high, low = halves(window)
            none = jnp.zeros((WRAP - 3 * WINDOW, 2 * side), jnp.bfloat16)
            right = jnp.concatenate([high, low, high, none], axis=0)
            across.append(dot(left, right, ((1,), (0,)))[:, :span])
        offset = offsets[1, k]
        col_taps = pltpu.roll(mixed(1, k, col_tables), side - offset, 1)
        total = jnp.zeros((2 * side, 2 * side), jnp.float32)
        for m in range(widths):
            bell = col_taps[2 * m : 2 * m + 1]
            quad = col_taps[2 * m + 1 : 2 * m + 2]
            pair = (
                coefs[k, 3 * m] * bell + coefs[k, 3 * m + 2] * quad,
                coefs[k, 3 * m + 1] * bell,
            )
            for kind in range(2):
                q = 2 * m + kind
                high, low = halves(toeplitz(pair[kind], side))
                both = jnp.concatenate([high, low], axis=1)
                right = jnp.concatenate([both * masks[0], both[:rest] * masks[1, :rest]], axis=0)
                cut = slice(q * slices, (q + 1) * slices)
                high, low = halves(jnp.concatenate([part[cut] for part in across], axis=0))
                total = total + dot(jnp.concatenate([high, low], axis=0), right, ((1,), (0,)))
        warped = total[:side, :side] + (total[:side, side:] + total[side:, :side])
        weight = 1.0 / variance[k]
        weighted = weight * warped
        column = lax.rem(pos[k], PB)
        for m in range(slices // RF):
            first = lax.rem(m + PB - column, PB) * (RF * pitch) + k
            for r in range(depth):
                cut = slice(r * slices + m * RF, r * slices + (m + 1) * RF)
                out[pl.ds(first + r * count, RF, stride=pitch), :] = weighted[cut]
                out[pl.ds(first + (depth + r) * count, RF, stride=pitch), :] = weight[cut]

    for k in range(count):
        one_block(k, k)


def tile_kernel(incoming, out, cells, strips, *, slices, count, visits, prows, pcols):
    pitch = incoming.shape[0] // slices
    side = incoming.shape[1]
    depth = side // slices
    owners = prows * pcols
    per_patch = PB * PB
    tiles = owners * per_patch
    blocks = slices * count
    names = incoming[pl.ds(pitch - 1, slices, stride=pitch), :]
    names = pltpu.roll(names, 0, 1, stride=count, stride_axis=0)
    per_row = side // count
    named = jnp.concatenate(
        [
            jnp.sum(names[first : first + per_row], axis=0, keepdims=True)
            for first in range(0, slices, per_row)
        ],
        axis=1,
    )
    places = lax.broadcasted_iota(jnp.int32, (tiles, blocks), 0).astype(jnp.float32)
    chosen = jnp.where(named == places, 1.0, 0.0).astype(jnp.bfloat16)

    def summed(index):
        starts = [j * pitch + index * count for j in range(slices)]
        data = jnp.concatenate([incoming[start : start + count, :] for start in starts], axis=0)
        high, low = halves(data)
        both = dot(chosen, jnp.concatenate([high, low], axis=1), ((1,), (0,)))
        return both[:, :side] + both[:, side:]

    for r in range(depth):
        cells[r * tiles : (r + 1) * tiles, :] = summed(r) / (1.0 + summed(depth + r))
    lane = lax.broadcasted_iota(jnp.int32, (PB, side), 1)
    for o in range(owners):
        for r in range(depth):
            strip = jnp.zeros((PB, side), jnp.float32)
            if o % pcols < pcols - 1:
                after = cells[pl.ds(r * tiles + (o + 1) * per_patch, PB, stride=PB), :]
                strip = jnp.where(lane < RF, after, strip)
            if o % pcols > 0:
                before = cells[pl.ds(r * tiles + (o - 1) * per_patch + PB - 1, PB, stride=PB), :]
                strip = jnp.where(lane >= side - RF, before, strip)
            strips[(o * depth + r) * PB : (o * depth + r + 1) * PB, :] = strip
    group = side // (2 * RF)
    packed = pltpu.roll(strips[...], RF, 1, stride=2 * RF, stride_axis=0)
    packed = jnp.sum(packed.reshape(owners * depth * PB // group, group, side), axis=1)
    lines = depth * PB // group
    turn = lax.div(lax.axis_index(AXES), RF)
    for o in range(owners):
        below = jnp.zeros((1, side), jnp.float32)
        above = jnp.zeros((1, side), jnp.float32)
        corner = jnp.zeros((1, side), jnp.float32)
        if o + pcols < owners:
            start = (o + pcols) * per_patch
            below = cells[pl.ds(start + lax.rem(PB - turn, PB), 1), :]
            start = (o + pcols) * depth * PB
            corner = strips[start : start + 1, :]
        if o >= pcols:
            start = (depth - 1) * tiles + (o - pcols + 1) * per_patch - 1
            above = cells[pl.ds(start - turn, 1), :]
            start = (o - pcols + 1) * depth * PB - 1
            corner = corner + pltpu.roll(strips[start : start + 1, :], 2 * RF, 1)
        for v in range(visits):
            to = (o * visits + v) * (out.shape[0] // slices)
            for r in range(depth):
                start = r * tiles + o * per_patch
                out[to + r * per_patch : to + (r + 1) * per_patch, :] = cells[start : start + per_patch, :]
            start = to + depth * per_patch
            out[start : start + lines, :] = packed[o * lines : (o + 1) * lines]
            start = start + lines
            out[start : start + 1, :] = below
            out[start + 1 : start + 2, :] = above
            out[start + 2 : start + 3, :] = corner


def filter_kernel(
    taps, incoming, coadd, detection, across, coadd_part, detection_part, sems, *, slices
):
    pitch = incoming.shape[0] // slices
    side = incoming.shape[1]
    depth = side // slices
    per_patch = PB * PB
    group = side // (2 * RF)
    lines = depth * PB // group
    lane = lax.broadcasted_iota(jnp.int32, (8, WRAP), 1)
    centred = jnp.zeros((8, WRAP), jnp.float32)
    leading = jnp.zeros((8, WRAP), jnp.float32)
    for b in range(2 * RF + 1):
        centred = jnp.where(lane == (RF - b) % WRAP, taps[b], centred)
        leading = jnp.where(lane == b, taps[b], leading)
    across_band = toeplitz(centred[0:1], WRAP)[:, :side]
    down_band = toeplitz(leading[0:1], side)
    across_high, across_low = halves(across_band)
    across_both = jnp.concatenate([across_high, across_low], axis=1)
    down_high, down_low = halves(down_band[:, : side + 2 * RF])
    down_both = jnp.concatenate([down_high, down_low], axis=0)

    def filtered(parts, ends, start):
        rows = ends.shape[0]
        left = lax.broadcasted_iota(jnp.int32, (rows, side), 1) < side // 2
        whole = []
        for c in range(PB):
            after = parts[c + 1] if c < PB - 1 else ends
            before = parts[c - 1] if c > 0 else ends
            beside = jnp.where(left, after, before)
            whole.append(jnp.concatenate([parts[c], beside], axis=1))
        return [(start, c, part) for c, part in enumerate(whole)]

    def product(pieces):
        high, low = halves(jnp.concatenate([part for _, _, part in pieces], axis=0))
        both = dot(high, across_both, ((1,), (0,)))
        result = both[:, :side] + both[:, side:] + dot(low, across_high, ((1,), (0,)))
        first = 0
        for start, c, part in pieces:
            cut = result[first : first + part.shape[0]]
            across[start : start + part.shape[0], c * side : (c + 1) * side] = cut
            first += part.shape[0]

    def line(index, first, rows):
        return incoming[pl.ds(first * pitch + index, rows, stride=pitch), :]

    def leave(part, whole, p, index):
        cut = pl.ds(p * side, side)
        copy = pltpu.make_async_copy(part.at[cut], whole.at[cut], sems.at[index, p])
        copy.start()
        return copy

    def down(p):
        high, low = halves(across[p * side : (p + 1) * side + 2 * RF, :])
        both = dot(down_both, high, ((1,), (0,)))
        result = both[:side] + both[side:] + dot(down_high, low, ((1,), (0,)))
        detection_part[p * side : (p + 1) * side, :] = result
        return leave(detection_part, detection, p, 1)

    def owner(m, c):
        return RF * ((m - c) % PB)

    copies = []
    pieces = []
    right_side = lax.broadcasted_iota(jnp.int32, (RF, side), 1) < side // 2
    start = depth * per_patch + lines
    for index, m, place in ((start + 1, PB - 1, 0), (start, 0, RF + PB * side)):
        parts = [line(index, owner(m, c), RF) for c in range(PB)]
        after = line(start + 2, owner(m, 0), RF)
        before = line(start + 2, owner(m, PB - 1), RF)
        ends = jnp.where(right_side, after, before)
        if m:
            after = pltpu.roll(after, side - 2 * RF, 1)
            before = pltpu.roll(before, side - 2 * RF, 1)
            ends = jnp.where(right_side, after, before)
        pieces += filtered(parts, ends, place)
    for p in range(PB):
        parts = []
        for c in range(PB):
            tile = jnp.concatenate(
                [
                    line(r * per_patch + p * PB + c, owner(m, c), RF)
                    for r in range(depth)
                    for m in range(PB)
                ],
                axis=0,
            )
            coadd_part[p * side : (p + 1) * side, c * side : (c + 1) * side] = tile
            parts.append(tile)
        copies.append(leave(coadd_part, coadd, p, 0))
        ends = []
        for r in range(depth):
            number = r * PB + p
            index = depth * per_patch + number // group
            turn = -(2 * RF * (number % group) + RF) % side
            for m in range(PB):
                after = line(index, owner(m, 0), RF)
                before = line(index, owner(m, PB - 1), RF)
                ends.append((turn, after, before))
        after = [pltpu.roll(one, turn, 1) for turn, one, _ in ends]
        before = [pltpu.roll(one, turn, 1) for turn, _, one in ends]
        ends = [jnp.where(right_side, one, two) for one, two in zip(after, before)]
        pieces += filtered(parts, jnp.concatenate(ends, axis=0), RF + p * side)
        if p % 2:
            product(pieces)
            pieces = []
            copies += [down(q) for q in range(max(p - 2, 0), p)]
    copies.append(down(PB - 1))
    for copy in copies:
        copy.wait()


def sliced_body(
    stamps, variance, coefficients, band_offsets, shifts, destination, position, psf_taps
):
    count = stamps.shape[0]
    side = variance.shape[1]
    slices = lax.axis_size(AXES)
    depth = side // slices
    visits = lax.axis_size("visit")
    prows = lax.axis_size("prow")
    pcols = lax.axis_size("pcol")
    owners = prows * pcols
    tiles = owners * PB * PB
    span = S
    batch = count
    smem = pl.BlockSpec(memory_space=pltpu.SMEM)
    vmem = pl.BlockSpec(memory_space=pltpu.VMEM)
    pitch = 2 * depth * count + 1
    lines = stamps.reshape(count, -1, side).transpose(1, 0, 2).reshape(-1, side)
    outgoing = pl.pallas_call(
        functools.partial(warp_kernel, slices=slices, span=span, batch=batch),
        in_specs=[vmem, vmem, smem, smem, smem, smem, smem, vmem, vmem],
        out_specs=vmem,
        out_shape=pltpu.VMEM((slices * pitch, side), jnp.float32),
        scratch_shapes=[
            pltpu.VMEM((batch, 2, span + 16, side), jnp.float32),
            pltpu.VMEM((2, side, 2 * side), jnp.bfloat16),
            pltpu.VMEM((2, count, side), jnp.float32),
        ],
    )(
        lines,
        variance,
        coefficients,
        band_offsets.T,
        shifts.T,
        destination,
        position,
        lagged_tables(KR, WRAP, 1),
        lagged_tables(KR, side, -1),
    )
    incoming = lax.all_to_all(
        outgoing.reshape(slices, pitch, 1, side), AXES, split_axis=0, concat_axis=0, tiled=True
    )
    group = side // (2 * RF)
    length = depth * PB * PB + depth * PB // group + 3
    shares = pl.pallas_call(
        functools.partial(
            tile_kernel, slices=slices, count=count, visits=visits, prows=prows, pcols=pcols
        ),
        in_specs=[vmem],
        out_specs=vmem,
        out_shape=pltpu.VMEM((slices * length, side), jnp.float32),
        scratch_shapes=[
            pltpu.VMEM((depth * tiles, side), jnp.float32),
            pltpu.VMEM((owners * depth * PB, side), jnp.float32),
        ],
    )(kept(incoming.reshape(-1, side)))
    gathered = lax.all_to_all(
        shares.reshape(slices, length, 1, side), AXES, split_axis=0, concat_axis=0, tiled=True
    )
    extent = PB * side
    return pl.pallas_call(
        functools.partial(filter_kernel, slices=slices),
        in_specs=[smem, vmem],
        out_specs=[pl.BlockSpec(memory_space=pl.ANY)] * 2,
        out_shape=[jax.ShapeDtypeStruct((extent, extent), jnp.float32)] * 2,
        scratch_shapes=[
            pltpu.VMEM((extent + 2 * RF, extent), jnp.float32),
            pltpu.VMEM((extent, extent), jnp.float32),
            pltpu.VMEM((extent, extent), jnp.float32),
            pltpu.SemaphoreType.DMA((2, PB)),
        ],
    )(psf_taps, kept(gathered.reshape(slices * length, side)))


def kept(values):
    return pltpu.with_memory_space_constraint(values, pltpu.VMEM)


def slices_fit(mesh, count, side):
    total = mesh.shape["visit"] * mesh.shape["prow"] * mesh.shape["pcol"]
    tiles = mesh.shape["prow"] * mesh.shape["pcol"] * PB * PB
    group = side // (2 * RF)
    if side % total or total != RF * PB or tiles % side or WRAP != 2 * side:
        return False
    if total + 2 * KR + TAPS + 8 > WINDOW or (side // total * PB) % group:
        return False
    return total * count % side == 0 and 2 * S == 3 * side


def body(*args):
    mesh = jax.sharding.get_abstract_mesh()
    if slices_fit(mesh, *args[1].shape[:2]):
        return tuple(sliced_body(*args))
    return owner_body(*args)


def solution(mesh):
    placed = (
        P(("visit", "prow", "pcol"), None),
        P(("visit", "prow", "pcol"), None, None),
        P(("visit", "prow", "pcol"), None),
        P(("visit", "prow", "pcol"), None),
        P(("visit", "prow", "pcol"), None),
        P(("visit", "prow", "pcol")),
        P(("visit", "prow", "pcol")),
        P(),
    )
    return jax.shard_map(
        body,
        mesh=mesh,
        in_specs=placed,
        out_specs=(P("prow", "pcol"), P("prow", "pcol")),
        check_vma=False,
    )
```

```python
import functools

import jax
import jax.numpy as jnp
import numpy as np
from jax import lax
from jax.experimental import pallas as pl
from jax.experimental.pallas import tpu as pltpu
from jax.sharding import PartitionSpec as P

S = 192
KR = 15
PB = 4
RF = 8


basis_widths = (1.0, 2.0, 4.0)


def extended(cells, sides, width):
    for axis, dim in sides:
        count = lax.axis_size(axis)
        ends = count - 1
        head = lax.slice_in_dim(cells, 0, width, axis=dim)
        tail = lax.slice_in_dim(cells, cells.shape[dim] - width, cells.shape[dim], axis=dim)
        cells = jnp.concatenate(
            [
                lax.ppermute(tail, axis, [(i, (i + 1) % count) for i in range(ends)]),
                cells,
                lax.ppermute(head, axis, [((i + 1) % count, i) for i in range(ends)]),
            ],
            axis=dim,
        )
    return cells


def factor_tables(span, radius):
    matched_len = span - 2 * radius
    row_index = jnp.arange(matched_len, dtype=jnp.int32)[:, None]
    col_index = jnp.arange(span, dtype=jnp.int32)[None, :]
    lag_index = col_index - row_index - radius
    inside = (jnp.abs(lag_index) <= radius).astype(jnp.float32)
    lagged = lag_index.astype(jnp.float32)
    offsets = jnp.arange(-radius, radius + 1, dtype=jnp.int32).astype(jnp.float32)
    result = []
    for width in basis_widths:
        scaled = offsets / width
        gauss_norm = jnp.sqrt(jnp.sum(jnp.exp(-scaled * scaled)))
        quad_norm = jnp.sqrt(jnp.sum(scaled**4 * jnp.exp(-scaled * scaled)))
        ratio = lagged / width
        bell = jnp.exp(-0.5 * ratio * ratio) * inside
        result.append(jnp.stack([bell / gauss_norm, ratio * ratio * bell / quad_norm]))
    return jnp.stack(result)


def lanczos_bands(offsets, fractions, out_len, in_len):
    row_index = jnp.arange(out_len, dtype=jnp.int32)[None, :, None]
    col_index = jnp.arange(in_len, dtype=jnp.int32)[None, None, :]
    start = offsets[:, None, None]
    distance = (col_index - row_index - start).astype(jnp.float32) - fractions[:, None, None]
    return jnp.where(jnp.abs(distance) < 3.0, jnp.sinc(distance) * jnp.sinc(distance / 3.0), 0.0)


def warp_blocks(stamps, coefficients, band_offsets, shifts, tables, side):
    highest = lax.Precision.HIGHEST
    count = stamps.shape[0]
    matched_len = tables.shape[2]
    matched = jnp.zeros((count, matched_len, matched_len), jnp.float32)
    for width_index in range(len(basis_widths)):
        bell = tables[width_index, 0]
        quad = tables[width_index, 1]
        rows_bell = jnp.einsum(
            "ms,bst->bmt", bell, stamps, precision=highest, preferred_element_type=jnp.float32
        )
        rows_quad = jnp.einsum(
            "ms,bst->bmt", quad, stamps, precision=highest, preferred_element_type=jnp.float32
        )
        first = coefficients[:, 3 * width_index][:, None, None]
        second = coefficients[:, 3 * width_index + 1][:, None, None]
        third = coefficients[:, 3 * width_index + 2][:, None, None]
        left = first * rows_bell + second * rows_quad
        matched = matched + jnp.einsum(
            "bmt,nt->bmn", left, bell, precision=highest, preferred_element_type=jnp.float32
        )
        matched = matched + third * jnp.einsum(
            "bmt,nt->bmn", rows_bell, quad, precision=highest, preferred_element_type=jnp.float32
        )
    band_rows = lanczos_bands(band_offsets[:, 0], shifts[:, 0], side, matched_len)
    band_cols = lanczos_bands(band_offsets[:, 1], shifts[:, 1], side, matched_len)
    halfway = jnp.einsum(
        "bim,bmn->bin", band_rows, matched, precision=highest, preferred_element_type=jnp.float32
    )
    return jnp.einsum(
        "bin,bjn->bij", halfway, band_cols, precision=highest, preferred_element_type=jnp.float32
    )


def filter_band(taps, length, radius):
    row_index = jnp.arange(length, dtype=jnp.int32)[:, None]
    col_index = jnp.arange(length + 2 * radius, dtype=jnp.int32)[None, :]
    lag_index = col_index - row_index
    band = jnp.zeros((length, length + 2 * radius), jnp.float32)
    for tap_index in range(2 * radius + 1):
        band = band + jnp.where(lag_index == tap_index, taps[tap_index], 0.0)
    return band


def owner_body(stamps, variance, coefficients, band_offsets, shifts, destination, position, psf_taps):
    highest = lax.Precision.HIGHEST
    count = stamps.shape[0]
    span = S
    side = variance.shape[1]
    row_owners = lax.axis_size("prow")
    col_owners = lax.axis_size("pcol")
    owners = row_owners * col_owners
    capacity = max(2, 2 * count // owners)
    tables = factor_tables(span, KR)
    images = stamps.reshape(count, span, span)
    warped = warp_blocks(images, coefficients, band_offsets, shifts, tables, side)
    weight = 1.0 / variance
    terms = jnp.stack([weight * warped, weight], axis=1)
    owner_ids = jnp.arange(owners, dtype=jnp.int32)
    onehot = (destination[:, None] == owner_ids[None, :]).astype(jnp.int32)
    block_ids = jnp.arange(count, dtype=jnp.int32)
    earlier = (block_ids[None, :] < block_ids[:, None]).astype(jnp.int32)
    before = jnp.sum(earlier[:, :, None] * onehot[None, :, :], axis=1)
    rank = jnp.sum(before * onehot, axis=1)
    slot_ids = jnp.arange(capacity, dtype=jnp.int32)
    select = onehot.T[:, None, :] * (rank[None, None, :] == slot_ids[None, :, None]).astype(
        jnp.int32
    )
    send_pos = jnp.sum(select * (position[None, None, :] + 1), axis=2) - 1
    outgoing = jnp.einsum(
        "okb,bxij->okxij",
        select.astype(jnp.float32),
        terms,
        precision=highest,
        preferred_element_type=jnp.float32,
    )
    incoming, arrived = (
        lax.all_to_all(outgoing, ("prow", "pcol"), split_axis=0, concat_axis=0, tiled=True),
        lax.all_to_all(send_pos, ("prow", "pcol"), split_axis=0, concat_axis=0, tiled=True),
    )
    flattened = incoming.reshape(owners * capacity, 2 * side * side)
    tile_ids = jnp.arange(PB * PB, dtype=jnp.int32)
    placing = (arrived.reshape(owners * capacity)[None, :] == tile_ids[:, None]).astype(jnp.float32)
    tile_sums = jnp.dot(placing, flattened, precision=highest, preferred_element_type=jnp.float32)
    patch_sums = (
        tile_sums.reshape(PB, PB, 2, side, side)
        .transpose(2, 0, 3, 1, 4)
        .reshape(2, PB * side, PB * side)
    )
    shares = lax.psum_scatter(patch_sums, "visit", scatter_dimension=1, tiled=True)
    coadd = lax.all_gather(shares[0] / (1.0 + shares[1]), "visit", axis=0, tiled=True)
    padded = extended(coadd, (("prow", 0), ("pcol", 1)), RF)
    band = filter_band(psf_taps, coadd.shape[0], RF)
    across = jnp.dot(band, padded, precision=highest, preferred_element_type=jnp.float32)
    detection = jnp.dot(across, band.T, precision=highest, preferred_element_type=jnp.float32)
    return (coadd, detection)


TAPS = 6
AXES = ("prow", "pcol", "visit")
WRAP = 256
WINDOW = 80


def halves(values):
    high = values.astype(jnp.bfloat16)
    return high, (values - high.astype(jnp.float32)).astype(jnp.bfloat16)


def dot(left, right, contract):
    return lax.dot_general(left, right, (contract, ((), ())), preferred_element_type=jnp.float32)


def toeplitz(row, rows):
    spread = jnp.broadcast_to(row, (rows, row.shape[1]))
    return pltpu.roll(spread, 0, 1, stride=1, stride_axis=0)


def lagged_tables(radius, period, sign):
    lags = np.arange(-radius, radius + 1, dtype=np.float64)
    tables = np.zeros((TAPS, 8, period), np.float64)
    for index, width in enumerate(basis_widths):
        ratio = lags / width
        bell = np.exp(-0.5 * ratio * ratio)
        quad = ratio * ratio * bell
        for kind, factor in enumerate((bell, quad)):
            normed = factor / np.sqrt(np.sum(factor * factor))
            for n in range(TAPS):
                places = sign * (np.arange(2 * radius + 1) + n - 2)
                tables[n, 2 * index + kind, places % period] = normed
    return jnp.asarray(tables.astype(np.float32))


def lanczos(distance):
    def sinc(x):
        angle = jnp.float32(np.pi) * x
        return jnp.where(x == 0.0, 1.0, jnp.sin(angle) / jnp.where(x == 0.0, 1.0, angle))

    return jnp.where(jnp.abs(distance) < 3.0, sinc(distance) * sinc(distance / 3.0), 0.0)


def warp_kernel(
    stamps,
    variance,
    coefs,
    offsets,
    shifts,
    dest,
    pos,
    row_tables,
    col_tables,
    out,
    image,
    masks,
    taps,
    *,
    slices,
    span,
    batch,
):
    count, side = variance.shape[:2]
    depth = side // slices
    pitch = 2 * depth * count + 1
    widths = len(basis_widths)
    rows_even = span // 2
    rest = span - side
    step = 3 * count
    image[...] = jnp.zeros(image.shape, image.dtype)
    row = lax.broadcasted_iota(jnp.int32, (side, side), 0)
    col = lax.broadcasted_iota(jnp.int32, (side, side), 1)
    for index, test in enumerate((col <= row, col > row)):
        mask = jnp.where(test, 1.0, 0.0).astype(jnp.bfloat16)
        masks[index] = jnp.concatenate([mask, mask], axis=1)
    lane = lax.broadcasted_iota(jnp.int32, (count, side), 1)
    level = lax.broadcasted_iota(jnp.int32, (count, side), 0)
    for axis in range(2):
        part = jnp.zeros((count, side), jnp.float32)
        for k in range(count):
            part = jnp.where(level == k, shifts[axis, k], part)
        taps[axis] = lanczos((lane - 2).astype(jnp.float32) - part)
    lane = lax.broadcasted_iota(jnp.int32, (slices, side), 1)
    names = jnp.zeros((slices, side), jnp.float32)
    for k in range(count):
        tile = (dest[k] * (PB * PB) + pos[k]).astype(jnp.float32)
        names = jnp.where(lane == k, tile, names)
    out[pl.ds(pitch - 1, slices, stride=pitch), :] = names
    early = lax.broadcasted_iota(jnp.int32, (rows_even, side), 1) < rest

    def mixed(axis, k, tables):
        values = taps[axis, pl.ds(k, 1), :]
        total = jnp.zeros(tables.shape[1:], jnp.float32)
        for n in range(TAPS):
            total = total + values[:, n : n + 1] * tables[n]
        return total

    def one_block(k, b):
        first = stamps[pl.ds(k, rows_even, stride=step), :]
        second = stamps[pl.ds(count + k, rows_even, stride=step), :]
        third = stamps[pl.ds(2 * count + k, rows_even, stride=step), :]
        second_turned = pltpu.roll(second, rest, 1)
        third_turned = pltpu.roll(third, rest, 1)
        image[b, 0, pl.ds(0, rows_even, stride=2), :] = first
        image[b, 1, pl.ds(0, rows_even, stride=2), :] = second
        image[b, 0, pl.ds(1, rows_even, stride=2), :] = jnp.where(
            early, second_turned, third_turned
        )
        image[b, 1, pl.ds(1, rows_even, stride=2), :] = third_turned
        offset = offsets[0, k]
        base = lax.div(offset - 2, 8) * 8
        row_taps = pltpu.roll(mixed(0, k, row_tables), offset - base, 1)
        high = row_taps.astype(jnp.bfloat16).astype(jnp.float32)
        low = (row_taps - high).astype(jnp.bfloat16).astype(jnp.float32)
        lined = high + pltpu.roll(high, WINDOW, 1) + pltpu.roll(low, 2 * WINDOW, 1)
        left = jnp.concatenate(
            [toeplitz(lined[q : q + 1], slices) for q in range(2 * widths)], axis=0
        ).astype(jnp.bfloat16)
        across = []
        for w in range(depth):
            start = pl.multiple_of(w * slices + base, 8)
            window = jnp.concatenate(
                [image[b, half, pl.ds(start, WINDOW), :] for half in range(2)], axis=1
            )
            high, low = halves(window)
            none = jnp.zeros((WRAP - 3 * WINDOW, 2 * side), jnp.bfloat16)
            right = jnp.concatenate([high, low, high, none], axis=0)
            across.append(dot(left, right, ((1,), (0,)))[:, :span])
        offset = offsets[1, k]
        col_taps = pltpu.roll(mixed(1, k, col_tables), side - offset, 1)
        total = jnp.zeros((2 * side, 2 * side), jnp.float32)
        for m in range(widths):
            bell = col_taps[2 * m : 2 * m + 1]
            quad = col_taps[2 * m + 1 : 2 * m + 2]
            pair = (
                coefs[k, 3 * m] * bell + coefs[k, 3 * m + 2] * quad,
                coefs[k, 3 * m + 1] * bell,
            )
            for kind in range(2):
                q = 2 * m + kind
                high, low = halves(toeplitz(pair[kind], side))
                both = jnp.concatenate([high, low], axis=1)
                right = jnp.concatenate([both * masks[0], both[:rest] * masks[1, :rest]], axis=0)
                cut = slice(q * slices, (q + 1) * slices)
                high, low = halves(jnp.concatenate([part[cut] for part in across], axis=0))
                total = total + dot(jnp.concatenate([high, low], axis=0), right, ((1,), (0,)))
        warped = total[:side, :side] + (total[:side, side:] + total[side:, :side])
        weighted = weights[k] * warped
        column = lax.rem(pos[k], PB)
        for m in range(slices // RF):
            first = lax.rem(m + PB - column, PB) * (RF * pitch) + k
            for r in range(depth):
                cut = slice(r * slices + m * RF, r * slices + (m + 1) * RF)
                out[pl.ds(first + r * count, RF, stride=pitch), :] = weighted[cut]

    weights = []
    for k in range(count):
        weight = 1.0 / variance[k]
        weights.append(weight)
        column = lax.rem(pos[k], PB)
        for m in range(slices // RF):
            first = lax.rem(m + PB - column, PB) * (RF * pitch) + k
            for r in range(depth):
                cut = slice(r * slices + m * RF, r * slices + (m + 1) * RF)
                out[pl.ds(first + (depth + r) * count, RF, stride=pitch), :] = weight[cut]
    for k in range(count):
        one_block(k, k)


def tile_kernel(incoming, out, cells, strips, *, slices, count, visits, prows, pcols):
    pitch = incoming.shape[0] // slices
    side = incoming.shape[1]
    depth = side // slices
    owners = prows * pcols
    per_patch = PB * PB
    tiles = owners * per_patch
    blocks = slices * count
    names = incoming[pl.ds(pitch - 1, slices, stride=pitch), :]
    names = pltpu.roll(names, 0, 1, stride=count, stride_axis=0)
    per_row = side // count
    named = jnp.concatenate(
        [
            jnp.sum(names[first : first + per_row], axis=0, keepdims=True)
            for first in range(0, slices, per_row)
        ],
        axis=1,
    )
    places = lax.broadcasted_iota(jnp.int32, (tiles, blocks), 0).astype(jnp.float32)
    chosen = jnp.where(named == places, 1.0, 0.0).astype(jnp.bfloat16)

    def summed(index):
        starts = [j * pitch + index * count for j in range(slices)]
        data = jnp.concatenate([incoming[start : start + count, :] for start in starts], axis=0)
        high, low = halves(data)
        both = dot(chosen, jnp.concatenate([high, low], axis=1), ((1,), (0,)))
        return both[:, :side] + both[:, side:]

    for r in range(depth):
        cells[r * tiles : (r + 1) * tiles, :] = summed(r) / (1.0 + summed(depth + r))
    lane = lax.broadcasted_iota(jnp.int32, (PB, side), 1)
    for o in range(owners):
        for r in range(depth):
            strip = jnp.zeros((PB, side), jnp.float32)
            if o % pcols < pcols - 1:
                after = cells[pl.ds(r * tiles + (o + 1) * per_patch, PB, stride=PB), :]
                strip = jnp.where(lane < RF, after, strip)
            if o % pcols > 0:
                before = cells[pl.ds(r * tiles + (o - 1) * per_patch + PB - 1, PB, stride=PB), :]
                strip = jnp.where(lane >= side - RF, before, strip)
            strips[(o * depth + r) * PB : (o * depth + r + 1) * PB, :] = strip
    group = side // (2 * RF)
    packed = pltpu.roll(strips[...], RF, 1, stride=2 * RF, stride_axis=0)
    packed = jnp.sum(packed.reshape(owners * depth * PB // group, group, side), axis=1)
    lines = depth * PB // group
    turn = lax.div(lax.axis_index(AXES), RF)
    for o in range(owners):
        below = jnp.zeros((1, side), jnp.float32)
        above = jnp.zeros((1, side), jnp.float32)
        corner = jnp.zeros((1, side), jnp.float32)
        if o + pcols < owners:
            start = (o + pcols) * per_patch
            below = cells[pl.ds(start + lax.rem(PB - turn, PB), 1), :]
            start = (o + pcols) * depth * PB
            corner = strips[start : start + 1, :]
        if o >= pcols:
            start = (depth - 1) * tiles + (o - pcols + 1) * per_patch - 1
            above = cells[pl.ds(start - turn, 1), :]
            start = (o - pcols + 1) * depth * PB - 1
            corner = corner + pltpu.roll(strips[start : start + 1, :], 2 * RF, 1)
        for v in range(visits):
            to = (o * visits + v) * (out.shape[0] // slices)
            for r in range(depth):
                start = r * tiles + o * per_patch
                out[to + r * per_patch : to + (r + 1) * per_patch, :] = cells[start : start + per_patch, :]
            start = to + depth * per_patch
            out[start : start + lines, :] = packed[o * lines : (o + 1) * lines]
            start = start + lines
            out[start : start + 1, :] = below
            out[start + 1 : start + 2, :] = above
            out[start + 2 : start + 3, :] = corner


def filter_kernel(
    taps, incoming, coadd, detection, across, coadd_part, detection_part, sems, *, slices
):
    pitch = incoming.shape[0] // slices
    side = incoming.shape[1]
    depth = side // slices
    per_patch = PB * PB
    group = side // (2 * RF)
    lines = depth * PB // group
    lane = lax.broadcasted_iota(jnp.int32, (8, WRAP), 1)
    centred = jnp.zeros((8, WRAP), jnp.float32)
    leading = jnp.zeros((8, WRAP), jnp.float32)
    for b in range(2 * RF + 1):
        centred = jnp.where(lane == (RF - b) % WRAP, taps[b], centred)
        leading = jnp.where(lane == b, taps[b], leading)
    across_band = toeplitz(centred[0:1], WRAP)[:, :side]
    down_band = toeplitz(leading[0:1], side)
    across_high, across_low = halves(across_band)
    across_both = jnp.concatenate([across_high, across_low], axis=1)
    down_high, down_low = halves(down_band[:, : side + 2 * RF])
    down_both = jnp.concatenate([down_high, down_low], axis=0)

    def filtered(parts, ends, start):
        rows = ends.shape[0]
        left = lax.broadcasted_iota(jnp.int32, (rows, side), 1) < side // 2
        whole = []
        for c in range(PB):
            after = parts[c + 1] if c < PB - 1 else ends
            before = parts[c - 1] if c > 0 else ends
            beside = jnp.where(left, after, before)
            whole.append(jnp.concatenate([parts[c], beside], axis=1))
        return [(start, c, part) for c, part in enumerate(whole)]

    def product(pieces):
        high, low = halves(jnp.concatenate([part for _, _, part in pieces], axis=0))
        both = dot(high, across_both, ((1,), (0,)))
        result = both[:, :side] + both[:, side:] + dot(low, across_high, ((1,), (0,)))
        first = 0
        for start, c, part in pieces:
            cut = result[first : first + part.shape[0]]
            across[start : start + part.shape[0], c * side : (c + 1) * side] = cut
            first += part.shape[0]

    def line(index, first, rows):
        return incoming[pl.ds(first * pitch + index, rows, stride=pitch), :]

    def leave(part, whole, p, index):
        cut = pl.ds(p * side, side)
        copy = pltpu.make_async_copy(part.at[cut], whole.at[cut], sems.at[index, p])
        copy.start()
        return copy

    def down(p):
        high, low = halves(across[p * side : (p + 1) * side + 2 * RF, :])
        both = dot(down_both, high, ((1,), (0,)))
        result = both[:side] + both[side:] + dot(down_high, low, ((1,), (0,)))
        detection_part[p * side : (p + 1) * side, :] = result
        return leave(detection_part, detection, p, 1)

    def owner(m, c):
        return RF * ((m - c) % PB)

    copies = []
    pieces = []
    right_side = lax.broadcasted_iota(jnp.int32, (RF, side), 1) < side // 2
    start = depth * per_patch + lines
    for index, m, place in ((start + 1, PB - 1, 0), (start, 0, RF + PB * side)):
        parts = [line(index, owner(m, c), RF) for c in range(PB)]
        after = line(start + 2, owner(m, 0), RF)
        before = line(start + 2, owner(m, PB - 1), RF)
        ends = jnp.where(right_side, after, before)
        if m:
            after = pltpu.roll(after, side - 2 * RF, 1)
            before = pltpu.roll(before, side - 2 * RF, 1)
            ends = jnp.where(right_side, after, before)
        pieces += filtered(parts, ends, place)
    for p in range(PB):
        parts = []
        for c in range(PB):
            tile = jnp.concatenate(
                [
                    line(r * per_patch + p * PB + c, owner(m, c), RF)
                    for r in range(depth)
                    for m in range(PB)
                ],
                axis=0,
            )
            coadd_part[p * side : (p + 1) * side, c * side : (c + 1) * side] = tile
            parts.append(tile)
        copies.append(leave(coadd_part, coadd, p, 0))
        ends = []
        for r in range(depth):
            number = r * PB + p
            index = depth * per_patch + number // group
            turn = -(2 * RF * (number % group) + RF) % side
            for m in range(PB):
                after = line(index, owner(m, 0), RF)
                before = line(index, owner(m, PB - 1), RF)
                ends.append((turn, after, before))
        after = [pltpu.roll(one, turn, 1) for turn, one, _ in ends]
        before = [pltpu.roll(one, turn, 1) for turn, _, one in ends]
        ends = [jnp.where(right_side, one, two) for one, two in zip(after, before)]
        pieces += filtered(parts, jnp.concatenate(ends, axis=0), RF + p * side)
        if p % 2:
            product(pieces)
            pieces = []
            copies += [down(q) for q in range(max(p - 2, 0), p)]
    copies.append(down(PB - 1))
    for copy in copies:
        copy.wait()


def sliced_body(
    stamps, variance, coefficients, band_offsets, shifts, destination, position, psf_taps
):
    count = stamps.shape[0]
    side = variance.shape[1]
    slices = lax.axis_size(AXES)
    depth = side // slices
    visits = lax.axis_size("visit")
    prows = lax.axis_size("prow")
    pcols = lax.axis_size("pcol")
    owners = prows * pcols
    tiles = owners * PB * PB
    span = S
    batch = count
    smem = pl.BlockSpec(memory_space=pltpu.SMEM)
    vmem = pl.BlockSpec(memory_space=pltpu.VMEM)
    pitch = 2 * depth * count + 1
    lines = stamps.reshape(count, -1, side).transpose(1, 0, 2).reshape(-1, side)
    outgoing = pl.pallas_call(
        functools.partial(warp_kernel, slices=slices, span=span, batch=batch),
        in_specs=[vmem, vmem, smem, smem, smem, smem, smem, vmem, vmem],
        out_specs=vmem,
        out_shape=pltpu.VMEM((slices * pitch, side), jnp.float32),
        scratch_shapes=[
            pltpu.VMEM((batch, 2, span + 16, side), jnp.float32),
            pltpu.VMEM((2, side, 2 * side), jnp.bfloat16),
            pltpu.VMEM((2, count, side), jnp.float32),
        ],
    )(
        lines,
        variance,
        coefficients,
        band_offsets.T,
        shifts.T,
        destination,
        position,
        lagged_tables(KR, WRAP, 1),
        lagged_tables(KR, side, -1),
    )
    incoming = lax.all_to_all(
        outgoing.reshape(slices, pitch, 1, side), AXES, split_axis=0, concat_axis=0, tiled=True
    )
    group = side // (2 * RF)
    length = depth * PB * PB + depth * PB // group + 3
    shares = pl.pallas_call(
        functools.partial(
            tile_kernel, slices=slices, count=count, visits=visits, prows=prows, pcols=pcols
        ),
        in_specs=[vmem],
        out_specs=vmem,
        out_shape=pltpu.VMEM((slices * length, side), jnp.float32),
        scratch_shapes=[
            pltpu.VMEM((depth * tiles, side), jnp.float32),
            pltpu.VMEM((owners * depth * PB, side), jnp.float32),
        ],
    )(kept(incoming.reshape(-1, side)))
    gathered = lax.all_to_all(
        shares.reshape(slices, length, 1, side), AXES, split_axis=0, concat_axis=0, tiled=True
    )
    extent = PB * side
    return pl.pallas_call(
        functools.partial(filter_kernel, slices=slices),
        compiler_params=pltpu.CompilerParams(),
        in_specs=[smem, vmem],
        out_specs=[pl.BlockSpec(memory_space=pl.ANY)] * 2,
        out_shape=[jax.ShapeDtypeStruct((extent, extent), jnp.float32)] * 2,
        scratch_shapes=[
            pltpu.VMEM((extent + 2 * RF, extent), jnp.float32),
            pltpu.VMEM((extent, extent), jnp.float32),
            pltpu.VMEM((extent, extent), jnp.float32),
            pltpu.SemaphoreType.DMA((2, PB)),
        ],
    )(psf_taps, kept(gathered.reshape(slices * length, side)))


def kept(values):
    return pltpu.with_memory_space_constraint(values, pltpu.VMEM)


def slices_fit(mesh, count, side):
    total = mesh.shape["visit"] * mesh.shape["prow"] * mesh.shape["pcol"]
    tiles = mesh.shape["prow"] * mesh.shape["pcol"] * PB * PB
    group = side // (2 * RF)
    if side % total or total != RF * PB or tiles % side or WRAP != 2 * side:
        return False
    if total + 2 * KR + TAPS + 8 > WINDOW or (side // total * PB) % group:
        return False
    return total * count % side == 0 and 2 * S == 3 * side


def body(*args):
    mesh = jax.sharding.get_abstract_mesh()
    if slices_fit(mesh, *args[1].shape[:2]):
        return tuple(sliced_body(*args))
    return owner_body(*args)


def solution(mesh):
    placed = (
        P(("visit", "prow", "pcol"), None),
        P(("visit", "prow", "pcol"), None, None),
        P(("visit", "prow", "pcol"), None),
        P(("visit", "prow", "pcol"), None),
        P(("visit", "prow", "pcol"), None),
        P(("visit", "prow", "pcol")),
        P(("visit", "prow", "pcol")),
        P(),
    )
    return jax.shard_map(
        body,
        mesh=mesh,
        in_specs=placed,
        out_specs=(P("prow", "pcol"), P("prow", "pcol")),
        check_vma=False,
    )
```
